256 devices in a mesh: gz: 8 (over z), gy: 8 (over y, core), gx: 4 (over x).
Axes of the slice: x: 4, y: 4, z: 8, core: 2. Of those that a mesh axis runs over, the one named last changes fastest.
Arguments:
- side_field: float32 [2, 384, 256, 512], P(None, 'gz', 'gy', 'gx'), may hold values from -6 to 6
- magnetogram: float32 [256, 512], P('gy', 'gx'), may hold values from -6 to 6
Outputs:
- potential: float32 [3, 384, 256, 512], P(None, 'gz', 'gy', 'gx')
The draws below stay inside these ranges and needn't reach their ends.
All inputs are finite; a program needn't handle non-finite values.
Results may differ from the reference program's by a relative error of at most 0.000021.
Values sent between devices are 32-bit elements; how exact they have to be, the bound alone decides.
A program may use at most 64 MiB of HBM per device.

```python
import jax
import jax.numpy as jnp
from jax import lax

CZ = 48
NZ = 384
NY = 256
NX = 512


def shard_levels(stream_key, shape, pieces, low, top_value):
    factor_of = 1.0
    for dim, blocks in pieces:
        steps = jax.random.uniform(jax.random.fold_in(jax.random.fold_in(stream_key, 6), dim), (blocks,), jnp.float32, low / len(pieces), top_value / len(pieces))
        factor_of = factor_of * jnp.repeat(jnp.exp(steps), shape[dim] // blocks).reshape((-1,) + (1,) * (len(shape) - 1 - dim))
    return factor_of


def normal_values(stream_key, shape, width, bound, shards=(), kind=jnp.bfloat16):
    loudness = shard_levels(stream_key, shape, shards, -0.22, 0.18) if shards else 1.0
    result = jax.random.normal(stream_key, shape, jnp.float32) * width * loudness
    return jnp.minimum(jnp.maximum(result, -bound), bound).astype(kind)


def setup_inputs(seed: int = 0) -> dict:
    keys = jax.random.split(jax.random.key(seed), 3)
    side_field = normal_values(keys[0], (2, NZ, NY, NX), 1.0, 6.0, ((1, 8), (2, 8), (3, 4)), jnp.float32)
    magnetogram = normal_values(keys[1], (NY, NX), 1.0, 6.0, ((0, 8), (1, 4)), jnp.float32)
    return {"side_field": side_field, "magnetogram": magnetogram}


spacing = 0.0625
friction = 0.004


def forward_parts(values):
    anchor = values[:-1, :-1, :-1]
    return (values[1:, :-1, :-1] - anchor, values[:-1, 1:, :-1] - anchor, values[:-1, :-1, 1:] - anchor)


def backward_parts(values):
    corner = values[1:, 1:, 1:]
    return (corner - values[:-1, 1:, 1:], corner - values[1:, :-1, 1:], corner - values[1:, 1:, :-1])


def advance(padded):
    along_x = forward_parts(padded[0])
    along_y = forward_parts(padded[1])
    along_z = forward_parts(padded[2])
    field_x = (along_z[1] - along_y[0]) / spacing
    field_y = (along_x[0] - along_z[2]) / spacing
    field_z = (along_y[2] - along_x[1]) / spacing
    back_x = backward_parts(field_x)
    back_y = backward_parts(field_y)
    back_z = backward_parts(field_z)
    current_x = (back_z[1] - back_y[0]) / spacing
    current_y = (back_x[0] - back_z[2]) / spacing
    current_z = (back_y[2] - back_x[1]) / spacing
    cell_x = field_x[1:, 1:, 1:]
    cell_y = field_y[1:, 1:, 1:]
    cell_z = field_z[1:, 1:, 1:]
    denominator = cell_x * cell_x + cell_y * cell_y + cell_z * cell_z + 1.0
    speed_x = (current_y * cell_z - current_z * cell_y) / denominator
    speed_y = (current_z * cell_x - current_x * cell_z) / denominator
    speed_z = (current_x * cell_y - current_y * cell_x) / denominator
    drive_x = speed_y * cell_z - speed_z * cell_y
    drive_y = speed_z * cell_x - speed_x * cell_z
    drive_z = speed_x * cell_y - speed_y * cell_x
    inner = padded[:, 1:-1, 1:-1, 1:-1]
    return inner + friction * jnp.stack([drive_x, drive_y, drive_z])


def advance_all(potential):
    padded = jnp.pad(potential, ((0, 0), (1, 1), (1, 1), (1, 1)))

    def one_block(start):
        piece = lax.dynamic_slice_in_dim(padded, start, CZ + 2, axis=1)
        return advance(piece)

    starts = jnp.arange(NZ // CZ, dtype=jnp.int32) * CZ
    blocks = lax.map(one_block, starts)
    return jnp.transpose(blocks, (1, 0, 2, 3, 4)).reshape(3, NZ, NY, NX)


def reference(side_field, magnetogram):
    half = 0.5 * spacing
    base_x = -half * jnp.cumsum(magnetogram, axis=0)
    base_y = half * jnp.cumsum(magnetogram, axis=1)
    rising = jnp.cumsum(side_field, axis=1)
    potential = jnp.stack([base_x[None] + spacing * rising[1], base_y[None] - spacing * rising[0], jnp.zeros_like(rising[0])])
    for _ in range(2):
        potential = advance_all(potential)
    return potential
```

```python
import functools

import jax
import jax.numpy as jnp
from jax import lax
from jax.experimental import pallas as pl
from jax.experimental.pallas import tpu as pltpu
from jax.sharding import PartitionSpec as P

spacing = 0.0625
friction = 0.004
MESH = pl.DeviceIdType.MESH

NZ_DEV, NY_DEV, NX_DEV = 8, 8, 4
CZ, CY, CX = 48, 32, 128
EZ = CZ + 3
EY = CY + 8
LEVEL = EZ * CY
UP, DOWN = 4, 3


def lanes(shape):
    return lax.broadcasted_iota(jnp.int32, shape, len(shape) - 1)


def rows(shape):
    return lax.broadcasted_iota(jnp.int32, shape, len(shape) - 2)


def comm_kernel(
    side_hbm,
    mag_ref,
    ext_out,
    zh_out,
    q_out,
    e_out,
    side_v,
    t_v,
    ring_up,
    ring_dn,
    ys_lo,
    ys_hi,
    yr_lo,
    yr_hi,
    cs_lo,
    cs_hi,
    cr_lo,
    cr_hi,
    w_hi,
    w_lo,
    wn_hi,
    wn_lo,
    mc_s,
    mr_s,
    mc_r,
    mr_r,
    q_v,
    qt_lo,
    qt_hi,
    qy_lo,
    qy_hi,
    qx_lo,
    qx_hi,
    qd,
    load_sem,
    s_up,
    r_up,
    s_dn,
    r_dn,
    s_z,
    r_z,
    s_y,
    r_y,
    s_c,
    r_c,
    s_w,
    r_w,
    s_mc,
    r_mc,
    s_mr,
    r_mr,
    s_q,
    r_q,
):
    gz, gy, gx = lax.axis_index("gz"), lax.axis_index("gy"), lax.axis_index("gx")

    def at(dz=0, dy=0, dx=0):
        where = {}
        if dz:
            where["gz"] = lax.rem(gz + dz + NZ_DEV, NZ_DEV)
        if dy:
            where["gy"] = lax.rem(gy + dy + NY_DEV, NY_DEV)
        if dx:
            where["gx"] = lax.rem(gx + dx + NX_DEV, NX_DEV)
        return where

    loads = [
        pltpu.make_async_copy(
            side_hbm.at[pl.ds(c * CZ * CY, CZ * CY)],
            side_v.at[pl.ds(c * LEVEL + CY, CZ * CY)],
            load_sem.at[c],
        )
        for c in range(2)
    ]
    for load in loads:
        load.start()

    barrier = pltpu.get_barrier_semaphore()
    peers = (
        [at(dz=1), at(dz=-1)]
        + [at(dy=d) for d in range(1, NY_DEV)]
        + [at(dx=d) for d in range(1, NX_DEV)]
        + [at(dy=a, dx=b) for a in (1, -1) for b in (1, -1)]
    )
    for peer in peers:
        pl.semaphore_signal(barrier, inc=1, device_id=peer, device_id_type=MESH)

    def send(src, dst, ssem, rsem, where):
        return pltpu.make_async_remote_copy(
            src_ref=src,
            dst_ref=dst,
            send_sem=ssem,
            recv_sem=rsem,
            device_id=where,
            device_id_type=MESH,
        )

    mag = mag_ref[...]
    mc_s[...] = jnp.broadcast_to(jnp.sum(mag, axis=0, keepdims=True), (8, CX))
    mr_s[...] = jnp.broadcast_to(jnp.sum(mag, axis=1, keepdims=True), (CY, CX))
    ext_out[...] = jnp.zeros_like(ext_out)

    for c in range(2):
        loads[c].wait()

        def add(z, total, c=c):
            return total + side_v[pl.ds(c * LEVEL + (z + 1) * CY, CY), :]

        t_v[pl.ds(c * CY, CY), :] = lax.fori_loop(
            0, CZ, add, jnp.zeros((CY, CX), jnp.float32), unroll=8
        )
    pl.semaphore_wait(barrier, len(peers))

    def up(s, c):
        src = t_v.at[pl.ds(c * CY, CY)] if s == 0 else ring_up.at[s - 1, pl.ds(c * CY, CY)]
        return send(
            src, ring_up.at[s, pl.ds(c * CY, CY)], s_up.at[s, c], r_up.at[s, c], at(dz=1)
        )

    def down(s, c):
        src = t_v.at[pl.ds(c * CY, CY)] if s == 0 else ring_dn.at[s - 1, pl.ds(c * CY, CY)]
        return send(
            src, ring_dn.at[s, pl.ds(c * CY, CY)], s_dn.at[s, c], r_dn.at[s, c], at(dz=-1)
        )

    ups = [[up(s, c) for c in range(2)] for s in range(UP)]
    downs = [[down(s, c) for c in range(2)] for s in range(DOWN)]
    for c in range(2):
        ups[0][c].start()
        downs[0][c].start()

    sums = [
        send(mc_s, mc_r.at[pl.ds(8 * (d - 1), 8)], s_mc.at[d - 1], r_mc.at[d - 1], at(dy=d))
        for d in range(1, NY_DEV)
    ] + [
        send(mr_s, mr_r.at[pl.ds(CY * (d - 1), CY)], s_mr.at[d - 1], r_mr.at[d - 1], at(dx=d))
        for d in range(1, NX_DEV)
    ]
    for one in sums:
        one.start()

    layers = []
    for c in range(2):
        layers.append(
            send(
                side_hbm.at[pl.ds(c * CZ * CY + (CZ - 1) * CY, CY)],
                side_v.at[pl.ds(c * LEVEL, CY)],
                s_z.at[0, c],
                r_z.at[0, c],
                at(dz=1),
            )
        )
        layers.append(
            send(
                side_hbm.at[pl.ds(c * CZ * CY, 2 * CY)],
                side_v.at[pl.ds(c * LEVEL + (CZ + 1) * CY, 2 * CY)],
                s_z.at[1, c],
                r_z.at[1, c],
                at(dz=-1),
            )
        )
    for one in layers:
        one.start()

    for c in range(2):
        for k in range(2):
            here = pl.ds((2 * c + k) * CZ, CZ)
            ys_lo[here, :] = side_v[pl.ds(c * LEVEL + CY + k, CZ, stride=CY), :]
            ys_hi[here, :] = side_v[pl.ds(c * LEVEL + CY + CY - 2 + k, CZ, stride=CY), :]
    faces = [
        send(ys_lo, yr_hi, s_y.at[0], r_y.at[0], at(dy=-1)),
        send(ys_hi, yr_lo, s_y.at[1], r_y.at[1], at(dy=1)),
    ]
    for one in faces:
        one.start()

    def pass_on(s):
        for c in range(2):
            ups[s][c].wait_recv()
            if s + 1 < UP:
                ups[s + 1][c].start()
            if s < DOWN:
                downs[s][c].wait_recv()
                if s + 1 < DOWN:
                    downs[s + 1][c].start()

    pass_on(0)

    for one in layers:
        one.wait_recv()
    for c in range(2):
        for i, level in enumerate((0, CZ + 1, CZ + 2)):
            first = c * LEVEL + level * CY
            to = (c * 3 + i) * 2
            cs_lo[pl.ds(to, 2), :] = side_v[pl.ds(first, 2), :]
            cs_hi[pl.ds(to, 2), :] = side_v[pl.ds(first + CY - 2, 2), :]
            zh_out[pl.ds((c * 3 + i) * CY, CY), :] = side_v[pl.ds(first, CY), :]
    cs_lo[pl.ds(12, 4), :] = jnp.zeros((4, CX), jnp.float32)
    cs_hi[pl.ds(12, 4), :] = jnp.zeros((4, CX), jnp.float32)
    corners = [
        send(cs_lo, cr_hi, s_c.at[0], r_c.at[0], at(dy=-1)),
        send(cs_hi, cr_lo, s_c.at[1], r_c.at[1], at(dy=1)),
    ]
    for one in corners:
        one.start()

    has_ylo = (gy > 0).astype(jnp.float32)
    has_yhi = (gy < NY_DEV - 1).astype(jnp.float32)
    has_xlo = (gx > 0).astype(jnp.float32)
    has_xhi = (gx < NX_DEV - 1).astype(jnp.float32)

    for one in faces:
        one.wait_recv()
    for c in range(2):
        for k in range(2):
            here = pl.ds((2 * c + k) * CZ, CZ)
            ext_out[pl.ds((c * EZ + 1) * 8 + k, CZ, stride=8), :] = yr_hi[here, :] * has_yhi
            ext_out[pl.ds((c * EZ + 1) * 8 + 6 + k, CZ, stride=8), :] = yr_lo[here, :] * has_ylo

    pass_on(1)

    for one in corners:
        one.wait_recv()
    for c in range(2):
        for i, level in enumerate((0, CZ + 1, CZ + 2)):
            first = (c * EZ + level) * 8
            of = (c * 3 + i) * 2
            ext_out[pl.ds(first, 2), :] = cr_hi[pl.ds(of, 2), :] * has_yhi
            ext_out[pl.ds(first + 6, 2), :] = cr_lo[pl.ds(of, 2), :] * has_ylo

    lane = lanes((EY, CX))

    def raw(c, level):
        return jnp.concatenate(
            [
                side_v[pl.ds(pl.multiple_of(c * LEVEL + level * CY, 8), CY), :],
                ext_out[pl.ds(pl.multiple_of((c * EZ + level) * 8, 8), 8), :],
            ],
            axis=0,
        )

    def place(zi, running, packed):
        first = 2 * zi
        out = []
        for c in range(2):
            turned = pltpu.roll(running[c], first + 2, 1)
            hi, lo = packed[2 * c], packed[2 * c + 1]
            out.append(jnp.where((lane == first) | (lane == first + 1), turned, hi))
            out.append(jnp.where((lane == first + 2) | (lane == first + 3), turned, lo))
        return tuple(out)

    nothing = jnp.zeros((EY, CX), jnp.float32)
    running = tuple(-raw(c, 0) for c in range(2))
    packed = place(0, running, (nothing,) * 4)

    def pack(zi, carry):
        running, packed = carry
        running = tuple(running[c] + raw(c, zi - 1) for c in range(2))
        return running, place(zi, running, packed)

    _, packed = lax.fori_loop(1, EZ + 1, pack, (running, packed))
    for c in range(2):
        w_hi[pl.ds(c * EY, EY), :] = packed[2 * c]
        w_lo[pl.ds(c * EY, EY), :] = packed[2 * c + 1]
    columns = [
        send(w_hi, wn_lo, s_w.at[0], r_w.at[0], at(dx=1)),
        send(w_lo, wn_hi, s_w.at[1], r_w.at[1], at(dx=-1)),
    ]
    for one in columns:
        one.start()

    for one in sums:
        one.wait_recv()
    col = mag
    row_of = rows((CY, CX))
    for k in (1, 2, 4, 8, 16):
        col = col + jnp.where(row_of >= k, pltpu.roll(col, k, 0), 0.0)
    lin = mag
    lane_of = lanes((CY, CX))
    for k in (1, 2, 4, 8, 16, 32, 64):
        lin = lin + jnp.where(lane_of >= k, pltpu.roll(lin, k, 1), 0.0)
    for d in range(1, NY_DEV):
        part = mc_r[pl.ds(8 * (d - 1), 1), :]
        col = col + jnp.where(d <= gy, part, 0.0)
    for d in range(1, NX_DEV):
        part = mr_r[pl.ds(CY * (d - 1), CY), :]
        lin = lin + jnp.where(d <= gx, part, 0.0)
    base = (-0.5 * spacing * col, 0.5 * spacing * lin)

    pass_on(2)
    below = [jnp.zeros((CY, CX), jnp.float32) for _ in range(2)]
    for c in range(2):
        for s in range(3):
            part = ring_up[s, pl.ds(c * CY, CY), :]
            below[c] = below[c] + jnp.where(gz - (s + 1) >= 0, part, 0.0)
            part = ring_dn[s, pl.ds(c * CY, CY), :]
            below[c] = below[c] + jnp.where(gz + (s + 1) >= NZ_DEV, part, 0.0)

    for one in columns:
        one.wait_recv()

    pass_on(3)
    for c in range(2):
        part = ring_up[3, pl.ds(c * CY, CY), :]
        below[c] = below[c] + jnp.where(gz - 4 >= 0, part, 0.0)
    q = (base[0] + spacing * below[1], base[1] - spacing * below[0])
    for c in range(2):
        q_v[pl.ds(c * CY, CY), :] = q[c]
        qt_lo[pl.ds(c * 8, 8), :] = q[c][:8]
        qt_hi[pl.ds(c * 8, 8), :] = q[c][CY - 8 :]
    planes = [
        send(q_v, qx_lo, s_q.at[0], r_q.at[0], at(dx=1)),
        send(q_v, qx_hi, s_q.at[1], r_q.at[1], at(dx=-1)),
        send(qt_lo, qy_hi, s_q.at[2], r_q.at[2], at(dy=-1)),
        send(qt_hi, qy_lo, s_q.at[3], r_q.at[3], at(dy=1)),
        send(qt_lo, qd.at[0], s_q.at[4], r_q.at[4], at(dy=-1, dx=1)),
        send(qt_lo, qd.at[1], s_q.at[5], r_q.at[5], at(dy=-1, dx=-1)),
        send(qt_hi, qd.at[2], s_q.at[6], r_q.at[6], at(dy=1, dx=1)),
        send(qt_hi, qd.at[3], s_q.at[7], r_q.at[7], at(dy=1, dx=-1)),
    ]
    for one in planes:
        one.start()
    for one in planes:
        one.wait_recv()

    row8 = rows((8, CX))

    def fifth(from_hi, from_lo):
        return jnp.where(
            row8 < 2, from_hi * has_yhi, jnp.where(row8 >= 6, from_lo * has_ylo, 0.0)
        )

    def plane(main, from_hi, from_lo, c):
        tile = fifth(from_hi[pl.ds(c * 8, 8), :], from_lo[pl.ds(c * 8, 8), :])
        return jnp.concatenate([main, tile], axis=0)

    even = lane % 2 == 0
    level_ok = ((lane >= 4) | (gz > 0)) & ((lane < 2 * (CZ + 2)) | (gz < NZ_DEV - 1))
    for c in range(2):
        own = plane(q[c], qy_hi, qy_lo, c)
        low = plane(qx_lo[pl.ds(c * CY, CY), :], qd.at[0], qd.at[2], c) * has_xlo
        high = plane(qx_hi[pl.ds(c * CY, CY), :], qd.at[1], qd.at[3], c) * has_xhi
        q_out[pl.ds(c * EY, EY), :] = own

        o, sign = (1, spacing) if c == 0 else (0, -spacing)
        there = pl.ds(o * EY, EY)
        hi, lo = w_hi[there, :], w_lo[there, :]
        hin, lon = wn_hi[there, :] * has_xhi, wn_lo[there, :] * has_xlo

        def spread(x, i):
            return jnp.broadcast_to(x[:, i : i + 1], (EY, CX))

        parts = (
            (spread(own, 126), spread(low, 126), hi, pltpu.roll(lon, 1, 1)),
            (spread(own, 127), spread(low, 127), pltpu.roll(hi, CX - 1, 1), lon),
            (spread(high, 0), spread(own, 0), pltpu.roll(hin, CX - 2, 1), pltpu.roll(lo, CX - 1, 1)),
            (spread(high, 1), spread(own, 1), pltpu.roll(hin, CX - 3, 1), pltpu.roll(lo, CX - 2, 1)),
        )
        for m, (q_hi, q_lo, l_hi, l_lo) in enumerate(parts):
            value = jnp.where(even, q_hi, q_lo) + sign * jnp.where(even, l_hi, l_lo)
            e_out[pl.ds((m * 2 + c) * EY, EY), :] = jnp.where(level_ok, value, 0.0)

    for group in ups + downs:
        for one in group:
            one.wait_send()
    for one in sums + layers + faces + corners + columns + planes:
        one.wait_send()


def turn(x, shift, axis):
    return pltpu.roll(x, shift % x.shape[axis], axis)


def fields(a, zp, yp, xp, first):
    ax, ay = a[0], a[1]
    if first:
        bx = ay - zp[1]
        by = zp[0] - ax
    else:
        bx = (yp[2] - a[2]) - (zp[1] - ay)
        by = (zp[0] - ax) - (xp[2] - a[2])
    bz = (xp[1] - ay) - (yp[0] - ax)
    return bx, by, bz


def drive(b, zm, ym, xm):
    bx, by, bz = b
    jx = (bz - ym[2]) - (by - zm[1])
    jy = (bx - zm[0]) - (bz - xm[2])
    jz = (by - xm[1]) - (bx - ym[0])
    square = bx * bx + by * by + bz * bz
    scale = (friction / spacing**2) / (square + spacing**2)
    along = (jx * bx + jy * by + jz * bz) * scale
    across = square * scale
    return (along * bx - across * jx, along * by - across * jy, along * bz - across * jz)


def step_kernel(
    side_hbm,
    ext_ref,
    zh_ref,
    q_ref,
    e_ref,
    out_hbm,
    side_v,
    a1m,
    a1e,
    out_v,
    load_sem,
    store_sem,
):
    gz, gy, gx = lax.axis_index("gz"), lax.axis_index("gy"), lax.axis_index("gx")
    loads = [
        pltpu.make_async_copy(
            side_hbm.at[pl.ds(c * CZ * CY, CZ * CY)],
            side_v.at[pl.ds(c * LEVEL + CY, CZ * CY)],
            load_sem.at[c],
        )
        for c in range(2)
    ]
    for load in loads:
        load.start()
    for c in range(2):
        for i, level in enumerate((0, CZ + 1, CZ + 2)):
            side_v[pl.ds(c * LEVEL + level * CY, CY), :] = zh_ref[pl.ds((c * 3 + i) * CY, CY), :]

    shape = (EY, CX)
    lane, row = lanes(shape), rows(shape)
    even = lane % 2 == 0
    row_ok = ((row < CY) | (row >= CY + 2) | (gy < NY_DEV - 1)) & (
        (row < CY + 2) | (gy > 0)
    )

    ea = [[e_ref[pl.ds((m * 2 + c) * EY, EY), :] for c in range(2)] for m in range(4)]
    eb = []
    for m in range(3):
        up_y = (turn(ea[m][0], -1, 0),)
        up_z = tuple(turn(x, -2, 1) for x in ea[m])
        eb.append(fields(ea[m], up_z, up_y, ea[m + 1], True))
    ea1 = []
    for m in (1, 2):
        down_z = tuple(turn(x, 2, 1) for x in eb[m])
        down_y = tuple(turn(x, 1, 0) for x in eb[m])
        d = drive(eb[m], down_z, down_y, eb[m - 1])
        outside = (lane % 2 == 1) & (gx == 0) if m == 1 else (lane % 2 == 0) & (gx == NX_DEV - 1)
        ok = (
            row_ok
            & jnp.logical_not(outside)
            & ((lane >= 4) | (gz > 0))
            & ((lane < 2 * (CZ + 2)) | (gz < NZ_DEV - 1))
        )
        a = (ea[m][0] + d[0], ea[m][1] + d[1], d[2])
        ea1.append(tuple(jnp.where(ok, x, 0.0) for x in a))
    u1 = jnp.where(even, ea[2][1], eb[1][2])
    u2 = eb[1][1]
    near = ea1[0]
    eb1 = fields(
        near,
        tuple(turn(x, -2, 1) for x in near),
        tuple(turn(x, -1, 0) for x in near),
        ea1[1],
        False,
    )
    v1 = jnp.where(even, ea1[1][1], eb1[2])
    v2 = jnp.where(even, ea1[1][2], eb1[1])

    def raw(c, level):
        return jnp.concatenate(
            [
                side_v[pl.ds(pl.multiple_of(c * LEVEL + level * CY, 8), CY), :],
                ext_ref[pl.ds(pl.multiple_of((c * EZ + level) * 8, 8), 8), :],
            ],
            axis=0,
        )

    in_lo = (gz > 0).astype(jnp.float32)
    in_hi = (gz < NZ_DEV - 1).astype(jnp.float32)
    first_lane, last_lane = lane == 0, lane == CX - 1
    tile_row = rows((8, CX))
    tile_ok = ((tile_row >= 2) | (gy < NY_DEV - 1)) & ((tile_row < 2) | (gy > 0))

    def grow(a, level):
        return (a[0] + spacing * raw(1, level), a[1] - spacing * raw(0, level))

    def field_at(a, a_up, u):
        xp = (None, jnp.where(last_lane, u[0], turn(a[1], -1, 1)))
        return fields(a, a_up, (turn(a[0], -1, 0),), xp, True)

    def first_step(a, b, before, u, store, ok=None):
        xm = (
            None,
            jnp.where(first_lane, u[1], turn(b[1], 1, 1)),
            jnp.where(first_lane, u[0], turn(b[2], 1, 1)),
        )
        ym = (turn(b[0], 1, 0), None, turn(b[2], 1, 0))
        d = drive(b, before, ym, xm)
        new = (a[0] + d[0], a[1] + d[1], d[2])
        for c in range(3):
            x = new[c] if ok is None else new[c] * ok
            a1m[pl.ds(pl.multiple_of((c * (CZ + 2) + store) * CY, 8), CY), :] = x[:CY]
            a1e[pl.ds(pl.multiple_of((c * (CZ + 2) + store) * 8, 8), 8), :] = jnp.where(
                tile_ok, x[CY:], 0.0
            )

    def advance_u(u):
        return tuple(turn(x, -2, 1) for x in u)

    for load in loads:
        load.wait()
    q = tuple(q_ref[pl.ds(c * EY, EY), :] for c in range(2))
    bottom = tuple(x * in_lo for x in q)
    lowest = (
        (q[0] - spacing * raw(1, 0)) * in_lo,
        (q[1] + spacing * raw(0, 0)) * in_lo,
    )
    u = tuple(turn(x, CX - 1, 1) for x in (u1, u2))
    b = field_at(lowest, bottom, u)
    u = advance_u(u)
    a = grow(q, 1)
    before = (b[0], b[1])
    b = field_at(bottom, a, u)
    first_step(bottom, b, before, u, 0, in_lo)
    u = advance_u(u)

    def level_one(z, carry):
        a, before, u = carry
        a_up = grow(a, z + 2)
        b = field_at(a, a_up, u)
        first_step(a, b, before, u, z + 1)
        return a_up, (b[0], b[1]), advance_u(u)

    a, before, u = lax.fori_loop(0, CZ - 1, level_one, (a, (b[0], b[1]), u))
    top = tuple(x * in_hi for x in grow(a, CZ + 1))
    b = field_at(a, top, u)
    first_step(a, b, before, u, CZ)
    u = advance_u(u)
    above = tuple(x * in_hi for x in grow(top, CZ + 2))
    before = (b[0], b[1])
    b = field_at(top, above, u)
    first_step(top, b, before, u, CZ + 1, in_hi)

    def new_at(store):
        return tuple(
            jnp.concatenate(
                [
                    a1m[pl.ds(pl.multiple_of((c * (CZ + 2) + store) * CY, 8), CY), :],
                    a1e[pl.ds(pl.multiple_of((c * (CZ + 2) + store) * 8, 8), 8), :],
                ],
                axis=0,
            )
            for c in range(3)
        )

    def second_field(a, a_up, v):
        yp = (turn(a[0], -1, 0), None, turn(a[2], -1, 0))
        xp = (
            None,
            jnp.where(last_lane, v[0], turn(a[1], -1, 1)),
            jnp.where(last_lane, v[1], turn(a[2], -1, 1)),
        )
        return fields(a, a_up, yp, xp, False)

    first_main, main = first_lane[:CY], slice(0, CY)

    def level_two(z, carry):
        a, before, v = carry
        a_up = new_at(z + 2)
        b = second_field(a, a_up, v)
        ym = (turn(b[0], 1, 0)[main], None, turn(b[2], 1, 0)[main])
        own = tuple(x[main] for x in b)
        xm = (
            None,
            jnp.where(first_main, v[1][main], turn(own[1], 1, 1)),
            jnp.where(first_main, v[0][main], turn(own[2], 1, 1)),
        )
        d = drive(own, before, ym, xm)
        for c in range(3):
            out_v[pl.ds(pl.multiple_of((c * CZ + z) * CY, 8), CY), :] = a[c][main] + d[c]
        return a_up, (own[0], own[1]), advance_u(v)

    v = tuple(turn(x, CX - 3, 1) for x in (v1, v2))
    below, a = new_at(0), new_at(1)
    b = second_field(below, a, v)
    carry = (a, (b[0][main], b[1][main]), advance_u(v))
    part = 8

    def store(k, c):
        there = pl.ds(pl.multiple_of((c * CZ + k * part) * CY, 8), part * CY)
        return pltpu.make_async_copy(out_v.at[there], out_hbm.at[there], store_sem.at[k, c])

    def chunk(k, carry):
        carry = lax.fori_loop(k * part, (k + 1) * part, level_two, carry)
        for c in range(3):
            store(k, c).start()
        return carry

    lax.fori_loop(0, CZ // part, chunk, carry)
    for k in range(CZ // part):
        for c in range(3):
            store(k, c).wait()


def f32(*shape):
    return jax.ShapeDtypeStruct(shape, jnp.float32)


def vmem(*shape):
    return pltpu.VMEM(shape, jnp.float32)


def local(side_field, magnetogram):
    side = side_field.reshape(2 * CZ * CY, CX)
    whole = pl.BlockSpec(memory_space=pltpu.VMEM)
    where_it_is = pl.BlockSpec(memory_space=pl.ANY)
    dma = pltpu.SemaphoreType.DMA
    ext, zh, q, e = pl.pallas_call(
        comm_kernel,
        out_shape=(f32(2 * EZ * 8, CX), f32(6 * CY, CX), f32(2 * EY, CX), f32(8 * EY, CX)),
        in_specs=[where_it_is, whole],
        out_specs=(whole,) * 4,
        scratch_shapes=[
            vmem(2 * LEVEL, CX),
            vmem(2 * CY, CX),
            vmem(UP, 2 * CY, CX),
            vmem(DOWN, 2 * CY, CX),
        ]
        + [vmem(4 * CZ, CX)] * 4
        + [vmem(16, CX)] * 4
        + [vmem(2 * EY, CX)] * 4
        + [
            vmem(8, CX),
            vmem(CY, CX),
            vmem(8 * (NY_DEV - 1), CX),
            vmem(CY * (NX_DEV - 1), CX),
            vmem(2 * CY, CX),
            vmem(16, CX),
            vmem(16, CX),
            vmem(16, CX),
            vmem(16, CX),
            vmem(2 * CY, CX),
            vmem(2 * CY, CX),
            vmem(4, 16, CX),
        ]
        + [dma((2,))]
        + [dma((UP, 2))] * 2
        + [dma((DOWN, 2))] * 2
        + [dma((2, 2))] * 2
        + [dma((2,))] * 6
        + [dma((NY_DEV - 1,))] * 2
        + [dma((NX_DEV - 1,))] * 2
        + [dma((8,))] * 2,
        compiler_params=pltpu.CompilerParams(collective_id=0, has_side_effects=True),
        name="exchange",
    )(side, magnetogram)
    out = pl.pallas_call(
        step_kernel,
        out_shape=f32(3 * CZ * CY, CX),
        in_specs=[where_it_is] + [whole] * 4,
        out_specs=where_it_is,
        scratch_shapes=[
            vmem(2 * LEVEL, CX),
            vmem(3 * (CZ + 2) * CY, CX),
            vmem(3 * (CZ + 2) * 8, CX),
            vmem(3 * CZ * CY, CX),
            dma((2,)),
            dma((CZ // 8, 3)),
        ],
        name="steps",
    )(side, ext, zh, q, e)
    return out.reshape(3, CZ, CY, CX)


def solution(mesh):
    return jax.shard_map(
        local,
        mesh=mesh,
        in_specs=(P(None, "gz", "gy", "gx"), P("gy", "gx")),
        out_specs=P(None, "gz", "gy", "gx"),
        check_vma=False,
    )
```

```python
import functools

import jax
import jax.numpy as jnp
from jax import lax
from jax.experimental import pallas as pl
from jax.experimental.pallas import tpu as pltpu
from jax.sharding import PartitionSpec as P

spacing = 0.0625
friction = 0.004
MESH = pl.DeviceIdType.MESH

NZ_DEV, NY_DEV, NX_DEV = 8, 8, 4
CZ, CY, CX = 48, 32, 128
EZ = CZ + 3
EY = CY + 8
LEVEL = EZ * CY


def lanes(shape):
    return lax.broadcasted_iota(jnp.int32, shape, len(shape) - 1)


def rows(shape):
    return lax.broadcasted_iota(jnp.int32, shape, len(shape) - 2)


def comm_kernel(
    side_hbm,
    mag_ref,
    ext_out,
    zh_out,
    q_out,
    e_out,
    side_v,
    t_v,
    tr,
    ys_lo,
    ys_hi,
    yr_lo,
    yr_hi,
    cs_lo,
    cs_hi,
    cr_lo,
    cr_hi,
    w_hi,
    w_lo,
    wn_hi,
    wn_lo,
    wt_lo,
    wt_hi,
    wy_lo,
    wy_hi,
    wd,
    mc_s,
    mr_s,
    mc_r,
    mr_r,
    q_v,
    qt_lo,
    qt_hi,
    qy_lo,
    qy_hi,
    qx_lo,
    qx_hi,
    qd,
    load_sem,
    s_t,
    r_t,
    s_z,
    r_z,
    s_y,
    r_y,
    s_c,
    r_c,
    s_w,
    r_w,
    s_mc,
    r_mc,
    s_mr,
    r_mr,
    s_q,
    r_q,
):
    gz, gy, gx = lax.axis_index("gz"), lax.axis_index("gy"), lax.axis_index("gx")

    def at(dz=0, dy=0, dx=0):
        where = {}
        if dz:
            where["gz"] = lax.rem(gz + dz + NZ_DEV, NZ_DEV)
        if dy:
            where["gy"] = lax.rem(gy + dy + NY_DEV, NY_DEV)
        if dx:
            where["gx"] = lax.rem(gx + dx + NX_DEV, NX_DEV)
        return where

    def there(dz=0, dy=0, dx=0):
        ok = None
        for here, d, size in ((gz, dz, NZ_DEV), (gy, dy, NY_DEV), (gx, dx, NX_DEV)):
            if d:
                one = here + d < size if d > 0 else here + d >= 0
                ok = one if ok is None else jnp.logical_and(ok, one)
        return ok

    class Hop:
        def __init__(self, src, dst, ssem, rsem, **by):
            self.copy = pltpu.make_async_remote_copy(
                src_ref=src,
                dst_ref=dst,
                send_sem=ssem,
                recv_sem=rsem,
                device_id=at(**by),
                device_id_type=MESH,
            )
            self.to = there(**by)
            self.back = there(**{k: -v for k, v in by.items()})

        def start(self):
            pl.when(self.to)(self.copy.start)

        def wait_send(self):
            pl.when(self.to)(self.copy.wait_send)

        def wait_recv(self):
            pl.when(self.back)(self.copy.wait_recv)

    loads = [
        pltpu.make_async_copy(
            side_hbm.at[pl.ds(c * CZ * CY, CZ * CY)],
            side_v.at[pl.ds(c * LEVEL + CY, CZ * CY)],
            load_sem.at[c],
        )
        for c in range(2)
    ]
    for load in loads:
        load.start()

    barrier = pltpu.get_barrier_semaphore()
    for peer in (
        [at(dz=d) for d in range(1, NZ_DEV)]
        + [at(dy=d) for d in range(1, NY_DEV)]
        + [at(dx=d) for d in range(1, NX_DEV)]
    ):
        pl.semaphore_signal(barrier, inc=1, device_id=peer, device_id_type=MESH)
    diagonal = [dict(dy=a, dx=b) for a in (1, -1) for b in (1, -1)]
    greeted = jnp.int32(NZ_DEV + NY_DEV + NX_DEV - 3)
    for by in diagonal:
        greeted = greeted + there(**by).astype(jnp.int32)

        @pl.when(there(**by))
        def _(by=by):
            pl.semaphore_signal(barrier, inc=1, device_id=at(**by), device_id_type=MESH)

    mag = mag_ref[...]
    mc_s[...] = jnp.broadcast_to(jnp.sum(mag, axis=0, keepdims=True), (8, CX))
    mr_s[...] = jnp.broadcast_to(jnp.sum(mag, axis=1, keepdims=True), (CY, CX))
    ext_out[...] = jnp.zeros_like(ext_out)

    def clear(by, *refs):
        @pl.when(jnp.logical_not(there(**by)))
        def _():
            for ref in refs:
                ref[...] = jnp.zeros_like(ref)

    clear(dict(dz=-1), side_v.at[pl.ds(0, CY)], side_v.at[pl.ds(LEVEL, CY)])
    clear(
        dict(dz=1),
        side_v.at[pl.ds((CZ + 1) * CY, 2 * CY)],
        side_v.at[pl.ds(LEVEL + (CZ + 1) * CY, 2 * CY)],
    )
    clear(dict(dy=-1), yr_lo, cr_lo, wy_lo, qy_lo)
    clear(dict(dy=1), yr_hi, cr_hi, wy_hi, qy_hi)
    clear(dict(dx=-1), wn_lo, qx_lo)
    clear(dict(dx=1), wn_hi, qx_hi)
    for i, by in enumerate((dict(dy=1, dx=-1), dict(dy=1, dx=1), dict(dy=-1, dx=-1), dict(dy=-1, dx=1))):
        clear(by, wd.at[i], qd.at[i])

    for c in range(2):
        loads[c].wait()

        def add(z, total, c=c):
            return total + side_v[pl.ds(c * LEVEL + (z + 1) * CY, CY), :]

        t_v[pl.ds(c * CY, CY), :] = lax.fori_loop(
            0, CZ, add, jnp.zeros((CY, CX), jnp.float32), unroll=8
        )
    pl.semaphore_wait(barrier, greeted)

    layers = []
    for c in range(2):
        layers.append(
            Hop(
                side_hbm.at[pl.ds(c * CZ * CY + (CZ - 1) * CY, CY)],
                side_v.at[pl.ds(c * LEVEL, CY)],
                s_z.at[0, c],
                r_z.at[0, c],
                dz=1,
            )
        )
        layers.append(
            Hop(
                side_hbm.at[pl.ds(c * CZ * CY, 2 * CY)],
                side_v.at[pl.ds(c * LEVEL + (CZ + 1) * CY, 2 * CY)],
                s_z.at[1, c],
                r_z.at[1, c],
                dz=-1,
            )
        )
    for one in layers:
        one.start()

    ups = [
        Hop(t_v, tr.at[d - 1], s_t.at[d - 1], r_t.at[d - 1], dz=d) for d in (4, 5, 3, 6, 2, 7, 1)
    ]
    for one in ups:
        one.start()

    sums = [
        Hop(mc_s, mc_r.at[pl.ds(8 * (d - 1), 8)], s_mc.at[d - 1], r_mc.at[d - 1], dy=d)
        for d in range(1, NY_DEV)
    ] + [
        Hop(mr_s, mr_r.at[pl.ds(CY * (d - 1), CY)], s_mr.at[d - 1], r_mr.at[d - 1], dx=d)
        for d in range(1, NX_DEV)
    ]
    for one in sums:
        one.start()

    for c in range(2):
        for k in range(2):
            here = pl.ds((2 * c + k) * CZ, CZ)
            ys_lo[here, :] = side_v[pl.ds(c * LEVEL + CY + k, CZ, stride=CY), :]
            ys_hi[here, :] = side_v[pl.ds(c * LEVEL + CY + CY - 2 + k, CZ, stride=CY), :]
    faces = [
        Hop(ys_lo, yr_hi, s_y.at[0], r_y.at[0], dy=-1),
        Hop(ys_hi, yr_lo, s_y.at[1], r_y.at[1], dy=1),
    ]
    for one in faces:
        one.start()

    main_lane = lanes((CY, CX))

    def main(c, level):
        return side_v[pl.ds(pl.multiple_of(c * LEVEL + level * CY, 8), CY), :]

    def place(zi, running, packed):
        first = 2 * zi
        out = []
        for c in range(2):
            turned = pltpu.roll(running[c], first + 2, 1)
            hi, lo = packed[2 * c], packed[2 * c + 1]
            out.append(jnp.where((main_lane == first) | (main_lane == first + 1), turned, hi))
            out.append(jnp.where((main_lane == first + 2) | (main_lane == first + 3), turned, lo))
        return tuple(out)

    nothing = jnp.zeros((CY, CX), jnp.float32)

    def pack(zi, carry):
        running, packed = carry
        running = tuple(running[c] + main(c, zi - 1) for c in range(2))
        return running, place(zi, running, packed)

    running, packed = lax.fori_loop(
        2, CZ + 2, pack, ((nothing,) * 2, (nothing,) * 4), unroll=4
    )

    for one in layers:
        one.wait_recv()
    for zi in (CZ + 2, CZ + 3):
        running, packed = pack(zi, (running, packed))
    packed = place(0, tuple(-main(c, 0) for c in range(2)), packed)
    for c in range(2):
        for k, (ref, x) in enumerate(((w_hi, packed[2 * c]), (w_lo, packed[2 * c + 1]))):
            ref[pl.ds(c * CY, CY), :] = x
            wt_lo[pl.ds((2 * k + c) * 8, 8), :] = x[:8]
            wt_hi[pl.ds((2 * k + c) * 8, 8), :] = x[CY - 8 :]
    columns = [
        Hop(w_hi, wn_lo, s_w.at[0], r_w.at[0], dx=1),
        Hop(w_lo, wn_hi, s_w.at[1], r_w.at[1], dx=-1),
        Hop(wt_lo, wy_hi, s_w.at[2], r_w.at[2], dy=-1),
        Hop(wt_hi, wy_lo, s_w.at[3], r_w.at[3], dy=1),
        Hop(wt_lo.at[pl.ds(0, 16)], wd.at[0], s_w.at[4], r_w.at[4], dy=-1, dx=1),
        Hop(wt_lo.at[pl.ds(16, 16)], wd.at[1], s_w.at[5], r_w.at[5], dy=-1, dx=-1),
        Hop(wt_hi.at[pl.ds(0, 16)], wd.at[2], s_w.at[6], r_w.at[6], dy=1, dx=1),
        Hop(wt_hi.at[pl.ds(16, 16)], wd.at[3], s_w.at[7], r_w.at[7], dy=1, dx=-1),
    ]
    for one in columns:
        one.start()

    for c in range(2):
        for i, level in enumerate((0, CZ + 1, CZ + 2)):
            first = c * LEVEL + level * CY
            to = (c * 3 + i) * 2
            cs_lo[pl.ds(to, 2), :] = side_v[pl.ds(first, 2), :]
            cs_hi[pl.ds(to, 2), :] = side_v[pl.ds(first + CY - 2, 2), :]
            zh_out[pl.ds((c * 3 + i) * CY, CY), :] = side_v[pl.ds(first, CY), :]
    cs_lo[pl.ds(12, 4), :] = jnp.zeros((4, CX), jnp.float32)
    cs_hi[pl.ds(12, 4), :] = jnp.zeros((4, CX), jnp.float32)
    corners = [
        Hop(cs_lo, cr_hi, s_c.at[0], r_c.at[0], dy=-1),
        Hop(cs_hi, cr_lo, s_c.at[1], r_c.at[1], dy=1),
    ]
    for one in corners:
        one.start()

    col = mag
    row_of = rows((CY, CX))
    for k in (1, 2, 4, 8, 16):
        col = col + jnp.where(row_of >= k, pltpu.roll(col, k, 0), 0.0)
    lin = mag
    lane_of = lanes((CY, CX))
    for k in (1, 2, 4, 8, 16, 32, 64):
        lin = lin + jnp.where(lane_of >= k, pltpu.roll(lin, k, 1), 0.0)
    q_v[pl.ds(0, CY), :] = col
    q_v[pl.ds(CY, CY), :] = lin
    for d, one in enumerate(sums[: NY_DEV - 1]):

        @pl.when(one.back)
        def _(d=d, one=one):
            one.wait_recv()
            q_v[pl.ds(0, CY), :] = q_v[pl.ds(0, CY), :] + mc_r[pl.ds(8 * d, 1), :]

    for d, one in enumerate(sums[NY_DEV - 1 :]):

        @pl.when(one.back)
        def _(d=d, one=one):
            one.wait_recv()
            q_v[pl.ds(CY, CY), :] = q_v[pl.ds(CY, CY), :] + mr_r[pl.ds(CY * d, CY), :]

    q_v[pl.ds(0, CY), :] = (-0.5 * spacing) * q_v[pl.ds(0, CY), :]
    q_v[pl.ds(CY, CY), :] = (0.5 * spacing) * q_v[pl.ds(CY, CY), :]

    for one in faces:
        one.wait_recv()
    for c in range(2):
        for k in range(2):
            here = pl.ds((2 * c + k) * CZ, CZ)
            ext_out[pl.ds((c * EZ + 1) * 8 + k, CZ, stride=8), :] = yr_hi[here, :]
            ext_out[pl.ds((c * EZ + 1) * 8 + 6 + k, CZ, stride=8), :] = yr_lo[here, :]

    for one in ups:

        @pl.when(one.back)
        def _(one=one):
            one.wait_recv()

    for d in range(1, NZ_DEV):

        @pl.when(there(dz=-d))
        def _(d=d):
            q_v[pl.ds(0, CY), :] = q_v[pl.ds(0, CY), :] + spacing * tr[d - 1, pl.ds(CY, CY), :]
            q_v[pl.ds(CY, CY), :] = q_v[pl.ds(CY, CY), :] - spacing * tr[d - 1, pl.ds(0, CY), :]

    q = tuple(q_v[pl.ds(c * CY, CY), :] for c in range(2))
    for c in range(2):
        qt_lo[pl.ds(c * 8, 8), :] = q[c][:8]
        qt_hi[pl.ds(c * 8, 8), :] = q[c][CY - 8 :]
    planes = [
        Hop(q_v, qx_lo, s_q.at[0], r_q.at[0], dx=1),
        Hop(q_v, qx_hi, s_q.at[1], r_q.at[1], dx=-1),
        Hop(qt_lo, qy_hi, s_q.at[2], r_q.at[2], dy=-1),
        Hop(qt_hi, qy_lo, s_q.at[3], r_q.at[3], dy=1),
        Hop(qt_lo, qd.at[0], s_q.at[4], r_q.at[4], dy=-1, dx=1),
        Hop(qt_lo, qd.at[1], s_q.at[5], r_q.at[5], dy=-1, dx=-1),
        Hop(qt_hi, qd.at[2], s_q.at[6], r_q.at[6], dy=1, dx=1),
        Hop(qt_hi, qd.at[3], s_q.at[7], r_q.at[7], dy=1, dx=-1),
    ]
    for one in planes:
        one.start()

    for one in corners:
        one.wait_recv()
    for c in range(2):
        for i, level in enumerate((0, CZ + 1, CZ + 2)):
            first = (c * EZ + level) * 8
            of = (c * 3 + i) * 2
            ext_out[pl.ds(first, 2), :] = cr_hi[pl.ds(of, 2), :]
            ext_out[pl.ds(first + 6, 2), :] = cr_lo[pl.ds(of, 2), :]

    row8 = rows((8, CX))

    def plane(middle, from_hi, from_lo):
        tile = jnp.where(row8 < 2, from_hi, jnp.where(row8 >= 6, from_lo, 0.0))
        return jnp.concatenate([middle, tile], axis=0)

    for one in columns:
        one.wait_recv()

    lane = lanes((EY, CX))
    even = lane % 2 == 0
    level_ok = ((lane >= 4) | (gz > 0)) & ((lane < 2 * (CZ + 2)) | (gz < NZ_DEV - 1))
    grown = []
    for c in range(2):
        o, sign = (1, spacing) if c == 0 else (0, -spacing)
        mine, tile = pl.ds(o * CY, CY), pl.ds(o * 8, 8)
        other = pl.ds(16 + o * 8, 8)
        hi = plane(w_hi[mine, :], wy_hi[tile, :], wy_lo[tile, :])
        lo = plane(w_lo[mine, :], wy_hi[other, :], wy_lo[other, :])
        lon = plane(wn_lo[mine, :], wd[0, tile, :], wd[2, tile, :])
        hin = plane(wn_hi[mine, :], wd[1, tile, :], wd[3, tile, :])
        pairs = (
            (hi, pltpu.roll(lon, 1, 1)),
            (pltpu.roll(hi, CX - 1, 1), lon),
            (pltpu.roll(hin, CX - 2, 1), pltpu.roll(lo, CX - 1, 1)),
            (pltpu.roll(hin, CX - 3, 1), pltpu.roll(lo, CX - 2, 1)),
        )
        grown.append([sign * jnp.where(even, *pair) for pair in pairs])

    for one in planes:
        one.wait_recv()
    for c in range(2):
        tile = pl.ds(c * 8, 8)
        own = plane(q[c], qy_hi[tile, :], qy_lo[tile, :])
        low = plane(qx_lo[pl.ds(c * CY, CY), :], qd[0, tile, :], qd[2, tile, :])
        high = plane(qx_hi[pl.ds(c * CY, CY), :], qd[1, tile, :], qd[3, tile, :])
        q_out[pl.ds(c * EY, EY), :] = own

        def spread(x, i):
            return jnp.broadcast_to(x[:, i : i + 1], (EY, CX))

        sides = (
            (spread(own, 126), spread(low, 126)),
            (spread(own, 127), spread(low, 127)),
            (spread(high, 0), spread(own, 0)),
            (spread(high, 1), spread(own, 1)),
        )
        for m, pair in enumerate(sides):
            value = jnp.where(even, *pair) + grown[c][m]
            e_out[pl.ds((m * 2 + c) * EY, EY), :] = jnp.where(level_ok, value, 0.0)

    for one in ups + sums + layers + faces + corners + columns + planes:
        one.wait_send()


def turn(x, shift, axis):
    return pltpu.roll(x, shift % x.shape[axis], axis)


def fields(a, zp, yp, xp, first):
    ax, ay = a[0], a[1]
    if first:
        bx = ay - zp[1]
        by = zp[0] - ax
    else:
        bx = (yp[2] - a[2]) - (zp[1] - ay)
        by = (zp[0] - ax) - (xp[2] - a[2])
    bz = (xp[1] - ay) - (yp[0] - ax)
    return bx, by, bz


def drive(b, zm, ym, xm):
    bx, by, bz = b
    jx = (bz - ym[2]) - (by - zm[1])
    jy = (bx - zm[0]) - (bz - xm[2])
    jz = (by - xm[1]) - (bx - ym[0])
    square = bx * bx + by * by + bz * bz
    scale = (friction / spacing**2) / (square + spacing**2)
    along = (jx * bx + jy * by + jz * bz) * scale
    across = square * scale
    return (along * bx - across * jx, along * by - across * jy, along * bz - across * jz)


def step_kernel(
    side_hbm,
    ext_ref,
    zh_ref,
    q_ref,
    e_ref,
    out_hbm,
    side_v,
    a1m,
    a1e,
    out_v,
    load_sem,
    store_sem,
):
    gz, gy, gx = lax.axis_index("gz"), lax.axis_index("gy"), lax.axis_index("gx")
    loads = [
        pltpu.make_async_copy(
            side_hbm.at[pl.ds(c * CZ * CY, CZ * CY)],
            side_v.at[pl.ds(c * LEVEL + CY, CZ * CY)],
            load_sem.at[c],
        )
        for c in range(2)
    ]
    for load in loads:
        load.start()
    for c in range(2):
        for i, level in enumerate((0, CZ + 1, CZ + 2)):
            side_v[pl.ds(c * LEVEL + level * CY, CY), :] = zh_ref[pl.ds((c * 3 + i) * CY, CY), :]

    shape = (EY, CX)
    lane, row = lanes(shape), rows(shape)
    even = lane % 2 == 0
    row_ok = ((row < CY) | (row >= CY + 2) | (gy < NY_DEV - 1)) & (
        (row < CY + 2) | (gy > 0)
    )

    ea = [[e_ref[pl.ds((m * 2 + c) * EY, EY), :] for c in range(2)] for m in range(4)]
    eb = []
    for m in range(3):
        up_y = (turn(ea[m][0], -1, 0),)
        up_z = tuple(turn(x, -2, 1) for x in ea[m])
        eb.append(fields(ea[m], up_z, up_y, ea[m + 1], True))
    ea1 = []
    for m in (1, 2):
        down_z = tuple(turn(x, 2, 1) for x in eb[m])
        down_y = tuple(turn(x, 1, 0) for x in eb[m])
        d = drive(eb[m], down_z, down_y, eb[m - 1])
        outside = (lane % 2 == 1) & (gx == 0) if m == 1 else (lane % 2 == 0) & (gx == NX_DEV - 1)
        ok = (
            row_ok
            & jnp.logical_not(outside)
            & ((lane >= 4) | (gz > 0))
            & ((lane < 2 * (CZ + 2)) | (gz < NZ_DEV - 1))
        )
        a = (ea[m][0] + d[0], ea[m][1] + d[1], d[2])
        ea1.append(tuple(jnp.where(ok, x, 0.0) for x in a))
    u1 = jnp.where(even, ea[2][1], eb[1][2])
    u2 = eb[1][1]
    near = ea1[0]
    eb1 = fields(
        near,
        tuple(turn(x, -2, 1) for x in near),
        tuple(turn(x, -1, 0) for x in near),
        ea1[1],
        False,
    )
    v1 = jnp.where(even, ea1[1][1], eb1[2])
    v2 = jnp.where(even, ea1[1][2], eb1[1])

    def raw(c, level):
        return jnp.concatenate(
            [
                side_v[pl.ds(pl.multiple_of(c * LEVEL + level * CY, 8), CY), :],
                ext_ref[pl.ds(pl.multiple_of((c * EZ + level) * 8, 8), 8), :],
            ],
            axis=0,
        )

    in_lo = (gz > 0).astype(jnp.float32)
    in_hi = (gz < NZ_DEV - 1).astype(jnp.float32)
    first_lane, last_lane = lane == 0, lane == CX - 1
    tile_row = rows((8, CX))
    tile_ok = ((tile_row >= 2) | (gy < NY_DEV - 1)) & ((tile_row < 2) | (gy > 0))

    def grow(a, level):
        return (a[0] + spacing * raw(1, level), a[1] - spacing * raw(0, level))

    def field_at(a, a_up, u):
        xp = (None, jnp.where(last_lane, u[0], turn(a[1], -1, 1)))
        return fields(a, a_up, (turn(a[0], -1, 0),), xp, True)

    def first_step(a, b, before, u, store, ok=None):
        xm = (
            None,
            jnp.where(first_lane, u[1], turn(b[1], 1, 1)),
            jnp.where(first_lane, u[0], turn(b[2], 1, 1)),
        )
        ym = (turn(b[0], 1, 0), None, turn(b[2], 1, 0))
        d = drive(b, before, ym, xm)
        new = (a[0] + d[0], a[1] + d[1], d[2])
        for c in range(3):
            x = new[c] if ok is None else new[c] * ok
            a1m[pl.ds(pl.multiple_of((c * (CZ + 2) + store) * CY, 8), CY), :] = x[:CY]
            a1e[pl.ds(pl.multiple_of((c * (CZ + 2) + store) * 8, 8), 8), :] = jnp.where(
                tile_ok, x[CY:], 0.0
            )

    def advance_u(u):
        return tuple(turn(x, -2, 1) for x in u)

    for load in loads:
        load.wait()
    q = tuple(q_ref[pl.ds(c * EY, EY), :] for c in range(2))
    bottom = tuple(x * in_lo for x in q)
    lowest = (
        (q[0] - spacing * raw(1, 0)) * in_lo,
        (q[1] + spacing * raw(0, 0)) * in_lo,
    )
    u = tuple(turn(x, CX - 1, 1) for x in (u1, u2))
    b = field_at(lowest, bottom, u)
    u = advance_u(u)
    a = grow(q, 1)
    before = (b[0], b[1])
    b = field_at(bottom, a, u)
    first_step(bottom, b, before, u, 0, in_lo)
    u = advance_u(u)

    def level_one(z, carry):
        a, before = carry
        a_up = grow(a, z + 2)
        u = tuple(pltpu.roll(x, lax.rem(2 * CX - 1 - 2 * (z + 2), CX), 1) for x in (u1, u2))
        b = field_at(a, a_up, u)
        first_step(a, b, before, u, z + 1)
        return a_up, (b[0], b[1])

    a, before = lax.fori_loop(0, CZ - 1, level_one, (a, (b[0], b[1])), unroll=4)
    u = tuple(turn(x, CX - 1 - 2 * (CZ + 1), 1) for x in (u1, u2))
    top = tuple(x * in_hi for x in grow(a, CZ + 1))
    b = field_at(a, top, u)
    first_step(a, b, before, u, CZ)
    u = advance_u(u)
    above = tuple(x * in_hi for x in grow(top, CZ + 2))
    before = (b[0], b[1])
    b = field_at(top, above, u)
    first_step(top, b, before, u, CZ + 1, in_hi)

    def new_at(store):
        return tuple(
            jnp.concatenate(
                [
                    a1m[pl.ds(pl.multiple_of((c * (CZ + 2) + store) * CY, 8), CY), :],
                    a1e[pl.ds(pl.multiple_of((c * (CZ + 2) + store) * 8, 8), 8), :],
                ],
                axis=0,
            )
            for c in range(3)
        )

    def second_field(a, a_up, v):
        yp = (turn(a[0], -1, 0), None, turn(a[2], -1, 0))
        xp = (
            None,
            jnp.where(last_lane, v[0], turn(a[1], -1, 1)),
            jnp.where(last_lane, v[1], turn(a[2], -1, 1)),
        )
        return fields(a, a_up, yp, xp, False)

    first_main, main = first_lane[:CY], slice(0, CY)

    def level_two(z, carry):
        a, before = carry
        v = tuple(pltpu.roll(x, lax.rem(2 * CX - 1 - 2 * (z + 2), CX), 1) for x in (v1, v2))
        a_up = new_at(z + 2)
        b = second_field(a, a_up, v)
        ym = (turn(b[0], 1, 0)[main], None, turn(b[2], 1, 0)[main])
        own = tuple(x[main] for x in b)
        xm = (
            None,
            jnp.where(first_main, v[1][main], turn(own[1], 1, 1)),
            jnp.where(first_main, v[0][main], turn(own[2], 1, 1)),
        )
        d = drive(own, before, ym, xm)
        for c in range(3):
            out_v[pl.ds(pl.multiple_of((c * CZ + z) * CY, 8), CY), :] = a[c][main] + d[c]
        return a_up, (own[0], own[1])

    v = tuple(turn(x, CX - 3, 1) for x in (v1, v2))
    below, a = new_at(0), new_at(1)
    b = second_field(below, a, v)
    carry = (a, (b[0][main], b[1][main]))
    part = 8

    def store(k, c):
        there = pl.ds(pl.multiple_of((c * CZ + k * part) * CY, 8), part * CY)
        return pltpu.make_async_copy(out_v.at[there], out_hbm.at[there], store_sem.at[k, c])

    def chunk(k, carry):
        carry = lax.fori_loop(0, part, lambda i, x: level_two(k * part + i, x), carry, unroll=4)
        for c in range(3):
            store(k, c).start()
        return carry

    lax.fori_loop(0, CZ // part, chunk, carry)
    for k in range(CZ // part):
        for c in range(3):
            store(k, c).wait()


def f32(*shape):
    return jax.ShapeDtypeStruct(shape, jnp.float32)


def vmem(*shape):
    return pltpu.VMEM(shape, jnp.float32)


def local(side_field, magnetogram):
    side = side_field.reshape(2 * CZ * CY, CX)
    whole = pl.BlockSpec(memory_space=pltpu.VMEM)
    where_it_is = pl.BlockSpec(memory_space=pl.ANY)
    dma = pltpu.SemaphoreType.DMA
    ext, zh, q, e = pl.pallas_call(
        comm_kernel,
        out_shape=(f32(2 * EZ * 8, CX), f32(6 * CY, CX), f32(2 * EY, CX), f32(8 * EY, CX)),
        in_specs=[where_it_is, whole],
        out_specs=(whole,) * 4,
        scratch_shapes=[
            vmem(2 * LEVEL, CX),
            vmem(2 * CY, CX),
            vmem(NZ_DEV - 1, 2 * CY, CX),
        ]
        + [vmem(4 * CZ, CX)] * 4
        + [vmem(16, CX)] * 4
        + [vmem(2 * CY, CX)] * 4
        + [vmem(32, CX)] * 4
        + [
            vmem(4, 16, CX),
            vmem(8, CX),
            vmem(CY, CX),
            vmem(8 * (NY_DEV - 1), CX),
            vmem(CY * (NX_DEV - 1), CX),
            vmem(2 * CY, CX),
            vmem(16, CX),
            vmem(16, CX),
            vmem(16, CX),
            vmem(16, CX),
            vmem(2 * CY, CX),
            vmem(2 * CY, CX),
            vmem(4, 16, CX),
        ]
        + [dma((2,))]
        + [dma((NZ_DEV - 1,))] * 2
        + [dma((2, 2))] * 2
        + [dma((2,))] * 4
        + [dma((8,))] * 2
        + [dma((NY_DEV - 1,))] * 2
        + [dma((NX_DEV - 1,))] * 2
        + [dma((8,))] * 2,
        compiler_params=pltpu.CompilerParams(collective_id=0, has_side_effects=True),
        name="exchange",
    )(side, magnetogram)
    out = pl.pallas_call(
        step_kernel,
        out_shape=f32(3 * CZ * CY, CX),
        in_specs=[where_it_is] + [whole] * 4,
        out_specs=where_it_is,
        scratch_shapes=[
            vmem(2 * LEVEL, CX),
            vmem(3 * (CZ + 2) * CY, CX),
            vmem(3 * (CZ + 2) * 8, CX),
            vmem(3 * CZ * CY, CX),
            dma((2,)),
            dma((CZ // 8, 3)),
        ],
        name="steps",
    )(side, ext, zh, q, e)
    return out.reshape(3, CZ, CY, CX)


def solution(mesh):
    return jax.shard_map(
        local,
        mesh=mesh,
        in_specs=(P(None, "gz", "gy", "gx"), P("gy", "gx")),
        out_specs=P(None, "gz", "gy", "gx"),
        check_vma=False,
    )
```

```python
import functools

import jax
import jax.numpy as jnp
from jax import lax
from jax.experimental import pallas as pl
from jax.experimental.pallas import tpu as pltpu
from jax.sharding import PartitionSpec as P

spacing = 0.0625
friction = 0.004
MESH = pl.DeviceIdType.MESH

VMEM_BYTES = 24 * 2**20
UNROLL_PRE, UNROLL_STRIP, UNROLL_POST, UNROLL_EDGE, UNROLL_PACK = 8, 8, 4, 25, 8
NZ_DEV, NY_DEV, NX_DEV = 8, 8, 4
CZ, CY, CX = 48, 32, 128
EZ = CZ + 3
EY = CY + 8
LEVEL = EZ * CY


def lanes(shape):
    return lax.broadcasted_iota(jnp.int32, shape, len(shape) - 1)


def rows(shape):
    return lax.broadcasted_iota(jnp.int32, shape, len(shape) - 2)


def turn(x, shift, axis):
    return pltpu.roll(x, shift % x.shape[axis], axis)


def fields(a, zp, yp, xp, first):
    ax, ay = a[0], a[1]
    if first:
        bx = ay - zp[1]
        by = zp[0] - ax
    else:
        bx = (yp[2] - a[2]) - (zp[1] - ay)
        by = (zp[0] - ax) - (xp[2] - a[2])
    bz = (xp[1] - ay) - (yp[0] - ax)
    return bx, by, bz


def drive(b, zm, ym, xm):
    bx, by, bz = b
    jx = (bz - ym[2]) - (by - zm[1])
    jy = (bx - zm[0]) - (bz - xm[2])
    jz = (by - xm[1]) - (bx - ym[0])
    return push(b, (jx, jy, jz))


def push(b, j):
    bx, by, bz = b
    jx, jy, jz = j
    square = bx * bx + by * by + bz * bz
    scale = (friction / spacing**2) / (square + spacing**2)
    along = (jx * bx + jy * by + jz * bz) * scale
    across = square * scale
    return (along * bx - across * jx, along * by - across * jy, along * bz - across * jz)


def comm_kernel(
    side_hbm,
    mag_ref,
    a1_out,
    v_out,
    ext_v,
    pre_m,
    pre_e,
    side_v,
    t_v,
    tr,
    ys_lo,
    ys_hi,
    yr_lo,
    yr_hi,
    cs_lo,
    cs_hi,
    cr_lo,
    cr_hi,
    w_hi,
    w_lo,
    wn_hi,
    wn_lo,
    wt_lo,
    wt_hi,
    wy_lo,
    wy_hi,
    wd,
    mc_s,
    mr_s,
    mc_r,
    mr_r,
    q_v,
    qt_lo,
    qt_hi,
    qy_lo,
    qy_hi,
    load_sem,
    s_t,
    r_t,
    s_z,
    r_z,
    s_y,
    r_y,
    s_c,
    r_c,
    s_w,
    r_w,
    s_mc,
    r_mc,
    s_mr,
    r_mr,
    s_q,
    r_q,
):
    gz, gy, gx = lax.axis_index("gz"), lax.axis_index("gy"), lax.axis_index("gx")

    def at(dz=0, dy=0, dx=0):
        where = {}
        if dz:
            where["gz"] = lax.rem(gz + dz + NZ_DEV, NZ_DEV)
        if dy:
            where["gy"] = lax.rem(gy + dy + NY_DEV, NY_DEV)
        if dx:
            where["gx"] = lax.rem(gx + dx + NX_DEV, NX_DEV)
        return where

    def there(dz=0, dy=0, dx=0):
        ok = None
        for here, d, size in ((gz, dz, NZ_DEV), (gy, dy, NY_DEV), (gx, dx, NX_DEV)):
            if d:
                one = here + d < size if d > 0 else here + d >= 0
                ok = one if ok is None else jnp.logical_and(ok, one)
        return ok

    class Hop:
        def __init__(self, src, dst, ssem, rsem, **by):
            self.copy = pltpu.make_async_remote_copy(
                src_ref=src,
                dst_ref=dst,
                send_sem=ssem,
                recv_sem=rsem,
                device_id=at(**by),
                device_id_type=MESH,
            )
            self.to = there(**by)
            self.back = there(**{k: -v for k, v in by.items()})

        def start(self):
            pl.when(self.to)(self.copy.start)

        def wait_send(self):
            pl.when(self.to)(self.copy.wait_send)

        def wait_recv(self):
            pl.when(self.back)(self.copy.wait_recv)

    loads = [
        pltpu.make_async_copy(
            side_hbm.at[pl.ds(c * CZ * CY, CZ * CY)],
            side_v.at[pl.ds(c * LEVEL + CY, CZ * CY)],
            load_sem.at[c],
        )
        for c in range(2)
    ]
    for load in loads:
        load.start()

    barrier = pltpu.get_barrier_semaphore()
    for peer in (
        [at(dz=d) for d in range(1, NZ_DEV)]
        + [at(dy=d) for d in range(1, NY_DEV)]
        + [at(dx=d) for d in range(1, NX_DEV)]
    ):
        pl.semaphore_signal(barrier, inc=1, device_id=peer, device_id_type=MESH)
    diagonal = [dict(dy=a, dx=b) for a in (1, -1) for b in (1, -1)]
    greeted = jnp.int32(NZ_DEV + NY_DEV + NX_DEV - 3)
    for by in diagonal:
        greeted = greeted + there(**by).astype(jnp.int32)

        @pl.when(there(**by))
        def _(by=by):
            pl.semaphore_signal(barrier, inc=1, device_id=at(**by), device_id_type=MESH)

    mag = mag_ref[...]
    mc_s[...] = jnp.broadcast_to(jnp.sum(mag, axis=0, keepdims=True), (8, CX))
    mr_s[...] = jnp.broadcast_to(jnp.sum(mag, axis=1, keepdims=True), (CY, CX))

    def clear(by, *refs):
        @pl.when(jnp.logical_not(there(**by)))
        def _():
            for ref in refs:
                ref[...] = jnp.zeros_like(ref)

    clear(dict(dz=-1), side_v.at[pl.ds(0, CY)], side_v.at[pl.ds(LEVEL, CY)])
    clear(
        dict(dz=1),
        side_v.at[pl.ds((CZ + 1) * CY, 2 * CY)],
        side_v.at[pl.ds(LEVEL + (CZ + 1) * CY, 2 * CY)],
    )
    clear(dict(dy=-1), yr_lo, cr_lo, wy_lo, qy_lo)
    clear(dict(dy=1), yr_hi, cr_hi, wy_hi, qy_hi)
    clear(dict(dx=-1), wn_lo)
    clear(dict(dx=1), wn_hi)
    for i, by in enumerate((dict(dy=1, dx=-1), dict(dy=1, dx=1), dict(dy=-1, dx=-1), dict(dy=-1, dx=1))):
        clear(by, wd.at[i])

    for c in range(2):
        loads[c].wait()

        def add(z, total, c=c):
            return total + side_v[pl.ds(c * LEVEL + (z + 1) * CY, CY), :]

        t_v[pl.ds(c * CY, CY), :] = lax.fori_loop(
            0, CZ, add, jnp.zeros((CY, CX), jnp.float32), unroll=8
        )
    pl.semaphore_wait(barrier, greeted)

    layers = []
    for c in range(2):
        layers.append(
            Hop(
                side_hbm.at[pl.ds(c * CZ * CY + (CZ - 1) * CY, CY)],
                side_v.at[pl.ds(c * LEVEL, CY)],
                s_z.at[0, c],
                r_z.at[0, c],
                dz=1,
            )
        )
        layers.append(
            Hop(
                side_hbm.at[pl.ds(c * CZ * CY, 2 * CY)],
                side_v.at[pl.ds(c * LEVEL + (CZ + 1) * CY, 2 * CY)],
                s_z.at[1, c],
                r_z.at[1, c],
                dz=-1,
            )
        )
    for one in layers:
        one.start()

    ups = [
        Hop(t_v, tr.at[d - 1], s_t.at[d - 1], r_t.at[d - 1], dz=d) for d in (4, 5, 3, 6, 2, 7, 1)
    ]
    for one in ups:
        one.start()

    sums = [
        Hop(mc_s, mc_r.at[pl.ds(8 * (d - 1), 8)], s_mc.at[d - 1], r_mc.at[d - 1], dy=d)
        for d in range(1, NY_DEV)
    ] + [
        Hop(mr_s, mr_r.at[pl.ds(CY * (d - 1), CY)], s_mr.at[d - 1], r_mr.at[d - 1], dx=d)
        for d in range(1, NX_DEV)
    ]
    for one in sums:
        one.start()

    for c in range(2):
        for k in range(2):
            here = pl.ds((2 * c + k) * CZ, CZ)
            ys_lo[here, :] = side_v[pl.ds(c * LEVEL + CY + k, CZ, stride=CY), :]
            ys_hi[here, :] = side_v[pl.ds(c * LEVEL + CY + CY - 2 + k, CZ, stride=CY), :]
    faces = [
        Hop(ys_lo, yr_hi, s_y.at[0], r_y.at[0], dy=-1),
        Hop(ys_hi, yr_lo, s_y.at[1], r_y.at[1], dy=1),
    ]
    for one in faces:
        one.start()

    main_lane = lanes((CY, CX))

    def main(c, level):
        return side_v[pl.ds(pl.multiple_of(c * LEVEL + level * CY, 8), CY), :]

    def place(zi, running, packed):
        first = 2 * zi
        out = []
        for c in range(2):
            turned = pltpu.roll(running[c], first + 2, 1)
            hi, lo = packed[2 * c], packed[2 * c + 1]
            out.append(jnp.where((main_lane == first) | (main_lane == first + 1), turned, hi))
            out.append(jnp.where((main_lane == first + 2) | (main_lane == first + 3), turned, lo))
        return tuple(out)

    nothing = jnp.zeros((CY, CX), jnp.float32)

    def pack(zi, carry):
        running, packed = carry
        running = tuple(running[c] + main(c, zi - 1) for c in range(2))
        return running, place(zi, running, packed)

    running, packed = lax.fori_loop(
        2, CZ + 2, pack, ((nothing,) * 2, (nothing,) * 4), unroll=UNROLL_PACK
    )

    def slot(k, z, high):
        return pl.ds(pl.multiple_of((k * (CZ + 2) + z + 1) * high, 8), high)

    class Strip:
        def __init__(self, source, store, high):
            self.source, self.store, self.high = source, store, high

        def raw(self, c, level):
            first = pl.multiple_of((c * EZ + level) * self.high, 8)
            return spacing * self.source[pl.ds(first, self.high), :]

        def level(self, z, ax, ay, before):
            bx, by = self.raw(0, z + 2), self.raw(1, z + 2)
            bz = (turn(ay, -1, 1) - ay) - (turn(ax, -1, 0) - ax)
            values = (
                bx,
                by,
                bz,
                (bz - turn(bz, 1, 0)) - (by - before[1]),
                (bx - before[0]) - (bz - turn(bz, 1, 1)),
                (by - turn(by, 1, 1)) - (bx - turn(bx, 1, 0)),
                ax,
                ay,
            )
            for k, x in enumerate(values):
                self.store[slot(k, z, self.high), :] = x
            return ax + by, ay - bx, (bx, by)

        def middle(self, unroll):
            ground = (self.raw(0, 1), self.raw(1, 1))
            return lax.fori_loop(
                0,
                CZ - 1,
                lambda z, carry: self.level(z, *carry),
                (ground[1], -ground[0], ground),
                unroll=unroll,
            )

        def ends(self, ax, ay, before):
            level_zero = jnp.zeros((self.high, CX), jnp.float32)
            self.level(-1, level_zero, level_zero, (self.raw(0, 0), self.raw(1, 0)))
            ax, ay, before = self.level(CZ - 1, ax, ay, before)
            self.level(CZ, ax, ay, before)

        def at_the_bounds(self, qx, qy):
            pre, high = self.store, self.high

            @pl.when(gz == 0)
            def _():
                pre[slot(3, 0, high), :] = pre[slot(3, 0, high), :] + qx
                pre[slot(4, 0, high), :] = pre[slot(4, 0, high), :] + qy

            @pl.when(gz == NZ_DEV - 1)
            def _():
                z = CZ - 1
                bx, by = pre[slot(0, z, high), :], pre[slot(1, z, high), :]
                tx = pre[slot(7, z, high), :] + qy
                ty = -(pre[slot(6, z, high), :] + qx)
                pre[slot(0, z, high), :] = tx
                pre[slot(1, z, high), :] = ty
                pre[slot(3, z, high), :] = pre[slot(3, z, high), :] - (ty - by)
                pre[slot(4, z, high), :] = pre[slot(4, z, high), :] + (tx - bx)
                pre[slot(5, z, high), :] = (ty - turn(ty, 1, 1)) - (tx - turn(tx, 1, 0))

        def finish(self, z, planes_of):
            qx, qy, cz, cjx, cjy = planes_of
            bx, by, bz, jx, jy, jz, ax, ay = (
                self.store[slot(k, z, self.high), :] for k in range(8)
            )
            d = push((bx, by, bz + cz), (jx + cjx, jy + cjy, jz))
            return (ax + qx + d[0], ay + qy + d[1], d[2])

    def planes_for(qx, qy):
        cz = (turn(qy, -1, 1) - qy) - (turn(qx, -1, 0) - qx)
        return qx, qy, cz, cz - turn(cz, 1, 0), turn(cz, 1, 1) - cz

    block = Strip(side_v, pre_m, CY)
    strip = Strip(ext_v, pre_e, 8)
    block_end = block.middle(UNROLL_PRE)

    col = mag
    row_of = rows((CY, CX))
    for k in (1, 2, 4, 8, 16):
        col = col + jnp.where(row_of >= k, pltpu.roll(col, k, 0), 0.0)
    lin = mag
    lane_of = lanes((CY, CX))
    for k in (1, 2, 4, 8, 16, 32, 64):
        lin = lin + jnp.where(lane_of >= k, pltpu.roll(lin, k, 1), 0.0)
    q_v[pl.ds(0, CY), :] = col
    q_v[pl.ds(CY, CY), :] = lin
    for d, one in enumerate(sums[: NY_DEV - 1]):

        @pl.when(one.back)
        def _(d=d, one=one):
            one.wait_recv()
            q_v[pl.ds(0, CY), :] = q_v[pl.ds(0, CY), :] + mc_r[pl.ds(8 * d, 1), :]

    for d, one in enumerate(sums[NY_DEV - 1 :]):

        @pl.when(one.back)
        def _(d=d, one=one):
            one.wait_recv()
            q_v[pl.ds(CY, CY), :] = q_v[pl.ds(CY, CY), :] + mr_r[pl.ds(CY * d, CY), :]

    q_v[pl.ds(0, CY), :] = (-0.5 * spacing) * q_v[pl.ds(0, CY), :]
    q_v[pl.ds(CY, CY), :] = (0.5 * spacing) * q_v[pl.ds(CY, CY), :]

    for one in faces:
        one.wait_recv()
    for c in range(2):
        for k in range(2):
            here = pl.ds((2 * c + k) * CZ, CZ)
            for j, ref in enumerate((ys_hi, yr_hi, yr_lo, ys_lo)):
                ext_v[pl.ds((c * EZ + 1) * 8 + 2 * j + k, CZ, stride=8), :] = ref[here, :]

    strip_end = strip.middle(UNROLL_STRIP)

    for one in layers:
        one.wait_recv()
    for zi in (CZ + 2, CZ + 3):
        running, packed = pack(zi, (running, packed))
    packed = place(0, tuple(-main(c, 0) for c in range(2)), packed)

    for c in range(2):
        for i, level in enumerate((0, CZ + 1, CZ + 2)):
            first = c * LEVEL + level * CY
            to = (c * 3 + i) * 2
            cs_lo[pl.ds(to, 2), :] = side_v[pl.ds(first, 2), :]
            cs_hi[pl.ds(to, 2), :] = side_v[pl.ds(first + CY - 2, 2), :]
    cs_lo[pl.ds(12, 4), :] = jnp.zeros((4, CX), jnp.float32)
    cs_hi[pl.ds(12, 4), :] = jnp.zeros((4, CX), jnp.float32)
    corners = [
        Hop(cs_lo, cr_hi, s_c.at[0], r_c.at[0], dy=-1),
        Hop(cs_hi, cr_lo, s_c.at[1], r_c.at[1], dy=1),
    ]
    for one in corners:
        one.start()

    block.ends(*block_end)

    for one in ups:

        @pl.when(one.back)
        def _(one=one):
            one.wait_recv()

    for d in range(1, NZ_DEV):

        @pl.when(there(dz=-d))
        def _(d=d):
            q_v[pl.ds(0, CY), :] = q_v[pl.ds(0, CY), :] + spacing * tr[d - 1, pl.ds(CY, CY), :]
            q_v[pl.ds(CY, CY), :] = q_v[pl.ds(CY, CY), :] - spacing * tr[d - 1, pl.ds(0, CY), :]

    q = tuple(q_v[pl.ds(c * CY, CY), :] for c in range(2))
    def spread(x, i):
        return jnp.broadcast_to(x[:, i : i + 1], x.shape)

    main_even = main_lane % 2 == 0
    for c in range(2):
        o, sign = (1, spacing) if c == 0 else (0, -spacing)
        hi = jnp.where(main_even, spread(q[c], CX - 2), spread(q[c], CX - 1))
        lo = jnp.where(main_even, spread(q[c], 0), spread(q[c], 1))
        hi, lo = hi + sign * packed[2 * o], lo + sign * packed[2 * o + 1]
        for k, (ref, x) in enumerate(((w_hi, hi), (w_lo, lo))):
            ref[pl.ds(c * CY, CY), :] = x
            wt_lo[pl.ds((2 * k + c) * 8, 8), :] = x[:8]
            wt_hi[pl.ds((2 * k + c) * 8, 8), :] = x[CY - 8 :]
        qt_lo[pl.ds(c * 8, 8), :] = q[c][:8]
        qt_hi[pl.ds(c * 8, 8), :] = q[c][CY - 8 :]
    columns = [
        Hop(w_hi, wn_lo, s_w.at[0], r_w.at[0], dx=1),
        Hop(w_lo, wn_hi, s_w.at[1], r_w.at[1], dx=-1),
        Hop(wt_lo.at[pl.ds(0, 16)], wd.at[0], s_w.at[4], r_w.at[4], dy=-1, dx=1),
        Hop(wt_lo.at[pl.ds(16, 16)], wd.at[1], s_w.at[5], r_w.at[5], dy=-1, dx=-1),
        Hop(wt_hi.at[pl.ds(0, 16)], wd.at[2], s_w.at[6], r_w.at[6], dy=1, dx=1),
        Hop(wt_hi.at[pl.ds(16, 16)], wd.at[3], s_w.at[7], r_w.at[7], dy=1, dx=-1),
        Hop(wt_lo, wy_hi, s_w.at[2], r_w.at[2], dy=-1),
        Hop(wt_hi, wy_lo, s_w.at[3], r_w.at[3], dy=1),
        Hop(qt_lo, qy_hi, s_q.at[0], r_q.at[0], dy=-1),
        Hop(qt_hi, qy_lo, s_q.at[1], r_q.at[1], dy=1),
    ]
    for one in columns:
        one.start()

    block.at_the_bounds(*q)
    block_planes = planes_for(*q)

    def finish_block(z, _):
        new = block.finish(z, block_planes)
        for c in range(3):
            first = pl.multiple_of((c * (CZ + 2) + z + 1) * EY, 8)
            a1_out[pl.ds(first, CY), :] = new[c]
        return 0

    lax.fori_loop(-1, CZ + 1, finish_block, 0, unroll=UNROLL_POST)

    for one in corners:
        one.wait_recv()
    for c in range(2):
        for i, level in enumerate((0, CZ + 1, CZ + 2)):
            first = (c * EZ + level) * 8
            of = pl.ds((c * 3 + i) * 2, 2)
            for j, ref in enumerate((cs_hi, cr_hi, cr_lo, cs_lo)):
                ext_v[pl.ds(first + 2 * j, 2), :] = ref[of, :]
    strip.ends(*strip_end)

    row8 = rows((8, CX))

    def plane(middle, from_hi, from_lo):
        tile = jnp.where(row8 < 2, from_hi, jnp.where(row8 >= 6, from_lo, 0.0))
        return jnp.concatenate([middle, tile], axis=0)

    for one in columns:
        one.wait_recv()
    lane, row = lanes((EY, CX)), rows((EY, CX))
    even = lane % 2 == 0
    level_ok = ((lane >= 4) | (gz > 0)) & ((lane < 2 * (CZ + 2)) | (gz < NZ_DEV - 1))
    ea = [[None, None] for _ in range(4)]
    carry_plane = []
    for c in range(2):
        mine, tile, other = pl.ds(c * CY, CY), pl.ds(c * 8, 8), pl.ds(16 + c * 8, 8)
        hi = plane(w_hi[mine, :], wy_hi[tile, :], wy_lo[tile, :])
        lo = plane(w_lo[mine, :], wy_hi[other, :], wy_lo[other, :])
        lon = plane(wn_lo[mine, :], wd[0, tile, :], wd[2, tile, :])
        hin = plane(wn_hi[mine, :], wd[1, tile, :], wd[3, tile, :])
        pairs = (
            (hi, turn(lon, 1, 1)),
            (turn(hi, -1, 1), lon),
            (turn(hin, -2, 1), turn(lo, -1, 1)),
            (turn(hin, -3, 1), turn(lo, -2, 1)),
        )
        for m, pair in enumerate(pairs):
            ea[m][c] = jnp.where(level_ok, jnp.where(even, *pair), 0.0)
        around = (q[c][CY - 8 :], qy_hi[tile, :], qy_lo[tile, :], q[c][:8])
        turned = [turn(x, by, 0) for x, by in zip(around, (2, 2, -2, -2))]
        carry_plane.append(
            jnp.where(
                row8 < 4,
                jnp.where(row8 < 2, turned[0], turned[1]),
                jnp.where(row8 < 6, turned[2], turned[3]),
            )
        )

    row_ok = ((row < CY) | (row >= CY + 2) | (gy < NY_DEV - 1)) & ((row < CY + 2) | (gy > 0))
    eb = []
    for m in range(3):
        up_y = (turn(ea[m][0], -1, 0),)
        up_z = tuple(turn(x, -2, 1) for x in ea[m])
        eb.append(fields(ea[m], up_z, up_y, ea[m + 1], True))
    ea1 = []
    for m in (1, 2):
        down_z = tuple(turn(x, 2, 1) for x in eb[m])
        down_y = tuple(turn(x, 1, 0) for x in eb[m])
        d = drive(eb[m], down_z, down_y, eb[m - 1])
        if m == 1:
            outside = (lane % 2 == 1) & (gx == 0)
        else:
            outside = (lane % 2 == 0) & (gx == NX_DEV - 1)
        ok = row_ok & jnp.logical_not(outside) & level_ok
        a = (ea[m][0] + d[0], ea[m][1] + d[1], d[2])
        ea1.append(tuple(jnp.where(ok, x, 0.0) for x in a))
    near = ea1[0]
    eb1 = fields(
        near,
        tuple(turn(x, -2, 1) for x in near),
        tuple(turn(x, -1, 0) for x in near),
        ea1[1],
        False,
    )
    v_out[pl.ds(0, EY), :] = jnp.where(even, ea1[1][1], eb1[2])
    v_out[pl.ds(EY, EY), :] = jnp.where(even, ea1[1][2], eb1[1])
    edge = tuple(jnp.where(even, ea1[0][c], ea1[1][c]) for c in range(3))

    strip.at_the_bounds(*carry_plane)
    strip_planes = planes_for(*carry_plane)
    rim = (lane == 0) | (lane == CX - 1)
    tile_ok = ((row8 >= 2) | (gy < NY_DEV - 1)) & ((row8 < 2) | (gy > 0))

    def finish_strip(z, _):
        new = strip.finish(z, strip_planes)
        shift = lax.rem(2 * CX - 1 - 2 * (z + 2), CX)
        for c in range(3):
            first = pl.multiple_of((c * (CZ + 2) + z + 1) * EY, 8)
            left, right = turn(new[c], -2, 0), turn(new[c], 2, 0)
            x = jnp.concatenate(
                [
                    jnp.where(row8 == 0, right, a1_out[pl.ds(first, 8), :]),
                    a1_out[pl.ds(first + 8, 16), :],
                    jnp.where(row8 == 7, left, a1_out[pl.ds(first + 24, 8), :]),
                    jnp.where(row8 < 4, left, right),
                ],
                axis=0,
            )
            x = jnp.where(rim, pltpu.roll(edge[c], shift, 1), x)
            a1_out[pl.ds(first, CY), :] = x[:CY]
            a1_out[pl.ds(first + CY, 8), :] = jnp.where(tile_ok, x[CY:], 0.0)
        return 0

    lax.fori_loop(-1, CZ + 1, finish_strip, 0, unroll=UNROLL_EDGE)

    @pl.when(gz == 0)
    def _():
        for c in range(3):
            a1_out[slot(c, -1, EY), :] = jnp.zeros((EY, CX), jnp.float32)

    @pl.when(gz == NZ_DEV - 1)
    def _():
        for c in range(3):
            a1_out[slot(c, CZ, EY), :] = jnp.zeros((EY, CX), jnp.float32)

    for one in ups + sums + layers + faces + corners + columns:
        one.wait_send()


def step_kernel(a1, v_ref, out_hbm, out_v, store_sem):
    lane = lanes((EY, CX))
    first_lane, last_lane = lane == 0, lane == CX - 1

    def new_at(z):
        return tuple(
            a1[pl.ds(pl.multiple_of((c * (CZ + 2) + z + 1) * EY, 8), EY), :] for c in range(3)
        )

    def beside(z):
        shift = lax.rem(2 * CX - 1 - 2 * (z + 2), CX)
        return tuple(pltpu.roll(v_ref[pl.ds(k * EY, EY), :], shift, 1) for k in range(2))

    def second_field(a, a_up, v):
        yp = (turn(a[0], -1, 0), None, turn(a[2], -1, 0))
        xp = (
            None,
            jnp.where(last_lane, v[0], turn(a[1], -1, 1)),
            jnp.where(last_lane, v[1], turn(a[2], -1, 1)),
        )
        return fields(a, a_up, yp, xp, False)

    first_main, main = first_lane[:CY], slice(0, CY)

    def level_two(z, carry):
        a, before = carry
        v = beside(z)
        a_up = new_at(z + 1)
        b = second_field(a, a_up, v)
        ym = (turn(b[0], 1, 0)[main], None, turn(b[2], 1, 0)[main])
        own = tuple(x[main] for x in b)
        xm = (
            None,
            jnp.where(first_main, v[1][main], turn(own[1], 1, 1)),
            jnp.where(first_main, v[0][main], turn(own[2], 1, 1)),
        )
        d = drive(own, before, ym, xm)
        for c in range(3):
            out_v[pl.ds(pl.multiple_of((c * CZ + z) * CY, 8), CY), :] = a[c][main] + d[c]
        return a_up, (own[0], own[1])

    below, a = new_at(-1), new_at(0)
    b = second_field(below, a, beside(-1))
    carry = (a, (b[0][main], b[1][main]))
    part = 8

    def store(k, c):
        there = pl.ds(pl.multiple_of((c * CZ + k * part) * CY, 8), part * CY)
        return pltpu.make_async_copy(out_v.at[there], out_hbm.at[there], store_sem.at[k, c])

    def chunk(k, carry):
        carry = lax.fori_loop(
            0, part, lambda i, x: level_two(k * part + i, x), carry, unroll=4
        )
        for c in range(3):
            store(k, c).start()
        return carry

    lax.fori_loop(0, CZ // part, chunk, carry)
    for k in range(CZ // part):
        for c in range(3):
            store(k, c).wait()


def f32(*shape):
    return jax.ShapeDtypeStruct(shape, jnp.float32)


def vmem(*shape):
    return pltpu.VMEM(shape, jnp.float32)


def local(side_field, magnetogram):
    side = pltpu.with_memory_space_constraint(side_field.reshape(2 * CZ * CY, CX), pltpu.HBM)
    magnetogram = pltpu.with_memory_space_constraint(magnetogram, pltpu.HBM)
    whole = pl.BlockSpec(memory_space=pltpu.VMEM)
    dma = pltpu.SemaphoreType.DMA
    a1, v = pl.pallas_call(
        comm_kernel,
        out_shape=(f32(3 * (CZ + 2) * EY, CX), f32(2 * EY, CX)),
        in_specs=[pl.BlockSpec(memory_space=pltpu.HBM), whole],
        out_specs=(whole,) * 2,
        scratch_shapes=[
            vmem(2 * EZ * 8, CX),
            vmem(8 * (CZ + 2) * CY, CX),
            vmem(8 * (CZ + 2) * 8, CX),
            vmem(2 * LEVEL, CX),
            vmem(2 * CY, CX),
            vmem(NZ_DEV - 1, 2 * CY, CX),
        ]
        + [vmem(4 * CZ, CX)] * 4
        + [vmem(16, CX)] * 4
        + [vmem(2 * CY, CX)] * 4
        + [vmem(32, CX)] * 4
        + [
            vmem(4, 16, CX),
            vmem(8, CX),
            vmem(CY, CX),
            vmem(8 * (NY_DEV - 1), CX),
            vmem(CY * (NX_DEV - 1), CX),
            vmem(2 * CY, CX),
            vmem(16, CX),
            vmem(16, CX),
            vmem(16, CX),
            vmem(16, CX),
        ]
        + [dma((2,))]
        + [dma((NZ_DEV - 1,))] * 2
        + [dma((2, 2))] * 2
        + [dma((2,))] * 4
        + [dma((8,))] * 2
        + [dma((NY_DEV - 1,))] * 2
        + [dma((NX_DEV - 1,))] * 2
        + [dma((2,))] * 2,
        compiler_params=pltpu.CompilerParams(
            collective_id=0, has_side_effects=True, vmem_limit_bytes=VMEM_BYTES
        ),
        name="exchange",
    )(side, magnetogram)
    out = pl.pallas_call(
        step_kernel,
        out_shape=f32(3 * CZ * CY, CX),
        in_specs=[whole] * 2,
        out_specs=pl.BlockSpec(memory_space=pltpu.HBM),
        scratch_shapes=[vmem(3 * CZ * CY, CX), dma((CZ // 8, 3))],
        compiler_params=pltpu.CompilerParams(vmem_limit_bytes=VMEM_BYTES),
        name="steps",
    )(a1, v)
    return out.reshape(3, CZ, CY, CX)


def solution(mesh):
    return jax.shard_map(
        local,
        mesh=mesh,
        in_specs=(P(None, "gz", "gy", "gx"), P("gy", "gx")),
        out_specs=P(None, "gz", "gy", "gx"),
        check_vma=False,
    )
```

```python
import functools

import jax
import jax.numpy as jnp
from jax import lax
from jax.experimental import pallas as pl
from jax.experimental.pallas import tpu as pltpu
from jax.sharding import PartitionSpec as P

spacing = 0.0625
friction = 0.004
MESH = pl.DeviceIdType.MESH

VMEM_BYTES = 24 * 2**20
UNROLL_PRE, UNROLL_STRIP, UNROLL_POST, UNROLL_EDGE, UNROLL_PACK = 8, 8, 4, 25, 8
NZ_DEV, NY_DEV, NX_DEV = 8, 8, 4
CZ, CY, CX = 48, 32, 128
EZ = CZ + 3
EY = CY + 8
LEVEL = EZ * CY


def lanes(shape):
    return lax.broadcasted_iota(jnp.int32, shape, len(shape) - 1)


def rows(shape):
    return lax.broadcasted_iota(jnp.int32, shape, len(shape) - 2)


def turn(x, shift, axis):
    return pltpu.roll(x, shift % x.shape[axis], axis)


def fields(a, zp, yp, xp, first):
    ax, ay = a[0], a[1]
    if first:
        bx = ay - zp[1]
        by = zp[0] - ax
    else:
        bx = (yp[2] - a[2]) - (zp[1] - ay)
        by = (zp[0] - ax) - (xp[2] - a[2])
    bz = (xp[1] - ay) - (yp[0] - ax)
    return bx, by, bz


def drive(b, zm, ym, xm):
    bx, by, bz = b
    jx = (bz - ym[2]) - (by - zm[1])
    jy = (bx - zm[0]) - (bz - xm[2])
    jz = (by - xm[1]) - (bx - ym[0])
    return push(b, (jx, jy, jz))


def push(b, j):
    bx, by, bz = b
    jx, jy, jz = j
    square = bx * bx + by * by + bz * bz
    scale = (friction / spacing**2) / (square + spacing**2)
    along = (jx * bx + jy * by + jz * bz) * scale
    across = square * scale
    return (along * bx - across * jx, along * by - across * jy, along * bz - across * jz)


def comm_kernel(
    side_hbm,
    mag_ref,
    a1_out,
    v_out,
    ext_v,
    pre_m,
    pre_e,
    side_v,
    t_v,
    tr,
    ys_lo,
    ys_hi,
    yr_lo,
    yr_hi,
    cs_lo,
    cs_hi,
    cr_lo,
    cr_hi,
    w_hi,
    w_lo,
    wn_hi,
    wn_lo,
    wt_lo,
    wt_hi,
    wy_lo,
    wy_hi,
    wd,
    mc_s,
    mr_s,
    mc_r,
    mr_r,
    q_v,
    qt_lo,
    qt_hi,
    qy_lo,
    qy_hi,
    here_sem,
    wide,
    far,
    load_sem,
    s_t,
    r_t,
    s_z,
    r_z,
    s_y,
    r_y,
    s_c,
    r_c,
    s_w,
    r_w,
    s_mc,
    r_mc,
    s_mr,
    r_mr,
    s_q,
    r_q,
):
    gz, gy, gx = lax.axis_index("gz"), lax.axis_index("gy"), lax.axis_index("gx")

    def at(dz=0, dy=0, dx=0):
        where = {}
        if dz:
            where["gz"] = lax.rem(gz + dz + NZ_DEV, NZ_DEV)
        if dy:
            where["gy"] = lax.rem(gy + dy + NY_DEV, NY_DEV)
        if dx:
            where["gx"] = lax.rem(gx + dx + NX_DEV, NX_DEV)
        return where

    def there(dz=0, dy=0, dx=0):
        ok = None
        for here, d, size in ((gz, dz, NZ_DEV), (gy, dy, NY_DEV), (gx, dx, NX_DEV)):
            if d:
                one = here + d < size if d > 0 else here + d >= 0
                ok = one if ok is None else jnp.logical_and(ok, one)
        return ok

    class Hop:
        def __init__(self, src, dst, ssem, rsem, **by):
            self.copy = pltpu.make_async_remote_copy(
                src_ref=src,
                dst_ref=dst,
                send_sem=ssem,
                recv_sem=rsem,
                device_id=at(**by),
                device_id_type=MESH,
            )
            self.to = there(**by)
            self.back = there(**{k: -v for k, v in by.items()})

        def start(self):
            pl.when(self.to)(self.copy.start)

        def wait_send(self):
            pl.when(self.to)(self.copy.wait_send)

        def wait_recv(self):
            pl.when(self.back)(self.copy.wait_recv)

    loads = [
        pltpu.make_async_copy(
            side_hbm.at[pl.ds(c * CZ * CY, CZ * CY)],
            side_v.at[pl.ds(c * LEVEL + CY, CZ * CY)],
            load_sem.at[c],
        )
        for c in range(2)
    ]
    for load in loads:
        load.start()

    half = NZ_DEV // 2
    place_z = lax.rem(gz, half)
    middle = (gz == half - 1).astype(jnp.int32)
    barrier = pltpu.get_barrier_semaphore()

    def tell(sem, ok, **by):
        @pl.when(ok)
        def _():
            pl.semaphore_signal(sem, inc=1, device_id=at(**by), device_id_type=MESH)

    def wait_for(sem, count):
        @pl.when(count > 0)
        def _():
            pl.semaphore_wait(sem, count)

    def close(d):
        return jnp.logical_or(place_z >= d, jnp.logical_and(gz == half, d == 1))

    higher = (
        [dict(dz=d) for d in range(1, NZ_DEV)]
        + [dict(dy=d) for d in range(1, NY_DEV)]
        + [dict(dx=d) for d in range(1, NX_DEV)]
        + [dict(dy=1, dx=1), dict(dy=1, dx=-1)]
    )
    heard, answers = gz + gy + gx, (half - 1 - place_z) + middle
    answers = answers + there(dy=1).astype(jnp.int32) + there(dx=1).astype(jnp.int32)
    others = jnp.maximum(NY_DEV - 2 - gy, 0) + jnp.maximum(NX_DEV - 2 - gx, 0)
    for by in higher:
        tell(barrier, there(**by), **by)
    for by in higher[-2:]:
        heard = heard + there(**{k: -v for k, v in by.items()}).astype(jnp.int32)
        answers = answers + there(**by).astype(jnp.int32)
    wait_for(barrier, heard)
    for by in higher:
        back = {k: -v for k, v in by.items()}
        if "dz" in by:
            tell(here_sem, there(**back) & close(by["dz"]), **back)
            tell(far, there(**back) & jnp.logical_not(close(by["dz"])), **back)
        else:
            step = max(by.values())
            tell(here_sem if step == 1 else wide, there(**back), **back)

    mag = mag_ref[...]
    mc_s[...] = jnp.broadcast_to(jnp.sum(mag, axis=0, keepdims=True), (8, CX))
    mr_s[...] = jnp.broadcast_to(jnp.sum(mag, axis=1, keepdims=True), (CY, CX))

    def clear(by, *refs):
        @pl.when(jnp.logical_not(there(**by)))
        def _():
            for ref in refs:
                ref[...] = jnp.zeros_like(ref)

    clear(dict(dz=-1), side_v.at[pl.ds(0, CY)], side_v.at[pl.ds(LEVEL, CY)])
    clear(
        dict(dz=1),
        side_v.at[pl.ds((CZ + 1) * CY, 2 * CY)],
        side_v.at[pl.ds(LEVEL + (CZ + 1) * CY, 2 * CY)],
    )
    clear(dict(dy=-1), yr_lo, cr_lo, wy_lo, qy_lo)
    clear(dict(dy=1), yr_hi, cr_hi, wy_hi, qy_hi)
    clear(dict(dx=-1), wn_lo)
    clear(dict(dx=1), wn_hi)
    for i, by in enumerate((dict(dy=1, dx=-1), dict(dy=1, dx=1), dict(dy=-1, dx=-1), dict(dy=-1, dx=1))):
        clear(by, wd.at[i])

    for c in range(2):
        loads[c].wait()

        def add(z, total, c=c):
            return total + side_v[pl.ds(c * LEVEL + (z + 1) * CY, CY), :]

        t_v[pl.ds(c * CY, CY), :] = lax.fori_loop(
            0, CZ, add, jnp.zeros((CY, CX), jnp.float32), unroll=8
        )

    wait_for(here_sem, answers)

    layers = []
    for c in range(2):
        layers.append(
            Hop(
                side_hbm.at[pl.ds(c * CZ * CY + (CZ - 1) * CY, CY)],
                side_v.at[pl.ds(c * LEVEL, CY)],
                s_z.at[0, c],
                r_z.at[0, c],
                dz=1,
            )
        )
        layers.append(
            Hop(
                side_hbm.at[pl.ds(c * CZ * CY, 2 * CY)],
                side_v.at[pl.ds(c * LEVEL + (CZ + 1) * CY, 2 * CY)],
                s_z.at[1, c],
                r_z.at[1, c],
                dz=-1,
            )
        )
    for one in layers:
        one.start()

    ups = [
        Hop(t_v, tr.at[d - 1], s_t.at[d - 1], r_t.at[d - 1], dz=d) for d in range(1, NZ_DEV)
    ]

    def near(d):
        return jnp.logical_or(place_z + d < half, jnp.logical_and(gz == half - 1, d == 1))

    for d, one in enumerate(ups, 1):
        pl.when(one.to & near(d))(one.copy.start)

    sums = [
        Hop(mc_s, mc_r.at[pl.ds(8 * (d - 1), 8)], s_mc.at[d - 1], r_mc.at[d - 1], dy=d)
        for d in range(1, NY_DEV)
    ] + [
        Hop(mr_s, mr_r.at[pl.ds(CY * (d - 1), CY)], s_mr.at[d - 1], r_mr.at[d - 1], dx=d)
        for d in range(1, NX_DEV)
    ]

    for c in range(2):
        for k in range(2):
            here = pl.ds((2 * c + k) * CZ, CZ)
            ys_lo[here, :] = side_v[pl.ds(c * LEVEL + CY + k, CZ, stride=CY), :]
            ys_hi[here, :] = side_v[pl.ds(c * LEVEL + CY + CY - 2 + k, CZ, stride=CY), :]
    faces = [
        Hop(ys_lo, yr_hi, s_y.at[0], r_y.at[0], dy=-1),
        Hop(ys_hi, yr_lo, s_y.at[1], r_y.at[1], dy=1),
    ]
    for one in faces:
        one.start()

    main_lane = lanes((CY, CX))

    def main(c, level):
        return side_v[pl.ds(pl.multiple_of(c * LEVEL + level * CY, 8), CY), :]

    def place(zi, running, packed):
        first = 2 * zi
        out = []
        for c in range(2):
            turned = pltpu.roll(running[c], first + 2, 1)
            hi, lo = packed[2 * c], packed[2 * c + 1]
            out.append(jnp.where((main_lane == first) | (main_lane == first + 1), turned, hi))
            out.append(jnp.where((main_lane == first + 2) | (main_lane == first + 3), turned, lo))
        return tuple(out)

    nothing = jnp.zeros((CY, CX), jnp.float32)

    def pack(zi, carry):
        running, packed = carry
        running = tuple(running[c] + main(c, zi - 1) for c in range(2))
        return running, place(zi, running, packed)

    running, packed = lax.fori_loop(
        2, CZ + 2, pack, ((nothing,) * 2, (nothing,) * 4), unroll=UNROLL_PACK
    )

    wait_for(wide, others)
    for one in sums:
        one.start()

    @pl.when(gz < half)
    def _():
        pl.semaphore_wait(far, half - middle)

    for d, one in enumerate(ups, 1):
        pl.when(one.to & jnp.logical_not(near(d)))(one.copy.start)

    def slot(k, z, high):
        return pl.ds(pl.multiple_of((k * (CZ + 2) + z + 1) * high, 8), high)

    class Strip:
        def __init__(self, source, store, high):
            self.source, self.store, self.high = source, store, high

        def raw(self, c, level):
            first = pl.multiple_of((c * EZ + level) * self.high, 8)
            return spacing * self.source[pl.ds(first, self.high), :]

        def level(self, z, ax, ay, before):
            bx, by = self.raw(0, z + 2), self.raw(1, z + 2)
            bz = (turn(ay, -1, 1) - ay) - (turn(ax, -1, 0) - ax)
            values = (
                bx,
                by,
                bz,
                (bz - turn(bz, 1, 0)) - (by - before[1]),
                (bx - before[0]) - (bz - turn(bz, 1, 1)),
                (by - turn(by, 1, 1)) - (bx - turn(bx, 1, 0)),
                ax,
                ay,
            )
            for k, x in enumerate(values):
                self.store[slot(k, z, self.high), :] = x
            return ax + by, ay - bx, (bx, by)

        def middle(self, unroll):
            ground = (self.raw(0, 1), self.raw(1, 1))
            return lax.fori_loop(
                0,
                CZ - 1,
                lambda z, carry: self.level(z, *carry),
                (ground[1], -ground[0], ground),
                unroll=unroll,
            )

        def ends(self, ax, ay, before):
            level_zero = jnp.zeros((self.high, CX), jnp.float32)
            self.level(-1, level_zero, level_zero, (self.raw(0, 0), self.raw(1, 0)))
            ax, ay, before = self.level(CZ - 1, ax, ay, before)
            self.level(CZ, ax, ay, before)

        def at_the_bounds(self, qx, qy):
            pre, high = self.store, self.high

            @pl.when(gz == 0)
            def _():
                pre[slot(3, 0, high), :] = pre[slot(3, 0, high), :] + qx
                pre[slot(4, 0, high), :] = pre[slot(4, 0, high), :] + qy

            @pl.when(gz == NZ_DEV - 1)
            def _():
                z = CZ - 1
                bx, by = pre[slot(0, z, high), :], pre[slot(1, z, high), :]
                tx = pre[slot(7, z, high), :] + qy
                ty = -(pre[slot(6, z, high), :] + qx)
                pre[slot(0, z, high), :] = tx
                pre[slot(1, z, high), :] = ty
                pre[slot(3, z, high), :] = pre[slot(3, z, high), :] - (ty - by)
                pre[slot(4, z, high), :] = pre[slot(4, z, high), :] + (tx - bx)
                pre[slot(5, z, high), :] = (ty - turn(ty, 1, 1)) - (tx - turn(tx, 1, 0))

        def finish(self, z, planes_of):
            qx, qy, cz, cjx, cjy = planes_of
            bx, by, bz, jx, jy, jz, ax, ay = (
                self.store[slot(k, z, self.high), :] for k in range(8)
            )
            d = push((bx, by, bz + cz), (jx + cjx, jy + cjy, jz))
            return (ax + qx + d[0], ay + qy + d[1], d[2])

    def planes_for(qx, qy):
        cz = (turn(qy, -1, 1) - qy) - (turn(qx, -1, 0) - qx)
        return qx, qy, cz, cz - turn(cz, 1, 0), turn(cz, 1, 1) - cz

    block = Strip(side_v, pre_m, CY)
    strip = Strip(ext_v, pre_e, 8)
    block_end = block.middle(UNROLL_PRE)

    col = mag
    row_of = rows((CY, CX))
    for k in (1, 2, 4, 8, 16):
        col = col + jnp.where(row_of >= k, pltpu.roll(col, k, 0), 0.0)
    lin = mag
    lane_of = lanes((CY, CX))
    for k in (1, 2, 4, 8, 16, 32, 64):
        lin = lin + jnp.where(lane_of >= k, pltpu.roll(lin, k, 1), 0.0)
    q_v[pl.ds(0, CY), :] = col
    q_v[pl.ds(CY, CY), :] = lin
    for d, one in enumerate(sums[: NY_DEV - 1]):

        @pl.when(one.back)
        def _(d=d, one=one):
            one.wait_recv()
            q_v[pl.ds(0, CY), :] = q_v[pl.ds(0, CY), :] + mc_r[pl.ds(8 * d, 1), :]

    for d, one in enumerate(sums[NY_DEV - 1 :]):

        @pl.when(one.back)
        def _(d=d, one=one):
            one.wait_recv()
            q_v[pl.ds(CY, CY), :] = q_v[pl.ds(CY, CY), :] + mr_r[pl.ds(CY * d, CY), :]

    q_v[pl.ds(0, CY), :] = (-0.5 * spacing) * q_v[pl.ds(0, CY), :]
    q_v[pl.ds(CY, CY), :] = (0.5 * spacing) * q_v[pl.ds(CY, CY), :]

    for one in layers:
        one.wait_recv()
    for zi in (CZ + 2, CZ + 3):
        running, packed = pack(zi, (running, packed))
    packed = place(0, tuple(-main(c, 0) for c in range(2)), packed)

    for c in range(2):
        for i, level in enumerate((0, CZ + 1, CZ + 2)):
            first = c * LEVEL + level * CY
            to = (c * 3 + i) * 2
            cs_lo[pl.ds(to, 2), :] = side_v[pl.ds(first, 2), :]
            cs_hi[pl.ds(to, 2), :] = side_v[pl.ds(first + CY - 2, 2), :]
    cs_lo[pl.ds(12, 4), :] = jnp.zeros((4, CX), jnp.float32)
    cs_hi[pl.ds(12, 4), :] = jnp.zeros((4, CX), jnp.float32)
    corners = [
        Hop(cs_lo, cr_hi, s_c.at[0], r_c.at[0], dy=-1),
        Hop(cs_hi, cr_lo, s_c.at[1], r_c.at[1], dy=1),
    ]
    for one in corners:
        one.start()

    block.ends(*block_end)

    for one in ups:

        @pl.when(one.back)
        def _(one=one):
            one.wait_recv()

    for d in range(1, NZ_DEV):

        @pl.when(there(dz=-d))
        def _(d=d):
            q_v[pl.ds(0, CY), :] = q_v[pl.ds(0, CY), :] + spacing * tr[d - 1, pl.ds(CY, CY), :]
            q_v[pl.ds(CY, CY), :] = q_v[pl.ds(CY, CY), :] - spacing * tr[d - 1, pl.ds(0, CY), :]

    q = tuple(q_v[pl.ds(c * CY, CY), :] for c in range(2))
    def spread(x, i):
        return jnp.broadcast_to(x[:, i : i + 1], x.shape)

    main_even = main_lane % 2 == 0
    for c in range(2):
        o, sign = (1, spacing) if c == 0 else (0, -spacing)
        hi = jnp.where(main_even, spread(q[c], CX - 2), spread(q[c], CX - 1))
        lo = jnp.where(main_even, spread(q[c], 0), spread(q[c], 1))
        hi, lo = hi + sign * packed[2 * o], lo + sign * packed[2 * o + 1]
        for k, (ref, x) in enumerate(((w_hi, hi), (w_lo, lo))):
            ref[pl.ds(c * CY, CY), :] = x
            wt_lo[pl.ds((2 * k + c) * 8, 8), :] = x[:8]
            wt_hi[pl.ds((2 * k + c) * 8, 8), :] = x[CY - 8 :]
        qt_lo[pl.ds(c * 8, 8), :] = q[c][:8]
        qt_hi[pl.ds(c * 8, 8), :] = q[c][CY - 8 :]
    columns = [
        Hop(w_hi, wn_lo, s_w.at[0], r_w.at[0], dx=1),
        Hop(w_lo, wn_hi, s_w.at[1], r_w.at[1], dx=-1),
        Hop(wt_lo.at[pl.ds(0, 16)], wd.at[0], s_w.at[4], r_w.at[4], dy=-1, dx=1),
        Hop(wt_lo.at[pl.ds(16, 16)], wd.at[1], s_w.at[5], r_w.at[5], dy=-1, dx=-1),
        Hop(wt_hi.at[pl.ds(0, 16)], wd.at[2], s_w.at[6], r_w.at[6], dy=1, dx=1),
        Hop(wt_hi.at[pl.ds(16, 16)], wd.at[3], s_w.at[7], r_w.at[7], dy=1, dx=-1),
        Hop(wt_lo, wy_hi, s_w.at[2], r_w.at[2], dy=-1),
        Hop(wt_hi, wy_lo, s_w.at[3], r_w.at[3], dy=1),
        Hop(qt_lo, qy_hi, s_q.at[0], r_q.at[0], dy=-1),
        Hop(qt_hi, qy_lo, s_q.at[1], r_q.at[1], dy=1),
    ]
    for one in columns:
        one.start()

    block.at_the_bounds(*q)
    block_planes = planes_for(*q)

    def finish_block(z, _):
        new = block.finish(z, block_planes)
        for c in range(3):
            first = pl.multiple_of((c * (CZ + 2) + z + 1) * EY, 8)
            a1_out[pl.ds(first, CY), :] = new[c]
        return 0

    lax.fori_loop(-1, CZ + 1, finish_block, 0, unroll=UNROLL_POST)

    for one in faces:
        one.wait_recv()
    for c in range(2):
        for k in range(2):
            here = pl.ds((2 * c + k) * CZ, CZ)
            for j, ref in enumerate((ys_hi, yr_hi, yr_lo, ys_lo)):
                ext_v[pl.ds((c * EZ + 1) * 8 + 2 * j + k, CZ, stride=8), :] = ref[here, :]

    for one in corners:
        one.wait_recv()
    for c in range(2):
        for i, level in enumerate((0, CZ + 1, CZ + 2)):
            first = (c * EZ + level) * 8
            of = pl.ds((c * 3 + i) * 2, 2)
            for j, ref in enumerate((cs_hi, cr_hi, cr_lo, cs_lo)):
                ext_v[pl.ds(first + 2 * j, 2), :] = ref[of, :]
    strip.ends(*strip.middle(UNROLL_STRIP))

    row8 = rows((8, CX))

    def plane(middle, from_hi, from_lo):
        tile = jnp.where(row8 < 2, from_hi, jnp.where(row8 >= 6, from_lo, 0.0))
        return jnp.concatenate([middle, tile], axis=0)

    for one in columns:
        one.wait_recv()
    lane, row = lanes((EY, CX)), rows((EY, CX))
    even = lane % 2 == 0
    level_ok = ((lane >= 4) | (gz > 0)) & ((lane < 2 * (CZ + 2)) | (gz < NZ_DEV - 1))
    ea = [[None, None] for _ in range(4)]
    carry_plane = []
    for c in range(2):
        mine, tile, other = pl.ds(c * CY, CY), pl.ds(c * 8, 8), pl.ds(16 + c * 8, 8)
        hi = plane(w_hi[mine, :], wy_hi[tile, :], wy_lo[tile, :])
        lo = plane(w_lo[mine, :], wy_hi[other, :], wy_lo[other, :])
        lon = plane(wn_lo[mine, :], wd[0, tile, :], wd[2, tile, :])
        hin = plane(wn_hi[mine, :], wd[1, tile, :], wd[3, tile, :])
        pairs = (
            (hi, turn(lon, 1, 1)),
            (turn(hi, -1, 1), lon),
            (turn(hin, -2, 1), turn(lo, -1, 1)),
            (turn(hin, -3, 1), turn(lo, -2, 1)),
        )
        for m, pair in enumerate(pairs):
            ea[m][c] = jnp.where(level_ok, jnp.where(even, *pair), 0.0)
        around = (q[c][CY - 8 :], qy_hi[tile, :], qy_lo[tile, :], q[c][:8])
        turned = [turn(x, by, 0) for x, by in zip(around, (2, 2, -2, -2))]
        carry_plane.append(
            jnp.where(
                row8 < 4,
                jnp.where(row8 < 2, turned[0], turned[1]),
                jnp.where(row8 < 6, turned[2], turned[3]),
            )
        )

    row_ok = ((row < CY) | (row >= CY + 2) | (gy < NY_DEV - 1)) & ((row < CY + 2) | (gy > 0))
    eb = []
    for m in range(3):
        up_y = (turn(ea[m][0], -1, 0),)
        up_z = tuple(turn(x, -2, 1) for x in ea[m])
        eb.append(fields(ea[m], up_z, up_y, ea[m + 1], True))
    ea1 = []
    for m in (1, 2):
        down_z = tuple(turn(x, 2, 1) for x in eb[m])
        down_y = tuple(turn(x, 1, 0) for x in eb[m])
        d = drive(eb[m], down_z, down_y, eb[m - 1])
        if m == 1:
            outside = (lane % 2 == 1) & (gx == 0)
        else:
            outside = (lane % 2 == 0) & (gx == NX_DEV - 1)
        ok = row_ok & jnp.logical_not(outside) & level_ok
        a = (ea[m][0] + d[0], ea[m][1] + d[1], d[2])
        ea1.append(tuple(jnp.where(ok, x, 0.0) for x in a))
    near = ea1[0]
    eb1 = fields(
        near,
        tuple(turn(x, -2, 1) for x in near),
        tuple(turn(x, -1, 0) for x in near),
        ea1[1],
        False,
    )
    v_out[pl.ds(0, EY), :] = jnp.where(even, ea1[1][1], eb1[2])
    v_out[pl.ds(EY, EY), :] = jnp.where(even, ea1[1][2], eb1[1])
    edge = tuple(jnp.where(even, ea1[0][c], ea1[1][c]) for c in range(3))

    strip.at_the_bounds(*carry_plane)
    strip_planes = planes_for(*carry_plane)
    rim = (lane == 0) | (lane == CX - 1)
    tile_ok = ((row8 >= 2) | (gy < NY_DEV - 1)) & ((row8 < 2) | (gy > 0))

    def finish_strip(z, _):
        new = strip.finish(z, strip_planes)
        shift = lax.rem(2 * CX - 1 - 2 * (z + 2), CX)
        for c in range(3):
            first = pl.multiple_of((c * (CZ + 2) + z + 1) * EY, 8)
            left, right = turn(new[c], -2, 0), turn(new[c], 2, 0)
            x = jnp.concatenate(
                [
                    jnp.where(row8 == 0, right, a1_out[pl.ds(first, 8), :]),
                    a1_out[pl.ds(first + 8, 16), :],
                    jnp.where(row8 == 7, left, a1_out[pl.ds(first + 24, 8), :]),
                    jnp.where(row8 < 4, left, right),
                ],
                axis=0,
            )
            x = jnp.where(rim, pltpu.roll(edge[c], shift, 1), x)
            a1_out[pl.ds(first, CY), :] = x[:CY]
            a1_out[pl.ds(first + CY, 8), :] = jnp.where(tile_ok, x[CY:], 0.0)
        return 0

    lax.fori_loop(-1, CZ + 1, finish_strip, 0, unroll=UNROLL_EDGE)

    @pl.when(gz == 0)
    def _():
        for c in range(3):
            a1_out[slot(c, -1, EY), :] = jnp.zeros((EY, CX), jnp.float32)

    @pl.when(gz == NZ_DEV - 1)
    def _():
        for c in range(3):
            a1_out[slot(c, CZ, EY), :] = jnp.zeros((EY, CX), jnp.float32)

    for one in ups + sums + layers + faces + corners + columns:
        one.wait_send()


def step_kernel(a1, v_ref, out_hbm, out_v, store_sem):
    lane = lanes((EY, CX))
    first_lane, last_lane = lane == 0, lane == CX - 1

    def new_at(z):
        return tuple(
            a1[pl.ds(pl.multiple_of((c * (CZ + 2) + z + 1) * EY, 8), EY), :] for c in range(3)
        )

    def beside(z):
        shift = lax.rem(2 * CX - 1 - 2 * (z + 2), CX)
        return tuple(pltpu.roll(v_ref[pl.ds(k * EY, EY), :], shift, 1) for k in range(2))

    def second_field(a, a_up, v):
        yp = (turn(a[0], -1, 0), None, turn(a[2], -1, 0))
        xp = (
            None,
            jnp.where(last_lane, v[0], turn(a[1], -1, 1)),
            jnp.where(last_lane, v[1], turn(a[2], -1, 1)),
        )
        return fields(a, a_up, yp, xp, False)

    first_main, main = first_lane[:CY], slice(0, CY)

    def level_two(z, carry):
        a, before = carry
        v = beside(z)
        a_up = new_at(z + 1)
        b = second_field(a, a_up, v)
        ym = (turn(b[0], 1, 0)[main], None, turn(b[2], 1, 0)[main])
        own = tuple(x[main] for x in b)
        xm = (
            None,
            jnp.where(first_main, v[1][main], turn(own[1], 1, 1)),
            jnp.where(first_main, v[0][main], turn(own[2], 1, 1)),
        )
        d = drive(own, before, ym, xm)
        for c in range(3):
            out_v[pl.ds(pl.multiple_of((c * CZ + z) * CY, 8), CY), :] = a[c][main] + d[c]
        return a_up, (own[0], own[1])

    below, a = new_at(-1), new_at(0)
    b = second_field(below, a, beside(-1))
    carry = (a, (b[0][main], b[1][main]))
    part = 8

    def store(k, c):
        there = pl.ds(pl.multiple_of((c * CZ + k * part) * CY, 8), part * CY)
        return pltpu.make_async_copy(out_v.at[there], out_hbm.at[there], store_sem.at[k, c])

    def chunk(k, carry):
        carry = lax.fori_loop(
            0, part, lambda i, x: level_two(k * part + i, x), carry, unroll=4
        )
        for c in range(3):
            store(k, c).start()
        return carry

    lax.fori_loop(0, CZ // part, chunk, carry)
    for k in range(CZ // part):
        for c in range(3):
            store(k, c).wait()


def f32(*shape):
    return jax.ShapeDtypeStruct(shape, jnp.float32)


def vmem(*shape):
    return pltpu.VMEM(shape, jnp.float32)


def local(side_field, magnetogram):
    side = pltpu.with_memory_space_constraint(side_field.reshape(2 * CZ * CY, CX), pltpu.HBM)
    magnetogram = pltpu.with_memory_space_constraint(magnetogram, pltpu.HBM)
    whole = pl.BlockSpec(memory_space=pltpu.VMEM)
    dma = pltpu.SemaphoreType.DMA
    a1, v = pl.pallas_call(
        comm_kernel,
        out_shape=(f32(3 * (CZ + 2) * EY, CX), f32(2 * EY, CX)),
        in_specs=[pl.BlockSpec(memory_space=pltpu.HBM), whole],
        out_specs=(whole,) * 2,
        scratch_shapes=[
            vmem(2 * EZ * 8, CX),
            vmem(8 * (CZ + 2) * CY, CX),
            vmem(8 * (CZ + 2) * 8, CX),
            vmem(2 * LEVEL, CX),
            vmem(2 * CY, CX),
            vmem(NZ_DEV - 1, 2 * CY, CX),
        ]
        + [vmem(4 * CZ, CX)] * 4
        + [vmem(16, CX)] * 4
        + [vmem(2 * CY, CX)] * 4
        + [vmem(32, CX)] * 4
        + [
            vmem(4, 16, CX),
            vmem(8, CX),
            vmem(CY, CX),
            vmem(8 * (NY_DEV - 1), CX),
            vmem(CY * (NX_DEV - 1), CX),
            vmem(2 * CY, CX),
            vmem(16, CX),
            vmem(16, CX),
            vmem(16, CX),
            vmem(16, CX),
        ]
        + [pltpu.SemaphoreType.REGULAR] * 3
        + [dma((2,))]
        + [dma((NZ_DEV - 1,))] * 2
        + [dma((2, 2))] * 2
        + [dma((2,))] * 4
        + [dma((8,))] * 2
        + [dma((NY_DEV - 1,))] * 2
        + [dma((NX_DEV - 1,))] * 2
        + [dma((2,))] * 2,
        compiler_params=pltpu.CompilerParams(
            collective_id=0, has_side_effects=True, vmem_limit_bytes=VMEM_BYTES
        ),
        name="exchange",
    )(side, magnetogram)
    out = pl.pallas_call(
        step_kernel,
        out_shape=f32(3 * CZ * CY, CX),
        in_specs=[whole] * 2,
        out_specs=pl.BlockSpec(memory_space=pltpu.HBM),
        scratch_shapes=[vmem(3 * CZ * CY, CX), dma((CZ // 8, 3))],
        compiler_params=pltpu.CompilerParams(vmem_limit_bytes=VMEM_BYTES),
        name="steps",
    )(a1, v)
    return out.reshape(3, CZ, CY, CX)


def solution(mesh):
    return jax.shard_map(
        local,
        mesh=mesh,
        in_specs=(P(None, "gz", "gy", "gx"), P("gy", "gx")),
        out_specs=P(None, "gz", "gy", "gx"),
        check_vma=False,
    )
```

```python
import functools

import jax
import jax.numpy as jnp
from jax import lax
from jax.experimental import pallas as pl
from jax.experimental.pallas import tpu as pltpu
from jax.sharding import PartitionSpec as P

spacing = 0.0625
friction = 0.004
MESH = pl.DeviceIdType.MESH

VMEM_BYTES = 24 * 2**20
UNROLL_PRE, UNROLL_STRIP, UNROLL_POST, UNROLL_EDGE, UNROLL_PACK = 8, 8, 4, 25, 8
NZ_DEV, NY_DEV, NX_DEV = 8, 8, 4
CZ, CY, CX = 48, 32, 128
EZ = CZ + 3
EY = CY + 8
LEVEL = EZ * CY


def lanes(shape):
    return lax.broadcasted_iota(jnp.int32, shape, len(shape) - 1)


def rows(shape):
    return lax.broadcasted_iota(jnp.int32, shape, len(shape) - 2)


def turn(x, shift, axis):
    return pltpu.roll(x, shift % x.shape[axis], axis)


def fields(a, zp, yp, xp, first):
    ax, ay = a[0], a[1]
    if first:
        bx = ay - zp[1]
        by = zp[0] - ax
    else:
        bx = (yp[2] - a[2]) - (zp[1] - ay)
        by = (zp[0] - ax) - (xp[2] - a[2])
    bz = (xp[1] - ay) - (yp[0] - ax)
    return bx, by, bz


def drive(b, zm, ym, xm):
    bx, by, bz = b
    jx = (bz - ym[2]) - (by - zm[1])
    jy = (bx - zm[0]) - (bz - xm[2])
    jz = (by - xm[1]) - (bx - ym[0])
    return push(b, (jx, jy, jz))


def push(b, j):
    bx, by, bz = b
    jx, jy, jz = j
    square = bx * bx + by * by + bz * bz
    scale = (friction / spacing**2) / (square + spacing**2)
    along = (jx * bx + jy * by + jz * bz) * scale
    across = square * scale
    return (along * bx - across * jx, along * by - across * jy, along * bz - across * jz)


def comm_kernel(
    side_hbm,
    mag_hbm,
    a1_out,
    v_out,
    mag_ref,
    ext_v,
    pre_m,
    pre_e,
    side_v,
    t_v,
    tr,
    ys_lo,
    ys_hi,
    yr_lo,
    yr_hi,
    cs_lo,
    cs_hi,
    cr_lo,
    cr_hi,
    w_hi,
    w_lo,
    wn_hi,
    wn_lo,
    wt_lo,
    wt_hi,
    wy_lo,
    wy_hi,
    wd,
    mc_s,
    mr_s,
    mc_r,
    mr_r,
    q_v,
    qc,
    qn,
    qt_lo,
    qt_hi,
    qy_lo,
    qy_hi,
    here_sem,
    wide,
    far,
    load_sem,
    s_t,
    r_t,
    s_z,
    r_z,
    s_y,
    r_y,
    s_c,
    r_c,
    s_w,
    r_w,
    s_mc,
    r_mc,
    s_mr,
    r_mr,
    s_q,
    r_q,
):
    gz, gy, gx = lax.axis_index("gz"), lax.axis_index("gy"), lax.axis_index("gx")

    def at(dz=0, dy=0, dx=0):
        where = {}
        if dz:
            where["gz"] = lax.rem(gz + dz + NZ_DEV, NZ_DEV)
        if dy:
            where["gy"] = lax.rem(gy + dy + NY_DEV, NY_DEV)
        if dx:
            where["gx"] = lax.rem(gx + dx + NX_DEV, NX_DEV)
        return where

    def there(dz=0, dy=0, dx=0):
        ok = None
        for here, d, size in ((gz, dz, NZ_DEV), (gy, dy, NY_DEV), (gx, dx, NX_DEV)):
            if d:
                one = here + d < size if d > 0 else here + d >= 0
                ok = one if ok is None else jnp.logical_and(ok, one)
        return ok

    class Hop:
        def __init__(self, src, dst, ssem, rsem, **by):
            self.copy = pltpu.make_async_remote_copy(
                src_ref=src,
                dst_ref=dst,
                send_sem=ssem,
                recv_sem=rsem,
                device_id=at(**by),
                device_id_type=MESH,
            )
            self.to = there(**by)
            self.back = there(**{k: -v for k, v in by.items()})

        def start(self):
            pl.when(self.to)(self.copy.start)

        def wait_send(self):
            pl.when(self.to)(self.copy.wait_send)

        def wait_recv(self):
            pl.when(self.back)(self.copy.wait_recv)

    half = NZ_DEV // 2
    place_z = lax.rem(gz, half)
    middle = (gz == half - 1).astype(jnp.int32)
    barrier = pltpu.get_barrier_semaphore()

    def tell(sem, ok, **by):
        @pl.when(ok)
        def _():
            pl.semaphore_signal(sem, inc=1, device_id=at(**by), device_id_type=MESH)

    def wait_for(sem, count):
        @pl.when(count > 0)
        def _():
            pl.semaphore_wait(sem, count)

    def close(d):
        return jnp.logical_or(place_z >= d, jnp.logical_and(gz == half, d == 1))

    higher = (
        [dict(dz=d) for d in range(1, NZ_DEV)]
        + [dict(dy=d) for d in range(1, NY_DEV)]
        + [dict(dx=d) for d in range(1, NX_DEV)]
        + [dict(dy=1, dx=1), dict(dy=1, dx=-1)]
    )
    heard, answers = gz + gy + gx, (half - 1 - place_z) + middle
    answers = answers + there(dy=1).astype(jnp.int32) + there(dx=1).astype(jnp.int32)
    others = jnp.maximum(NY_DEV - 2 - gy, 0) + jnp.maximum(NX_DEV - 2 - gx, 0)
    for by in higher:
        tell(barrier, there(**by), **by)
    for by in higher[-2:]:
        heard = heard + there(**{k: -v for k, v in by.items()}).astype(jnp.int32)
        answers = answers + there(**by).astype(jnp.int32)
    part = CZ // 2 * CY
    loads = [
        pltpu.make_async_copy(
            side_hbm.at[pl.ds(c * CZ * CY + k * part, part)],
            side_v.at[pl.ds(c * LEVEL + CY + k * part, part)],
            load_sem.at[2 * c + k],
        )
        for c in range(2)
        for k in range(2)
    ]
    loads.append(pltpu.make_async_copy(mag_hbm, mag_ref, load_sem.at[4]))
    for load in loads:
        load.start()
    wait_for(barrier, heard)
    for by in higher:
        back = {k: -v for k, v in by.items()}
        if "dz" in by:
            tell(here_sem, there(**back) & close(by["dz"]), **back)
            tell(far, there(**back) & jnp.logical_not(close(by["dz"])), **back)
        else:
            step = max(by.values())
            tell(here_sem if step == 1 else wide, there(**back), **back)

    def clear(by, *refs):
        @pl.when(jnp.logical_not(there(**by)))
        def _():
            for ref in refs:
                ref[...] = jnp.zeros_like(ref)

    clear(dict(dz=-1), side_v.at[pl.ds(0, CY)], side_v.at[pl.ds(LEVEL, CY)])
    clear(
        dict(dz=1),
        side_v.at[pl.ds((CZ + 1) * CY, 2 * CY)],
        side_v.at[pl.ds(LEVEL + (CZ + 1) * CY, 2 * CY)],
    )
    clear(dict(dy=-1), yr_lo, cr_lo, wy_lo, qy_lo)
    clear(dict(dy=1), yr_hi, cr_hi, wy_hi, qy_hi)
    clear(dict(dx=-1), wn_lo)
    clear(dict(dx=1), wn_hi)
    clear(dict(dx=-1), qn.at[0])
    clear(dict(dx=1), qn.at[1])
    for i, by in enumerate((dict(dy=1, dx=-1), dict(dy=1, dx=1), dict(dy=-1, dx=-1), dict(dy=-1, dx=1))):
        clear(by, wd.at[i], qn.at[2 + i])

    for c in range(2):
        total = jnp.zeros((CY, CX), jnp.float32)
        for k in range(2):
            loads[2 * c + k].wait()

            def add(z, total, c=c):
                return total + side_v[pl.ds(c * LEVEL + (z + 1) * CY, CY), :]

            total = lax.fori_loop(k * CZ // 2, (k + 1) * CZ // 2, add, total, unroll=8)
        t_v[pl.ds(c * CY, CY), :] = total
    wait_for(here_sem, answers)

    layers = []
    for c in range(2):
        layers.append(
            Hop(
                side_hbm.at[pl.ds(c * CZ * CY + (CZ - 1) * CY, CY)],
                side_v.at[pl.ds(c * LEVEL, CY)],
                s_z.at[0, c],
                r_z.at[0, c],
                dz=1,
            )
        )
        layers.append(
            Hop(
                side_hbm.at[pl.ds(c * CZ * CY, 2 * CY)],
                side_v.at[pl.ds(c * LEVEL + (CZ + 1) * CY, 2 * CY)],
                s_z.at[1, c],
                r_z.at[1, c],
                dz=-1,
            )
        )
    for one in layers:
        one.start()

    ups = [
        Hop(t_v, tr.at[d - 1], s_t.at[d - 1], r_t.at[d - 1], dz=d) for d in range(1, NZ_DEV)
    ]

    def near(d):
        return jnp.logical_or(place_z + d < half, jnp.logical_and(gz == half - 1, d == 1))

    for d, one in enumerate(ups, 1):
        pl.when(one.to & near(d))(one.copy.start)

    sums = [
        Hop(mc_s, mc_r.at[pl.ds(8 * (d - 1), 8)], s_mc.at[d - 1], r_mc.at[d - 1], dy=d)
        for d in range(1, NY_DEV)
    ] + [
        Hop(mr_s, mr_r.at[pl.ds(CY * (d - 1), CY)], s_mr.at[d - 1], r_mr.at[d - 1], dx=d)
        for d in range(1, NX_DEV)
    ]

    for c in range(2):
        for k in range(2):
            here = pl.ds((2 * c + k) * CZ, CZ)
            ys_lo[here, :] = side_v[pl.ds(c * LEVEL + CY + k, CZ, stride=CY), :]
            ys_hi[here, :] = side_v[pl.ds(c * LEVEL + CY + CY - 2 + k, CZ, stride=CY), :]
    faces = [
        Hop(ys_lo, yr_hi, s_y.at[0], r_y.at[0], dy=-1),
        Hop(ys_hi, yr_lo, s_y.at[1], r_y.at[1], dy=1),
    ]
    for one in faces:
        one.start()

    main_lane = lanes((CY, CX))

    def main(c, level):
        return side_v[pl.ds(pl.multiple_of(c * LEVEL + level * CY, 8), CY), :]

    def place(zi, running, packed):
        first = 2 * zi
        out = []
        for c in range(2):
            turned = pltpu.roll(running[c], first + 2, 1)
            hi, lo = packed[2 * c], packed[2 * c + 1]
            out.append(jnp.where((main_lane == first) | (main_lane == first + 1), turned, hi))
            out.append(jnp.where((main_lane == first + 2) | (main_lane == first + 3), turned, lo))
        return tuple(out)

    nothing = jnp.zeros((CY, CX), jnp.float32)

    def pack(zi, carry):
        running, packed = carry
        running = tuple(running[c] + main(c, zi - 1) for c in range(2))
        return running, place(zi, running, packed)

    running, packed = lax.fori_loop(
        2, CZ + 2, pack, ((nothing,) * 2, (nothing,) * 4), unroll=UNROLL_PACK
    )

    loads[4].wait()
    mag = mag_ref[...]
    mc_s[...] = jnp.broadcast_to(jnp.sum(mag, axis=0, keepdims=True), (8, CX))
    mr_s[...] = jnp.broadcast_to(jnp.sum(mag, axis=1, keepdims=True), (CY, CX))

    wait_for(wide, others)
    for one in sums:
        one.start()

    @pl.when(gz < half)
    def _():
        pl.semaphore_wait(far, half - middle)

    for d, one in enumerate(ups, 1):
        pl.when(one.to & jnp.logical_not(near(d)))(one.copy.start)

    def slot(k, z, high):
        return pl.ds(pl.multiple_of((k * (CZ + 2) + z + 1) * high, 8), high)

    class Strip:
        def __init__(self, source, store, high):
            self.source, self.store, self.high = source, store, high

        def raw(self, c, level):
            first = pl.multiple_of((c * EZ + level) * self.high, 8)
            return spacing * self.source[pl.ds(first, self.high), :]

        def level(self, z, ax, ay, before):
            bx, by = self.raw(0, z + 2), self.raw(1, z + 2)
            bz = (turn(ay, -1, 1) - ay) - (turn(ax, -1, 0) - ax)
            values = (
                bx,
                by,
                bz,
                (bz - turn(bz, 1, 0)) - (by - before[1]),
                (bx - before[0]) - (bz - turn(bz, 1, 1)),
                (by - turn(by, 1, 1)) - (bx - turn(bx, 1, 0)),
                ax,
                ay,
            )
            for k, x in enumerate(values):
                self.store[slot(k, z, self.high), :] = x
            return ax + by, ay - bx, (bx, by)

        def middle(self, unroll):
            ground = (self.raw(0, 1), self.raw(1, 1))
            return lax.fori_loop(
                0,
                CZ - 1,
                lambda z, carry: self.level(z, *carry),
                (ground[1], -ground[0], ground),
                unroll=unroll,
            )

        def ends(self, ax, ay, before):
            level_zero = jnp.zeros((self.high, CX), jnp.float32)
            self.level(-1, level_zero, level_zero, (self.raw(0, 0), self.raw(1, 0)))
            ax, ay, before = self.level(CZ - 1, ax, ay, before)
            self.level(CZ, ax, ay, before)

        def at_the_bounds(self, qx, qy):
            pre, high = self.store, self.high

            @pl.when(gz == 0)
            def _():
                pre[slot(3, 0, high), :] = pre[slot(3, 0, high), :] + qx
                pre[slot(4, 0, high), :] = pre[slot(4, 0, high), :] + qy

            @pl.when(gz == NZ_DEV - 1)
            def _():
                z = CZ - 1
                bx, by = pre[slot(0, z, high), :], pre[slot(1, z, high), :]
                tx = pre[slot(7, z, high), :] + qy
                ty = -(pre[slot(6, z, high), :] + qx)
                pre[slot(0, z, high), :] = tx
                pre[slot(1, z, high), :] = ty
                pre[slot(3, z, high), :] = pre[slot(3, z, high), :] - (ty - by)
                pre[slot(4, z, high), :] = pre[slot(4, z, high), :] + (tx - bx)
                pre[slot(5, z, high), :] = (ty - turn(ty, 1, 1)) - (tx - turn(tx, 1, 0))

        def finish(self, z, planes_of):
            qx, qy, cz, cjx, cjy = planes_of
            bx, by, bz, jx, jy, jz, ax, ay = (
                self.store[slot(k, z, self.high), :] for k in range(8)
            )
            d = push((bx, by, bz + cz), (jx + cjx, jy + cjy, jz))
            return (ax + qx + d[0], ay + qy + d[1], d[2])

    def planes_for(qx, qy):
        cz = (turn(qy, -1, 1) - qy) - (turn(qx, -1, 0) - qx)
        return qx, qy, cz, cz - turn(cz, 1, 0), turn(cz, 1, 1) - cz

    block = Strip(side_v, pre_m, CY)
    strip = Strip(ext_v, pre_e, 8)
    block_end = block.middle(UNROLL_PRE)

    col = mag
    row_of = rows((CY, CX))
    for k in (1, 2, 4, 8, 16):
        col = col + jnp.where(row_of >= k, pltpu.roll(col, k, 0), 0.0)
    lin = mag
    lane_of = lanes((CY, CX))
    for k in (1, 2, 4, 8, 16, 32, 64):
        lin = lin + jnp.where(lane_of >= k, pltpu.roll(lin, k, 1), 0.0)
    q_v[pl.ds(0, CY), :] = col
    q_v[pl.ds(CY, CY), :] = lin
    for d, one in enumerate(sums[: NY_DEV - 1]):

        @pl.when(one.back)
        def _(d=d, one=one):
            one.wait_recv()
            q_v[pl.ds(0, CY), :] = q_v[pl.ds(0, CY), :] + mc_r[pl.ds(8 * d, 1), :]

    for d, one in enumerate(sums[NY_DEV - 1 :]):

        @pl.when(one.back)
        def _(d=d, one=one):
            one.wait_recv()
            q_v[pl.ds(CY, CY), :] = q_v[pl.ds(CY, CY), :] + mr_r[pl.ds(CY * d, CY), :]

    q_v[pl.ds(0, CY), :] = (-0.5 * spacing) * q_v[pl.ds(0, CY), :]
    q_v[pl.ds(CY, CY), :] = (0.5 * spacing) * q_v[pl.ds(CY, CY), :]

    for one in layers:
        one.wait_recv()
    for zi in (CZ + 2, CZ + 3):
        running, packed = pack(zi, (running, packed))
    packed = place(0, tuple(-main(c, 0) for c in range(2)), packed)
    for c in range(2):
        o, sign = (1, spacing) if c == 0 else (0, -spacing)
        for k, (ref, x) in enumerate(((w_hi, packed[2 * o]), (w_lo, packed[2 * o + 1]))):
            x = sign * x
            ref[pl.ds(c * CY, CY), :] = x
            wt_lo[pl.ds((2 * k + c) * 8, 8), :] = x[:8]
            wt_hi[pl.ds((2 * k + c) * 8, 8), :] = x[CY - 8 :]
    columns = [
        Hop(w_hi, wn_lo, s_w.at[0], r_w.at[0], dx=1),
        Hop(w_lo, wn_hi, s_w.at[1], r_w.at[1], dx=-1),
        Hop(wt_lo.at[pl.ds(0, 16)], wd.at[0], s_w.at[4], r_w.at[4], dy=-1, dx=1),
        Hop(wt_lo.at[pl.ds(16, 16)], wd.at[1], s_w.at[5], r_w.at[5], dy=-1, dx=-1),
        Hop(wt_hi.at[pl.ds(0, 16)], wd.at[2], s_w.at[6], r_w.at[6], dy=1, dx=1),
        Hop(wt_hi.at[pl.ds(16, 16)], wd.at[3], s_w.at[7], r_w.at[7], dy=1, dx=-1),
        Hop(wt_lo, wy_hi, s_w.at[2], r_w.at[2], dy=-1),
        Hop(wt_hi, wy_lo, s_w.at[3], r_w.at[3], dy=1),
    ]
    for one in columns:
        one.start()

    for c in range(2):
        for i, level in enumerate((0, CZ + 1, CZ + 2)):
            first = c * LEVEL + level * CY
            to = (c * 3 + i) * 2
            cs_lo[pl.ds(to, 2), :] = side_v[pl.ds(first, 2), :]
            cs_hi[pl.ds(to, 2), :] = side_v[pl.ds(first + CY - 2, 2), :]
    cs_lo[pl.ds(12, 4), :] = jnp.zeros((4, CX), jnp.float32)
    cs_hi[pl.ds(12, 4), :] = jnp.zeros((4, CX), jnp.float32)
    corners = [
        Hop(cs_lo, cr_hi, s_c.at[0], r_c.at[0], dy=-1),
        Hop(cs_hi, cr_lo, s_c.at[1], r_c.at[1], dy=1),
    ]
    for one in corners:
        one.start()

    block.ends(*block_end)

    for one in ups:

        @pl.when(one.back)
        def _(one=one):
            one.wait_recv()

    for d in range(1, NZ_DEV):

        @pl.when(there(dz=-d))
        def _(d=d):
            q_v[pl.ds(0, CY), :] = q_v[pl.ds(0, CY), :] + spacing * tr[d - 1, pl.ds(CY, CY), :]
            q_v[pl.ds(CY, CY), :] = q_v[pl.ds(CY, CY), :] - spacing * tr[d - 1, pl.ds(0, CY), :]

    q = tuple(q_v[pl.ds(c * CY, CY), :] for c in range(2))
    lane8 = lanes((8, CX))
    few = jnp.zeros((8, CX), jnp.float32)
    for c in range(2):
        for t in range(CY // 8):
            first = 4 * (CY // 8 * c + t)
            here = (lane8 >= first) & (lane8 < first + 4)
            few = jnp.where(here, turn(q[c][8 * t : 8 * t + 8], first + 2, 1), few)
        qt_lo[pl.ds(c * 8, 8), :] = q[c][:8]
        qt_hi[pl.ds(c * 8, 8), :] = q[c][CY - 8 :]
    qc[...] = few
    planes = [
        Hop(qc, qn.at[0], s_q.at[0], r_q.at[0], dx=1),
        Hop(qc, qn.at[1], s_q.at[1], r_q.at[1], dx=-1),
        Hop(qc, qn.at[2], s_q.at[2], r_q.at[2], dy=-1, dx=1),
        Hop(qc, qn.at[3], s_q.at[3], r_q.at[3], dy=-1, dx=-1),
        Hop(qc, qn.at[4], s_q.at[4], r_q.at[4], dy=1, dx=1),
        Hop(qc, qn.at[5], s_q.at[5], r_q.at[5], dy=1, dx=-1),
        Hop(qt_lo, qy_hi, s_q.at[6], r_q.at[6], dy=-1),
        Hop(qt_hi, qy_lo, s_q.at[7], r_q.at[7], dy=1),
    ]
    for one in planes:
        one.start()

    block.at_the_bounds(*q)
    block_planes = planes_for(*q)

    def finish_block(z, _):
        new = block.finish(z, block_planes)
        for c in range(3):
            first = pl.multiple_of((c * (CZ + 2) + z + 1) * EY, 8)
            a1_out[pl.ds(first, CY), :] = new[c]
        return 0

    lax.fori_loop(-1, CZ + 1, finish_block, 0, unroll=UNROLL_POST)

    for one in faces:
        one.wait_recv()
    for c in range(2):
        for k in range(2):
            here = pl.ds((2 * c + k) * CZ, CZ)
            for j, ref in enumerate((ys_hi, yr_hi, yr_lo, ys_lo)):
                ext_v[pl.ds((c * EZ + 1) * 8 + 2 * j + k, CZ, stride=8), :] = ref[here, :]

    for one in corners:
        one.wait_recv()
    for c in range(2):
        for i, level in enumerate((0, CZ + 1, CZ + 2)):
            first = (c * EZ + level) * 8
            of = pl.ds((c * 3 + i) * 2, 2)
            for j, ref in enumerate((cs_hi, cr_hi, cr_lo, cs_lo)):
                ext_v[pl.ds(first + 2 * j, 2), :] = ref[of, :]
    strip.ends(*strip.middle(UNROLL_STRIP))

    row8 = rows((8, CX))

    def plane(middle, from_hi, from_lo):
        tile = jnp.where(row8 < 2, from_hi, jnp.where(row8 >= 6, from_lo, 0.0))
        return jnp.concatenate([middle, tile], axis=0)

    for one in columns:
        one.wait_recv()
    lane, row = lanes((EY, CX)), rows((EY, CX))
    even = lane % 2 == 0
    level_ok = ((lane >= 4) | (gz > 0)) & ((lane < 2 * (CZ + 2)) | (gz < NZ_DEV - 1))
    grown = []
    for c in range(2):
        mine, tile, other = pl.ds(c * CY, CY), pl.ds(c * 8, 8), pl.ds(16 + c * 8, 8)
        hi = plane(w_hi[mine, :], wy_hi[tile, :], wy_lo[tile, :])
        lo = plane(w_lo[mine, :], wy_hi[other, :], wy_lo[other, :])
        lon = plane(wn_lo[mine, :], wd[0, tile, :], wd[2, tile, :])
        hin = plane(wn_hi[mine, :], wd[1, tile, :], wd[3, tile, :])
        pairs = (
            (hi, turn(lon, 1, 1)),
            (turn(hi, -1, 1), lon),
            (turn(hin, -2, 1), turn(lo, -1, 1)),
            (turn(hin, -3, 1), turn(lo, -2, 1)),
        )
        grown.append([jnp.where(even, *pair) for pair in pairs])

    for one in planes:
        one.wait_recv()

    def spread(x, i):
        return jnp.broadcast_to(x[:, i : i + 1], x.shape)

    def beyond(side, from_hi, from_lo, c, i):
        first = 4 * (CY // 8) * c + i
        x, x_hi, x_lo = qn[side], qn[from_hi], qn[from_lo]
        middle = [spread(x, first + 4 * t) for t in range(CY // 8)]
        middle = jnp.concatenate(middle, axis=0)
        return plane(middle, spread(x_hi, first), spread(x_lo, first + 4 * (CY // 8 - 1)))

    ea = [[None, None] for _ in range(4)]
    carry_plane = []
    for c in range(2):
        tile = pl.ds(c * 8, 8)
        own = plane(q[c], qy_hi[tile, :], qy_lo[tile, :])
        sides = (
            (spread(own, CX - 2), beyond(0, 2, 4, c, 0)),
            (spread(own, CX - 1), beyond(0, 2, 4, c, 1)),
            (beyond(1, 3, 5, c, 2), spread(own, 0)),
            (beyond(1, 3, 5, c, 3), spread(own, 1)),
        )
        for m, pair in enumerate(sides):
            value = jnp.where(even, *pair) + grown[c][m]
            ea[m][c] = jnp.where(level_ok, value, 0.0)
        around = (q[c][CY - 8 :], qy_hi[tile, :], qy_lo[tile, :], q[c][:8])
        turned = [turn(x, by, 0) for x, by in zip(around, (2, 2, -2, -2))]
        carry_plane.append(
            jnp.where(
                row8 < 4,
                jnp.where(row8 < 2, turned[0], turned[1]),
                jnp.where(row8 < 6, turned[2], turned[3]),
            )
        )

    row_ok = ((row < CY) | (row >= CY + 2) | (gy < NY_DEV - 1)) & ((row < CY + 2) | (gy > 0))
    eb = []
    for m in range(3):
        up_y = (turn(ea[m][0], -1, 0),)
        up_z = tuple(turn(x, -2, 1) for x in ea[m])
        eb.append(fields(ea[m], up_z, up_y, ea[m + 1], True))
    ea1 = []
    for m in (1, 2):
        down_z = tuple(turn(x, 2, 1) for x in eb[m])
        down_y = tuple(turn(x, 1, 0) for x in eb[m])
        d = drive(eb[m], down_z, down_y, eb[m - 1])
        if m == 1:
            outside = (lane % 2 == 1) & (gx == 0)
        else:
            outside = (lane % 2 == 0) & (gx == NX_DEV - 1)
        ok = row_ok & jnp.logical_not(outside) & level_ok
        a = (ea[m][0] + d[0], ea[m][1] + d[1], d[2])
        ea1.append(tuple(jnp.where(ok, x, 0.0) for x in a))
    near = ea1[0]
    eb1 = fields(
        near,
        tuple(turn(x, -2, 1) for x in near),
        tuple(turn(x, -1, 0) for x in near),
        ea1[1],
        False,
    )
    v_out[pl.ds(0, EY), :] = jnp.where(even, ea1[1][1], eb1[2])
    v_out[pl.ds(EY, EY), :] = jnp.where(even, ea1[1][2], eb1[1])
    edge = tuple(jnp.where(even, ea1[0][c], ea1[1][c]) for c in range(3))

    strip.at_the_bounds(*carry_plane)
    strip_planes = planes_for(*carry_plane)
    rim = (lane == 0) | (lane == CX - 1)
    tile_ok = ((row8 >= 2) | (gy < NY_DEV - 1)) & ((row8 < 2) | (gy > 0))

    def finish_strip(z, _):
        new = strip.finish(z, strip_planes)
        shift = lax.rem(2 * CX - 1 - 2 * (z + 2), CX)
        for c in range(3):
            first = pl.multiple_of((c * (CZ + 2) + z + 1) * EY, 8)
            left, right = turn(new[c], -2, 0), turn(new[c], 2, 0)
            x = jnp.concatenate(
                [
                    jnp.where(row8 == 0, right, a1_out[pl.ds(first, 8), :]),
                    a1_out[pl.ds(first + 8, 16), :],
                    jnp.where(row8 == 7, left, a1_out[pl.ds(first + 24, 8), :]),
                    jnp.where(row8 < 4, left, right),
                ],
                axis=0,
            )
            x = jnp.where(rim, pltpu.roll(edge[c], shift, 1), x)
            a1_out[pl.ds(first, CY), :] = x[:CY]
            a1_out[pl.ds(first + CY, 8), :] = jnp.where(tile_ok, x[CY:], 0.0)
        return 0

    lax.fori_loop(-1, CZ + 1, finish_strip, 0, unroll=UNROLL_EDGE)

    @pl.when(gz == 0)
    def _():
        for c in range(3):
            a1_out[slot(c, -1, EY), :] = jnp.zeros((EY, CX), jnp.float32)

    @pl.when(gz == NZ_DEV - 1)
    def _():
        for c in range(3):
            a1_out[slot(c, CZ, EY), :] = jnp.zeros((EY, CX), jnp.float32)

    for one in ups + sums + layers + faces + corners + columns + planes:
        one.wait_send()


def step_kernel(a1, v_ref, out_hbm, out_v, store_sem):
    lane = lanes((EY, CX))
    first_lane, last_lane = lane == 0, lane == CX - 1

    def new_at(z):
        return tuple(
            a1[pl.ds(pl.multiple_of((c * (CZ + 2) + z + 1) * EY, 8), EY), :] for c in range(3)
        )

    def beside(z):
        shift = lax.rem(2 * CX - 1 - 2 * (z + 2), CX)
        return tuple(pltpu.roll(v_ref[pl.ds(k * EY, EY), :], shift, 1) for k in range(2))

    def second_field(a, a_up, v):
        yp = (turn(a[0], -1, 0), None, turn(a[2], -1, 0))
        xp = (
            None,
            jnp.where(last_lane, v[0], turn(a[1], -1, 1)),
            jnp.where(last_lane, v[1], turn(a[2], -1, 1)),
        )
        return fields(a, a_up, yp, xp, False)

    first_main, main = first_lane[:CY], slice(0, CY)

    def level_two(z, carry):
        a, before = carry
        v = beside(z)
        a_up = new_at(z + 1)
        b = second_field(a, a_up, v)
        ym = (turn(b[0], 1, 0)[main], None, turn(b[2], 1, 0)[main])
        own = tuple(x[main] for x in b)
        xm = (
            None,
            jnp.where(first_main, v[1][main], turn(own[1], 1, 1)),
            jnp.where(first_main, v[0][main], turn(own[2], 1, 1)),
        )
        d = drive(own, before, ym, xm)
        for c in range(3):
            out_v[pl.ds(pl.multiple_of((c * CZ + z) * CY, 8), CY), :] = a[c][main] + d[c]
        return a_up, (own[0], own[1])

    below, a = new_at(-1), new_at(0)
    b = second_field(below, a, beside(-1))
    carry = (a, (b[0][main], b[1][main]))
    part = 8

    def store(k, c):
        there = pl.ds(pl.multiple_of((c * CZ + k * part) * CY, 8), part * CY)
        return pltpu.make_async_copy(out_v.at[there], out_hbm.at[there], store_sem.at[k, c])

    def chunk(k, carry):
        carry = lax.fori_loop(
            0, part, lambda i, x: level_two(k * part + i, x), carry, unroll=4
        )
        for c in range(3):
            store(k, c).start()
        return carry

    lax.fori_loop(0, CZ // part, chunk, carry)
    for k in range(CZ // part):
        for c in range(3):
            store(k, c).wait()


def f32(*shape):
    return jax.ShapeDtypeStruct(shape, jnp.float32)


def vmem(*shape):
    return pltpu.VMEM(shape, jnp.float32)


def local(side_field, magnetogram):
    side = pltpu.with_memory_space_constraint(side_field.reshape(2 * CZ * CY, CX), pltpu.HBM)
    magnetogram = pltpu.with_memory_space_constraint(magnetogram, pltpu.HBM)
    whole = pl.BlockSpec(memory_space=pltpu.VMEM)
    dma = pltpu.SemaphoreType.DMA
    a1, v = pl.pallas_call(
        comm_kernel,
        out_shape=(f32(3 * (CZ + 2) * EY, CX), f32(2 * EY, CX)),
        in_specs=[pl.BlockSpec(memory_space=pltpu.HBM)] * 2,
        out_specs=(whole,) * 2,
        scratch_shapes=[
            vmem(CY, CX),
            vmem(2 * EZ * 8, CX),
            vmem(8 * (CZ + 2) * CY, CX),
            vmem(8 * (CZ + 2) * 8, CX),
            vmem(2 * LEVEL, CX),
            vmem(2 * CY, CX),
            vmem(NZ_DEV - 1, 2 * CY, CX),
        ]
        + [vmem(4 * CZ, CX)] * 4
        + [vmem(16, CX)] * 4
        + [vmem(2 * CY, CX)] * 4
        + [vmem(32, CX)] * 4
        + [
            vmem(4, 16, CX),
            vmem(8, CX),
            vmem(CY, CX),
            vmem(8 * (NY_DEV - 1), CX),
            vmem(CY * (NX_DEV - 1), CX),
            vmem(2 * CY, CX),
            vmem(8, CX),
            vmem(6, 8, CX),
            vmem(16, CX),
            vmem(16, CX),
            vmem(16, CX),
            vmem(16, CX),
        ]
        + [pltpu.SemaphoreType.REGULAR] * 3
        + [dma((5,))]
        + [dma((NZ_DEV - 1,))] * 2
        + [dma((2, 2))] * 2
        + [dma((2,))] * 4
        + [dma((8,))] * 2
        + [dma((NY_DEV - 1,))] * 2
        + [dma((NX_DEV - 1,))] * 2
        + [dma((8,))] * 2,
        compiler_params=pltpu.CompilerParams(
            collective_id=0, has_side_effects=True, vmem_limit_bytes=VMEM_BYTES
        ),
        name="exchange",
    )(side, magnetogram)
    out = pl.pallas_call(
        step_kernel,
        out_shape=f32(3 * CZ * CY, CX),
        in_specs=[whole] * 2,
        out_specs=pl.BlockSpec(memory_space=pltpu.HBM),
        scratch_shapes=[vmem(3 * CZ * CY, CX), dma((CZ // 8, 3))],
        compiler_params=pltpu.CompilerParams(vmem_limit_bytes=VMEM_BYTES),
        name="steps",
    )(a1, v)
    return out.reshape(3, CZ, CY, CX)


def solution(mesh):
    return jax.shard_map(
        local,
        mesh=mesh,
        in_specs=(P(None, "gz", "gy", "gx"), P("gy", "gx")),
        out_specs=P(None, "gz", "gy", "gx"),
        check_vma=False,
    )
```

```python
import functools

import jax
import jax.numpy as jnp
from jax import lax
from jax.experimental import pallas as pl
from jax.experimental.pallas import tpu as pltpu
from jax.sharding import PartitionSpec as P

spacing = 0.0625
friction = 0.004
MESH = pl.DeviceIdType.MESH

VMEM_BYTES = 24 * 2**20
UNROLL_PRE, UNROLL_STRIP, UNROLL_POST, UNROLL_EDGE, UNROLL_PACK = 8, 8, 4, 25, 8
NZ_DEV, NY_DEV, NX_DEV = 8, 8, 4
CZ, CY, CX = 48, 32, 128
EZ = CZ + 3
EY = CY + 8
LEVEL = EZ * CY


def lanes(shape):
    return lax.broadcasted_iota(jnp.int32, shape, len(shape) - 1)


def rows(shape):
    return lax.broadcasted_iota(jnp.int32, shape, len(shape) - 2)


def turn(x, shift, axis):
    return pltpu.roll(x, shift % x.shape[axis], axis)


def fields(a, zp, yp, xp, first):
    ax, ay = a[0], a[1]
    if first:
        bx = ay - zp[1]
        by = zp[0] - ax
    else:
        bx = (yp[2] - a[2]) - (zp[1] - ay)
        by = (zp[0] - ax) - (xp[2] - a[2])
    bz = (xp[1] - ay) - (yp[0] - ax)
    return bx, by, bz


def drive(b, zm, ym, xm):
    bx, by, bz = b
    jx = (bz - ym[2]) - (by - zm[1])
    jy = (bx - zm[0]) - (bz - xm[2])
    jz = (by - xm[1]) - (bx - ym[0])
    return push(b, (jx, jy, jz))


def push(b, j):
    bx, by, bz = b
    jx, jy, jz = j
    square = bx * bx + by * by + bz * bz
    scale = (friction / spacing**2) / (square + spacing**2)
    along = (jx * bx + jy * by + jz * bz) * scale
    across = square * scale
    return (along * bx - across * jx, along * by - across * jy, along * bz - across * jz)


def comm_kernel(
    side_hbm,
    mag_hbm,
    a1_out,
    v_out,
    mag_ref,
    ext_v,
    pre_m,
    pre_e,
    side_v,
    t_v,
    tr,
    half_s,
    half_r,
    ys_lo,
    ys_hi,
    yr_lo,
    yr_hi,
    cs_lo,
    cs_hi,
    cr_lo,
    cr_hi,
    w_hi,
    w_lo,
    wn_hi,
    wn_lo,
    wt_lo,
    wt_hi,
    wy_lo,
    wy_hi,
    wd,
    mc_s,
    mr_s,
    mc_r,
    mr_r,
    q_v,
    qc,
    qn,
    qt_lo,
    qt_hi,
    qy_lo,
    qy_hi,
    here_sem,
    wide,
    far,
    load_sem,
    s_t,
    r_t,
    s_z,
    r_z,
    s_y,
    r_y,
    s_c,
    r_c,
    s_w,
    r_w,
    s_mc,
    r_mc,
    s_mr,
    r_mr,
    s_q,
    r_q,
):
    gz, gy, gx = lax.axis_index("gz"), lax.axis_index("gy"), lax.axis_index("gx")

    def at(dz=0, dy=0, dx=0):
        where = {}
        if dz:
            where["gz"] = lax.rem(gz + dz + NZ_DEV, NZ_DEV)
        if dy:
            where["gy"] = lax.rem(gy + dy + NY_DEV, NY_DEV)
        if dx:
            where["gx"] = lax.rem(gx + dx + NX_DEV, NX_DEV)
        return where

    def there(dz=0, dy=0, dx=0):
        ok = None
        for here, d, size in ((gz, dz, NZ_DEV), (gy, dy, NY_DEV), (gx, dx, NX_DEV)):
            if d:
                one = here + d < size if d > 0 else here + d >= 0
                ok = one if ok is None else jnp.logical_and(ok, one)
        return ok

    class Hop:
        def __init__(self, src, dst, ssem, rsem, **by):
            self.copy = pltpu.make_async_remote_copy(
                src_ref=src,
                dst_ref=dst,
                send_sem=ssem,
                recv_sem=rsem,
                device_id=at(**by),
                device_id_type=MESH,
            )
            self.to = there(**by)
            self.back = there(**{k: -v for k, v in by.items()})

        def start(self):
            pl.when(self.to)(self.copy.start)

        def wait_send(self):
            pl.when(self.to)(self.copy.wait_send)

        def wait_recv(self):
            pl.when(self.back)(self.copy.wait_recv)

    half = NZ_DEV // 2
    place_z = lax.rem(gz, half)
    middle = (gz == half - 1).astype(jnp.int32)
    barrier = pltpu.get_barrier_semaphore()

    def tell(sem, ok, **by):
        @pl.when(ok)
        def _():
            pl.semaphore_signal(sem, inc=1, device_id=at(**by), device_id_type=MESH)

    def wait_for(sem, count):
        @pl.when(count > 0)
        def _():
            pl.semaphore_wait(sem, count)

    def close(d):
        return jnp.logical_or(place_z >= d, jnp.logical_and(gz == half, d == 1))

    higher = (
        [dict(dy=d) for d in range(1, NY_DEV)]
        + [dict(dx=d) for d in range(1, NX_DEV)]
        + [dict(dy=1, dx=1), dict(dy=1, dx=-1)]
    )
    heard = place_z + (gz >= half).astype(jnp.int32) + gy + gx
    answers = (half - 1 - place_z) + middle
    for d in range(1, half + 1):
        tell(barrier, there(dz=d) & ((place_z + d < half) | (gz == half - 1)), dz=d)
    answers = answers + there(dy=1).astype(jnp.int32) + there(dx=1).astype(jnp.int32)
    others = jnp.maximum(NY_DEV - 2 - gy, 0) + jnp.maximum(NX_DEV - 2 - gx, 0)
    for by in higher:
        tell(barrier, there(**by), **by)
    for by in higher[-2:]:
        heard = heard + there(**{k: -v for k, v in by.items()}).astype(jnp.int32)
        answers = answers + there(**by).astype(jnp.int32)
    part = CZ // 2 * CY
    loads = [
        pltpu.make_async_copy(
            side_hbm.at[pl.ds(c * CZ * CY + k * part, part)],
            side_v.at[pl.ds(c * LEVEL + CY + k * part, part)],
            load_sem.at[2 * c + k],
        )
        for c in range(2)
        for k in range(2)
    ]
    loads.append(pltpu.make_async_copy(mag_hbm, mag_ref, load_sem.at[4]))
    for load in loads:
        load.start()
    wait_for(barrier, heard)
    for d in range(1, half):
        tell(here_sem, there(dz=-d) & close(d), dz=-d)
    for d in range(2, half + 1):
        tell(far, gz == half - 1 + d, dz=-d)
    for by in higher:
        back = {k: -v for k, v in by.items()}
        step = max(by.values())
        tell(here_sem if step == 1 else wide, there(**back), **back)

    def clear(by, *refs):
        @pl.when(jnp.logical_not(there(**by)))
        def _():
            for ref in refs:
                ref[...] = jnp.zeros_like(ref)

    clear(dict(dz=-1), side_v.at[pl.ds(0, CY)], side_v.at[pl.ds(LEVEL, CY)])
    clear(
        dict(dz=1),
        side_v.at[pl.ds((CZ + 1) * CY, 2 * CY)],
        side_v.at[pl.ds(LEVEL + (CZ + 1) * CY, 2 * CY)],
    )
    clear(dict(dy=-1), yr_lo, cr_lo, wy_lo, qy_lo)
    clear(dict(dy=1), yr_hi, cr_hi, wy_hi, qy_hi)
    clear(dict(dx=-1), wn_lo)
    clear(dict(dx=1), wn_hi)
    clear(dict(dx=-1), qn.at[0])
    clear(dict(dx=1), qn.at[1])
    for i, by in enumerate((dict(dy=1, dx=-1), dict(dy=1, dx=1), dict(dy=-1, dx=-1), dict(dy=-1, dx=1))):
        clear(by, wd.at[i], qn.at[2 + i])

    for c in range(2):
        total = jnp.zeros((CY, CX), jnp.float32)
        for k in range(2):
            loads[2 * c + k].wait()

            def add(z, total, c=c):
                return total + side_v[pl.ds(c * LEVEL + (z + 1) * CY, CY), :]

            total = lax.fori_loop(k * CZ // 2, (k + 1) * CZ // 2, add, total, unroll=8)
        t_v[pl.ds(c * CY, CY), :] = total
    wait_for(here_sem, answers)

    layers = []
    for c in range(2):
        layers.append(
            Hop(
                side_hbm.at[pl.ds(c * CZ * CY + (CZ - 1) * CY, CY)],
                side_v.at[pl.ds(c * LEVEL, CY)],
                s_z.at[0, c],
                r_z.at[0, c],
                dz=1,
            )
        )
        layers.append(
            Hop(
                side_hbm.at[pl.ds(c * CZ * CY, 2 * CY)],
                side_v.at[pl.ds(c * LEVEL + (CZ + 1) * CY, 2 * CY)],
                s_z.at[1, c],
                r_z.at[1, c],
                dz=-1,
            )
        )
    for one in layers:
        one.start()

    ups = [Hop(t_v, tr.at[d - 1], s_t.at[d - 1], r_t.at[d - 1], dz=d) for d in range(1, half)]
    for d, one in enumerate(ups, 1):
        one.to = one.to & (place_z + d < half)
        one.back = place_z >= d
    across = [
        Hop(half_s, half_r, s_t.at[half - 2 + d], r_t.at[half - 2 + d], dz=d)
        for d in range(1, half + 1)
    ]
    for d, one in enumerate(across, 1):
        one.to = gz == half - 1
        one.back = gz == half - 1 + d
    for one in ups:
        one.start()

    sums = [
        Hop(mc_s, mc_r.at[pl.ds(8 * (d - 1), 8)], s_mc.at[d - 1], r_mc.at[d - 1], dy=d)
        for d in range(1, NY_DEV)
    ] + [
        Hop(mr_s, mr_r.at[pl.ds(CY * (d - 1), CY)], s_mr.at[d - 1], r_mr.at[d - 1], dx=d)
        for d in range(1, NX_DEV)
    ]

    for c in range(2):
        for k in range(2):
            here = pl.ds((2 * c + k) * CZ, CZ)
            ys_lo[here, :] = side_v[pl.ds(c * LEVEL + CY + k, CZ, stride=CY), :]
            ys_hi[here, :] = side_v[pl.ds(c * LEVEL + CY + CY - 2 + k, CZ, stride=CY), :]
    faces = [
        Hop(ys_lo, yr_hi, s_y.at[0], r_y.at[0], dy=-1),
        Hop(ys_hi, yr_lo, s_y.at[1], r_y.at[1], dy=1),
    ]
    for one in faces:
        one.start()

    main_lane = lanes((CY, CX))

    def main(c, level):
        return side_v[pl.ds(pl.multiple_of(c * LEVEL + level * CY, 8), CY), :]

    def place(zi, running, packed):
        first = 2 * zi
        out = []
        for c in range(2):
            turned = pltpu.roll(running[c], first + 2, 1)
            hi, lo = packed[2 * c], packed[2 * c + 1]
            out.append(jnp.where((main_lane == first) | (main_lane == first + 1), turned, hi))
            out.append(jnp.where((main_lane == first + 2) | (main_lane == first + 3), turned, lo))
        return tuple(out)

    nothing = jnp.zeros((CY, CX), jnp.float32)

    def pack(zi, carry):
        running, packed = carry
        running = tuple(running[c] + main(c, zi - 1) for c in range(2))
        return running, place(zi, running, packed)

    running, packed = lax.fori_loop(
        2, CZ + 2, pack, ((nothing,) * 2, (nothing,) * 4), unroll=UNROLL_PACK
    )

    loads[4].wait()
    mag = mag_ref[...]
    mc_s[...] = jnp.broadcast_to(jnp.sum(mag, axis=0, keepdims=True), (8, CX))
    mr_s[...] = jnp.broadcast_to(jnp.sum(mag, axis=1, keepdims=True), (CY, CX))

    wait_for(wide, others)
    for one in sums:
        one.start()

    def slot(k, z, high):
        return pl.ds(pl.multiple_of((k * (CZ + 2) + z + 1) * high, 8), high)

    class Strip:
        def __init__(self, source, store, high):
            self.source, self.store, self.high = source, store, high

        def raw(self, c, level):
            first = pl.multiple_of((c * EZ + level) * self.high, 8)
            return spacing * self.source[pl.ds(first, self.high), :]

        def level(self, z, ax, ay, before):
            bx, by = self.raw(0, z + 2), self.raw(1, z + 2)
            bz = (turn(ay, -1, 1) - ay) - (turn(ax, -1, 0) - ax)
            values = (
                bx,
                by,
                bz,
                (bz - turn(bz, 1, 0)) - (by - before[1]),
                (bx - before[0]) - (bz - turn(bz, 1, 1)),
                (by - turn(by, 1, 1)) - (bx - turn(bx, 1, 0)),
                ax,
                ay,
            )
            for k, x in enumerate(values):
                self.store[slot(k, z, self.high), :] = x
            return ax + by, ay - bx, (bx, by)

        def middle(self, unroll):
            ground = (self.raw(0, 1), self.raw(1, 1))
            return lax.fori_loop(
                0,
                CZ - 1,
                lambda z, carry: self.level(z, *carry),
                (ground[1], -ground[0], ground),
                unroll=unroll,
            )

        def ends(self, ax, ay, before):
            level_zero = jnp.zeros((self.high, CX), jnp.float32)
            self.level(-1, level_zero, level_zero, (self.raw(0, 0), self.raw(1, 0)))
            ax, ay, before = self.level(CZ - 1, ax, ay, before)
            self.level(CZ, ax, ay, before)

        def at_the_bounds(self, qx, qy):
            pre, high = self.store, self.high

            @pl.when(gz == 0)
            def _():
                pre[slot(3, 0, high), :] = pre[slot(3, 0, high), :] + qx
                pre[slot(4, 0, high), :] = pre[slot(4, 0, high), :] + qy

            @pl.when(gz == NZ_DEV - 1)
            def _():
                z = CZ - 1
                bx, by = pre[slot(0, z, high), :], pre[slot(1, z, high), :]
                tx = pre[slot(7, z, high), :] + qy
                ty = -(pre[slot(6, z, high), :] + qx)
                pre[slot(0, z, high), :] = tx
                pre[slot(1, z, high), :] = ty
                pre[slot(3, z, high), :] = pre[slot(3, z, high), :] - (ty - by)
                pre[slot(4, z, high), :] = pre[slot(4, z, high), :] + (tx - bx)
                pre[slot(5, z, high), :] = (ty - turn(ty, 1, 1)) - (tx - turn(tx, 1, 0))

        def finish(self, z, planes_of):
            qx, qy, cz, cjx, cjy = planes_of
            bx, by, bz, jx, jy, jz, ax, ay = (
                self.store[slot(k, z, self.high), :] for k in range(8)
            )
            d = push((bx, by, bz + cz), (jx + cjx, jy + cjy, jz))
            return (ax + qx + d[0], ay + qy + d[1], d[2])

    def planes_for(qx, qy):
        cz = (turn(qy, -1, 1) - qy) - (turn(qx, -1, 0) - qx)
        return qx, qy, cz, cz - turn(cz, 1, 0), turn(cz, 1, 1) - cz

    block = Strip(side_v, pre_m, CY)
    strip = Strip(ext_v, pre_e, 8)
    block_end = block.middle(UNROLL_PRE)

    @pl.when(gz == half - 1)
    def _():
        for one in ups:
            one.copy.wait_recv()
        half_s[...] = (t_v[...] + tr[0]) + (tr[1] + tr[2])
        pl.semaphore_wait(far, half - 1)
        for one in across:
            one.copy.start()

    col = mag
    row_of = rows((CY, CX))
    for k in (1, 2, 4, 8, 16):
        col = col + jnp.where(row_of >= k, pltpu.roll(col, k, 0), 0.0)
    lin = mag
    lane_of = lanes((CY, CX))
    for k in (1, 2, 4, 8, 16, 32, 64):
        lin = lin + jnp.where(lane_of >= k, pltpu.roll(lin, k, 1), 0.0)
    q_v[pl.ds(0, CY), :] = col
    q_v[pl.ds(CY, CY), :] = lin
    for d, one in enumerate(sums[: NY_DEV - 1]):

        @pl.when(one.back)
        def _(d=d, one=one):
            one.wait_recv()
            q_v[pl.ds(0, CY), :] = q_v[pl.ds(0, CY), :] + mc_r[pl.ds(8 * d, 1), :]

    for d, one in enumerate(sums[NY_DEV - 1 :]):

        @pl.when(one.back)
        def _(d=d, one=one):
            one.wait_recv()
            q_v[pl.ds(CY, CY), :] = q_v[pl.ds(CY, CY), :] + mr_r[pl.ds(CY * d, CY), :]

    q_v[pl.ds(0, CY), :] = (-0.5 * spacing) * q_v[pl.ds(0, CY), :]
    q_v[pl.ds(CY, CY), :] = (0.5 * spacing) * q_v[pl.ds(CY, CY), :]

    for one in layers:
        one.wait_recv()
    for zi in (CZ + 2, CZ + 3):
        running, packed = pack(zi, (running, packed))
    packed = place(0, tuple(-main(c, 0) for c in range(2)), packed)
    for c in range(2):
        o, sign = (1, spacing) if c == 0 else (0, -spacing)
        for k, (ref, x) in enumerate(((w_hi, packed[2 * o]), (w_lo, packed[2 * o + 1]))):
            x = sign * x
            ref[pl.ds(c * CY, CY), :] = x
            wt_lo[pl.ds((2 * k + c) * 8, 8), :] = x[:8]
            wt_hi[pl.ds((2 * k + c) * 8, 8), :] = x[CY - 8 :]
    columns = [
        Hop(w_hi, wn_lo, s_w.at[0], r_w.at[0], dx=1),
        Hop(w_lo, wn_hi, s_w.at[1], r_w.at[1], dx=-1),
        Hop(wt_lo.at[pl.ds(0, 16)], wd.at[0], s_w.at[4], r_w.at[4], dy=-1, dx=1),
        Hop(wt_lo.at[pl.ds(16, 16)], wd.at[1], s_w.at[5], r_w.at[5], dy=-1, dx=-1),
        Hop(wt_hi.at[pl.ds(0, 16)], wd.at[2], s_w.at[6], r_w.at[6], dy=1, dx=1),
        Hop(wt_hi.at[pl.ds(16, 16)], wd.at[3], s_w.at[7], r_w.at[7], dy=1, dx=-1),
        Hop(wt_lo, wy_hi, s_w.at[2], r_w.at[2], dy=-1),
        Hop(wt_hi, wy_lo, s_w.at[3], r_w.at[3], dy=1),
    ]
    for one in columns:
        one.start()

    for c in range(2):
        for i, level in enumerate((0, CZ + 1, CZ + 2)):
            first = c * LEVEL + level * CY
            to = (c * 3 + i) * 2
            cs_lo[pl.ds(to, 2), :] = side_v[pl.ds(first, 2), :]
            cs_hi[pl.ds(to, 2), :] = side_v[pl.ds(first + CY - 2, 2), :]
    cs_lo[pl.ds(12, 4), :] = jnp.zeros((4, CX), jnp.float32)
    cs_hi[pl.ds(12, 4), :] = jnp.zeros((4, CX), jnp.float32)
    corners = [
        Hop(cs_lo, cr_hi, s_c.at[0], r_c.at[0], dy=-1),
        Hop(cs_hi, cr_lo, s_c.at[1], r_c.at[1], dy=1),
    ]
    for one in corners:
        one.start()

    block.ends(*block_end)

    def raise_q(x):
        q_v[pl.ds(0, CY), :] = q_v[pl.ds(0, CY), :] + spacing * x[CY:]
        q_v[pl.ds(CY, CY), :] = q_v[pl.ds(CY, CY), :] - spacing * x[:CY]

    for d, one in enumerate(ups, 1):
        pl.when(one.back & (gz != half - 1))(one.copy.wait_recv)

        @pl.when(one.back)
        def _(d=d):
            raise_q(tr[d - 1])

    for one in faces:
        one.wait_recv()
    for c in range(2):
        for k in range(2):
            here = pl.ds((2 * c + k) * CZ, CZ)
            for j, ref in enumerate((ys_hi, yr_hi, yr_lo, ys_lo)):
                ext_v[pl.ds((c * EZ + 1) * 8 + 2 * j + k, CZ, stride=8), :] = ref[here, :]

    strip_end = strip.middle(UNROLL_STRIP)

    for one in across:
        one.wait_recv()

    @pl.when(gz >= half)
    def _():
        raise_q(half_r[...])

    q = tuple(q_v[pl.ds(c * CY, CY), :] for c in range(2))
    lane8 = lanes((8, CX))
    few = jnp.zeros((8, CX), jnp.float32)
    for c in range(2):
        for t in range(CY // 8):
            first = 4 * (CY // 8 * c + t)
            here = (lane8 >= first) & (lane8 < first + 4)
            few = jnp.where(here, turn(q[c][8 * t : 8 * t + 8], first + 2, 1), few)
        qt_lo[pl.ds(c * 8, 8), :] = q[c][:8]
        qt_hi[pl.ds(c * 8, 8), :] = q[c][CY - 8 :]
    qc[...] = few
    planes = [
        Hop(qc, qn.at[0], s_q.at[0], r_q.at[0], dx=1),
        Hop(qc, qn.at[1], s_q.at[1], r_q.at[1], dx=-1),
        Hop(qc, qn.at[2], s_q.at[2], r_q.at[2], dy=-1, dx=1),
        Hop(qc, qn.at[3], s_q.at[3], r_q.at[3], dy=-1, dx=-1),
        Hop(qc, qn.at[4], s_q.at[4], r_q.at[4], dy=1, dx=1),
        Hop(qc, qn.at[5], s_q.at[5], r_q.at[5], dy=1, dx=-1),
        Hop(qt_lo, qy_hi, s_q.at[6], r_q.at[6], dy=-1),
        Hop(qt_hi, qy_lo, s_q.at[7], r_q.at[7], dy=1),
    ]
    for one in planes:
        one.start()

    block.at_the_bounds(*q)
    block_planes = planes_for(*q)

    def finish_block(z, _):
        new = block.finish(z, block_planes)
        for c in range(3):
            first = pl.multiple_of((c * (CZ + 2) + z + 1) * EY, 8)
            a1_out[pl.ds(first, CY), :] = new[c]
        return 0

    lax.fori_loop(-1, CZ + 1, finish_block, 0, unroll=UNROLL_POST)

    for one in corners:
        one.wait_recv()
    for c in range(2):
        for i, level in enumerate((0, CZ + 1, CZ + 2)):
            first = (c * EZ + level) * 8
            of = pl.ds((c * 3 + i) * 2, 2)
            for j, ref in enumerate((cs_hi, cr_hi, cr_lo, cs_lo)):
                ext_v[pl.ds(first + 2 * j, 2), :] = ref[of, :]
    strip.ends(*strip_end)

    row8 = rows((8, CX))

    def plane(middle, from_hi, from_lo):
        tile = jnp.where(row8 < 2, from_hi, jnp.where(row8 >= 6, from_lo, 0.0))
        return jnp.concatenate([middle, tile], axis=0)

    for one in columns:
        one.wait_recv()
    lane, row = lanes((EY, CX)), rows((EY, CX))
    even = lane % 2 == 0
    level_ok = ((lane >= 4) | (gz > 0)) & ((lane < 2 * (CZ + 2)) | (gz < NZ_DEV - 1))
    grown = []
    for c in range(2):
        mine, tile, other = pl.ds(c * CY, CY), pl.ds(c * 8, 8), pl.ds(16 + c * 8, 8)
        hi = plane(w_hi[mine, :], wy_hi[tile, :], wy_lo[tile, :])
        lo = plane(w_lo[mine, :], wy_hi[other, :], wy_lo[other, :])
        lon = plane(wn_lo[mine, :], wd[0, tile, :], wd[2, tile, :])
        hin = plane(wn_hi[mine, :], wd[1, tile, :], wd[3, tile, :])
        pairs = (
            (hi, turn(lon, 1, 1)),
            (turn(hi, -1, 1), lon),
            (turn(hin, -2, 1), turn(lo, -1, 1)),
            (turn(hin, -3, 1), turn(lo, -2, 1)),
        )
        grown.append([jnp.where(even, *pair) for pair in pairs])

    for one in planes:
        one.wait_recv()

    def spread(x, i):
        return jnp.broadcast_to(x[:, i : i + 1], x.shape)

    def beyond(side, from_hi, from_lo, c, i):
        first = 4 * (CY // 8) * c + i
        x, x_hi, x_lo = qn[side], qn[from_hi], qn[from_lo]
        middle = [spread(x, first + 4 * t) for t in range(CY // 8)]
        middle = jnp.concatenate(middle, axis=0)
        return plane(middle, spread(x_hi, first), spread(x_lo, first + 4 * (CY // 8 - 1)))

    ea = [[None, None] for _ in range(4)]
    carry_plane = []
    for c in range(2):
        tile = pl.ds(c * 8, 8)
        own = plane(q[c], qy_hi[tile, :], qy_lo[tile, :])
        sides = (
            (spread(own, CX - 2), beyond(0, 2, 4, c, 0)),
            (spread(own, CX - 1), beyond(0, 2, 4, c, 1)),
            (beyond(1, 3, 5, c, 2), spread(own, 0)),
            (beyond(1, 3, 5, c, 3), spread(own, 1)),
        )
        for m, pair in enumerate(sides):
            value = jnp.where(even, *pair) + grown[c][m]
            ea[m][c] = jnp.where(level_ok, value, 0.0)
        around = (q[c][CY - 8 :], qy_hi[tile, :], qy_lo[tile, :], q[c][:8])
        turned = [turn(x, by, 0) for x, by in zip(around, (2, 2, -2, -2))]
        carry_plane.append(
            jnp.where(
                row8 < 4,
                jnp.where(row8 < 2, turned[0], turned[1]),
                jnp.where(row8 < 6, turned[2], turned[3]),
            )
        )

    row_ok = ((row < CY) | (row >= CY + 2) | (gy < NY_DEV - 1)) & ((row < CY + 2) | (gy > 0))
    eb = []
    for m in range(3):
        up_y = (turn(ea[m][0], -1, 0),)
        up_z = tuple(turn(x, -2, 1) for x in ea[m])
        eb.append(fields(ea[m], up_z, up_y, ea[m + 1], True))
    ea1 = []
    for m in (1, 2):
        down_z = tuple(turn(x, 2, 1) for x in eb[m])
        down_y = tuple(turn(x, 1, 0) for x in eb[m])
        d = drive(eb[m], down_z, down_y, eb[m - 1])
        if m == 1:
            outside = (lane % 2 == 1) & (gx == 0)
        else:
            outside = (lane % 2 == 0) & (gx == NX_DEV - 1)
        ok = row_ok & jnp.logical_not(outside) & level_ok
        a = (ea[m][0] + d[0], ea[m][1] + d[1], d[2])
        ea1.append(tuple(jnp.where(ok, x, 0.0) for x in a))
    near = ea1[0]
    eb1 = fields(
        near,
        tuple(turn(x, -2, 1) for x in near),
        tuple(turn(x, -1, 0) for x in near),
        ea1[1],
        False,
    )
    v_out[pl.ds(0, EY), :] = jnp.where(even, ea1[1][1], eb1[2])
    v_out[pl.ds(EY, EY), :] = jnp.where(even, ea1[1][2], eb1[1])
    edge = tuple(jnp.where(even, ea1[0][c], ea1[1][c]) for c in range(3))

    strip.at_the_bounds(*carry_plane)
    strip_planes = planes_for(*carry_plane)
    rim = (lane == 0) | (lane == CX - 1)
    tile_ok = ((row8 >= 2) | (gy < NY_DEV - 1)) & ((row8 < 2) | (gy > 0))

    def finish_strip(z, _):
        new = strip.finish(z, strip_planes)
        shift = lax.rem(2 * CX - 1 - 2 * (z + 2), CX)
        for c in range(3):
            first = pl.multiple_of((c * (CZ + 2) + z + 1) * EY, 8)
            left, right = turn(new[c], -2, 0), turn(new[c], 2, 0)
            x = jnp.concatenate(
                [
                    jnp.where(row8 == 0, right, a1_out[pl.ds(first, 8), :]),
                    a1_out[pl.ds(first + 8, 16), :],
                    jnp.where(row8 == 7, left, a1_out[pl.ds(first + 24, 8), :]),
                    jnp.where(row8 < 4, left, right),
                ],
                axis=0,
            )
            x = jnp.where(rim, pltpu.roll(edge[c], shift, 1), x)
            a1_out[pl.ds(first, CY), :] = x[:CY]
            a1_out[pl.ds(first + CY, 8), :] = jnp.where(tile_ok, x[CY:], 0.0)
        return 0

    lax.fori_loop(-1, CZ + 1, finish_strip, 0, unroll=UNROLL_EDGE)

    @pl.when(gz == 0)
    def _():
        for c in range(3):
            a1_out[slot(c, -1, EY), :] = jnp.zeros((EY, CX), jnp.float32)

    @pl.when(gz == NZ_DEV - 1)
    def _():
        for c in range(3):
            a1_out[slot(c, CZ, EY), :] = jnp.zeros((EY, CX), jnp.float32)

    for one in ups + across + sums + layers + faces + corners + columns + planes:
        one.wait_send()


def step_kernel(a1, v_ref, out_hbm, out_v, store_sem):
    lane = lanes((EY, CX))
    first_lane, last_lane = lane == 0, lane == CX - 1

    def new_at(z):
        return tuple(
            a1[pl.ds(pl.multiple_of((c * (CZ + 2) + z + 1) * EY, 8), EY), :] for c in range(3)
        )

    def beside(z):
        shift = lax.rem(2 * CX - 1 - 2 * (z + 2), CX)
        return tuple(pltpu.roll(v_ref[pl.ds(k * EY, EY), :], shift, 1) for k in range(2))

    def second_field(a, a_up, v):
        yp = (turn(a[0], -1, 0), None, turn(a[2], -1, 0))
        xp = (
            None,
            jnp.where(last_lane, v[0], turn(a[1], -1, 1)),
            jnp.where(last_lane, v[1], turn(a[2], -1, 1)),
        )
        return fields(a, a_up, yp, xp, False)

    first_main, main = first_lane[:CY], slice(0, CY)

    def level_two(z, carry):
        a, before = carry
        v = beside(z)
        a_up = new_at(z + 1)
        b = second_field(a, a_up, v)
        ym = (turn(b[0], 1, 0)[main], None, turn(b[2], 1, 0)[main])
        own = tuple(x[main] for x in b)
        xm = (
            None,
            jnp.where(first_main, v[1][main], turn(own[1], 1, 1)),
            jnp.where(first_main, v[0][main], turn(own[2], 1, 1)),
        )
        d = drive(own, before, ym, xm)
        for c in range(3):
            out_v[pl.ds(pl.multiple_of((c * CZ + z) * CY, 8), CY), :] = a[c][main] + d[c]
        return a_up, (own[0], own[1])

    below, a = new_at(-1), new_at(0)
    b = second_field(below, a, beside(-1))
    carry = (a, (b[0][main], b[1][main]))
    part = 8

    def store(k, c):
        there = pl.ds(pl.multiple_of((c * CZ + k * part) * CY, 8), part * CY)
        return pltpu.make_async_copy(out_v.at[there], out_hbm.at[there], store_sem.at[k, c])

    def chunk(k, carry):
        carry = lax.fori_loop(
            0, part, lambda i, x: level_two(k * part + i, x), carry, unroll=4
        )
        for c in range(3):
            store(k, c).start()
        return carry

    lax.fori_loop(0, CZ // part, chunk, carry)
    for k in range(CZ // part):
        for c in range(3):
            store(k, c).wait()


def f32(*shape):
    return jax.ShapeDtypeStruct(shape, jnp.float32)


def vmem(*shape):
    return pltpu.VMEM(shape, jnp.float32)


def local(side_field, magnetogram):
    side = pltpu.with_memory_space_constraint(side_field.reshape(2 * CZ * CY, CX), pltpu.HBM)
    magnetogram = pltpu.with_memory_space_constraint(magnetogram, pltpu.HBM)
    whole = pl.BlockSpec(memory_space=pltpu.VMEM)
    dma = pltpu.SemaphoreType.DMA
    a1, v = pl.pallas_call(
        comm_kernel,
        out_shape=(f32(3 * (CZ + 2) * EY, CX), f32(2 * EY, CX)),
        in_specs=[pl.BlockSpec(memory_space=pltpu.HBM)] * 2,
        out_specs=(whole,) * 2,
        scratch_shapes=[
            vmem(CY, CX),
            vmem(2 * EZ * 8, CX),
            vmem(8 * (CZ + 2) * CY, CX),
            vmem(8 * (CZ + 2) * 8, CX),
            vmem(2 * LEVEL, CX),
            vmem(2 * CY, CX),
            vmem(NZ_DEV // 2 - 1, 2 * CY, CX),
            vmem(2 * CY, CX),
            vmem(2 * CY, CX),
        ]
        + [vmem(4 * CZ, CX)] * 4
        + [vmem(16, CX)] * 4
        + [vmem(2 * CY, CX)] * 4
        + [vmem(32, CX)] * 4
        + [
            vmem(4, 16, CX),
            vmem(8, CX),
            vmem(CY, CX),
            vmem(8 * (NY_DEV - 1), CX),
            vmem(CY * (NX_DEV - 1), CX),
            vmem(2 * CY, CX),
            vmem(8, CX),
            vmem(6, 8, CX),
            vmem(16, CX),
            vmem(16, CX),
            vmem(16, CX),
            vmem(16, CX),
        ]
        + [pltpu.SemaphoreType.REGULAR] * 3
        + [dma((5,))]
        + [dma((NZ_DEV - 1,))] * 2
        + [dma((2, 2))] * 2
        + [dma((2,))] * 4
        + [dma((8,))] * 2
        + [dma((NY_DEV - 1,))] * 2
        + [dma((NX_DEV - 1,))] * 2
        + [dma((8,))] * 2,
        compiler_params=pltpu.CompilerParams(
            collective_id=0, has_side_effects=True, vmem_limit_bytes=VMEM_BYTES
        ),
        name="exchange",
    )(side, magnetogram)
    out = pl.pallas_call(
        step_kernel,
        out_shape=f32(3 * CZ * CY, CX),
        in_specs=[whole] * 2,
        out_specs=pl.BlockSpec(memory_space=pltpu.HBM),
        scratch_shapes=[vmem(3 * CZ * CY, CX), dma((CZ // 8, 3))],
        compiler_params=pltpu.CompilerParams(vmem_limit_bytes=VMEM_BYTES),
        name="steps",
    )(a1, v)
    return out.reshape(3, CZ, CY, CX)


def solution(mesh):
    return jax.shard_map(
        local,
        mesh=mesh,
        in_specs=(P(None, "gz", "gy", "gx"), P("gy", "gx")),
        out_specs=P(None, "gz", "gy", "gx"),
        check_vma=False,
    )
```

```python
import functools

import jax
import jax.numpy as jnp
from jax import lax
from jax.experimental import pallas as pl
from jax.experimental.pallas import tpu as pltpu
from jax.sharding import PartitionSpec as P

spacing = 0.0625
friction = 0.004
MESH = pl.DeviceIdType.MESH

VMEM_BYTES = 24 * 2**20
UNROLL_PRE, UNROLL_STRIP, UNROLL_POST, UNROLL_EDGE, UNROLL_PACK = 8, 8, 4, 25, 8
NZ_DEV, NY_DEV, NX_DEV = 8, 8, 4
CZ, CY, CX = 48, 32, 128
EZ = CZ + 3
EY = CY + 8
LEVEL = EZ * CY


def lanes(shape):
    return lax.broadcasted_iota(jnp.int32, shape, len(shape) - 1)


def rows(shape):
    return lax.broadcasted_iota(jnp.int32, shape, len(shape) - 2)


def turn(x, shift, axis):
    return pltpu.roll(x, shift % x.shape[axis], axis)


def fields(a, zp, yp, xp, first):
    ax, ay = a[0], a[1]
    if first:
        bx = ay - zp[1]
        by = zp[0] - ax
    else:
        bx = (yp[2] - a[2]) - (zp[1] - ay)
        by = (zp[0] - ax) - (xp[2] - a[2])
    bz = (xp[1] - ay) - (yp[0] - ax)
    return bx, by, bz


def drive(b, zm, ym, xm):
    bx, by, bz = b
    jx = (bz - ym[2]) - (by - zm[1])
    jy = (bx - zm[0]) - (bz - xm[2])
    jz = (by - xm[1]) - (bx - ym[0])
    return push(b, (jx, jy, jz))


def push(b, j):
    bx, by, bz = b
    jx, jy, jz = j
    square = bx * bx + by * by + bz * bz
    scale = (friction / spacing**2) / (square + spacing**2)
    along = (jx * bx + jy * by + jz * bz) * scale
    across = square * scale
    return (along * bx - across * jx, along * by - across * jy, along * bz - across * jz)


def comm_kernel(
    side_hbm,
    mag_hbm,
    a1_out,
    v_out,
    mag_ref,
    ext_v,
    pre_m,
    pre_e,
    side_v,
    t_v,
    tr,
    half_s,
    half_r,
    ys_lo,
    ys_hi,
    yr_lo,
    yr_hi,
    cs_lo,
    cs_hi,
    cr_lo,
    cr_hi,
    w_hi,
    w_lo,
    wn_hi,
    wn_lo,
    wt_lo,
    wt_hi,
    wy_lo,
    wy_hi,
    wd,
    mc_s,
    mr_s,
    mc_r,
    mr_r,
    q_v,
    qc,
    qn,
    qt_lo,
    qt_hi,
    qy_lo,
    qy_hi,
    here_sem,
    wide,
    far,
    load_sem,
    s_t,
    r_t,
    s_z,
    r_z,
    s_y,
    r_y,
    s_c,
    r_c,
    s_w,
    r_w,
    s_mc,
    r_mc,
    s_mr,
    r_mr,
    s_q,
    r_q,
):
    gz, gy, gx = lax.axis_index("gz"), lax.axis_index("gy"), lax.axis_index("gx")

    def at(dz=0, dy=0, dx=0):
        where = {}
        if dz:
            where["gz"] = lax.rem(gz + dz + NZ_DEV, NZ_DEV)
        if dy:
            where["gy"] = lax.rem(gy + dy + NY_DEV, NY_DEV)
        if dx:
            where["gx"] = lax.rem(gx + dx + NX_DEV, NX_DEV)
        return where

    def there(dz=0, dy=0, dx=0):
        ok = None
        for here, d, size in ((gz, dz, NZ_DEV), (gy, dy, NY_DEV), (gx, dx, NX_DEV)):
            if d:
                one = here + d < size if d > 0 else here + d >= 0
                ok = one if ok is None else jnp.logical_and(ok, one)
        return ok

    class Hop:
        def __init__(self, src, dst, ssem, rsem, **by):
            self.copy = pltpu.make_async_remote_copy(
                src_ref=src,
                dst_ref=dst,
                send_sem=ssem,
                recv_sem=rsem,
                device_id=at(**by),
                device_id_type=MESH,
            )
            self.to = there(**by)
            self.back = there(**{k: -v for k, v in by.items()})

        def start(self):
            pl.when(self.to)(self.copy.start)

        def wait_send(self):
            pl.when(self.to)(self.copy.wait_send)

        def wait_recv(self):
            pl.when(self.back)(self.copy.wait_recv)

    half = NZ_DEV // 2
    place_z = lax.rem(gz, half)
    middle = (gz == half - 1).astype(jnp.int32)
    barrier = pltpu.get_barrier_semaphore()

    def tell(sem, ok, **by):
        @pl.when(ok)
        def _():
            pl.semaphore_signal(sem, inc=1, device_id=at(**by), device_id_type=MESH)

    def wait_for(sem, count):
        @pl.when(count > 0)
        def _():
            pl.semaphore_wait(sem, count)

    def close(d):
        return jnp.logical_or(place_z >= d, jnp.logical_and(gz == half, d == 1))

    higher = (
        [dict(dy=d) for d in range(1, NY_DEV)]
        + [dict(dx=d) for d in range(1, NX_DEV)]
        + [dict(dy=1, dx=1), dict(dy=1, dx=-1)]
    )
    heard = place_z + (gz >= half).astype(jnp.int32) + gy + gx
    answers = (half - 1 - place_z) + middle
    for d in range(1, half + 1):
        tell(barrier, there(dz=d) & ((place_z + d < half) | (gz == half - 1)), dz=d)
    answers = answers + there(dy=1).astype(jnp.int32) + there(dx=1).astype(jnp.int32)
    others = jnp.maximum(NY_DEV - 2 - gy, 0) + jnp.maximum(NX_DEV - 2 - gx, 0)
    for by in higher:
        tell(barrier, there(**by), **by)
    for by in higher[-2:]:
        heard = heard + there(**{k: -v for k, v in by.items()}).astype(jnp.int32)
        answers = answers + there(**by).astype(jnp.int32)
    part = CZ // 2 * CY
    loads = [
        pltpu.make_async_copy(
            side_hbm.at[pl.ds(c * CZ * CY + k * part, part)],
            side_v.at[pl.ds(c * LEVEL + CY + k * part, part)],
            load_sem.at[2 * c + k],
        )
        for c in range(2)
        for k in range(2)
    ]
    loads.append(pltpu.make_async_copy(mag_hbm, mag_ref, load_sem.at[4]))
    for load in loads:
        load.start()
    wait_for(barrier, heard)
    for d in range(1, half):
        tell(here_sem, there(dz=-d) & close(d), dz=-d)
    for d in range(2, half + 1):
        tell(far, gz == half - 1 + d, dz=-d)
    for by in higher:
        back = {k: -v for k, v in by.items()}
        step = max(by.values())
        tell(here_sem if step == 1 else wide, there(**back), **back)

    def clear(by, *refs):
        @pl.when(jnp.logical_not(there(**by)))
        def _():
            for ref in refs:
                ref[...] = jnp.zeros_like(ref)

    clear(dict(dz=-1), side_v.at[pl.ds(0, CY)], side_v.at[pl.ds(LEVEL, CY)])
    clear(
        dict(dz=1),
        side_v.at[pl.ds((CZ + 1) * CY, 2 * CY)],
        side_v.at[pl.ds(LEVEL + (CZ + 1) * CY, 2 * CY)],
    )
    clear(dict(dy=-1), yr_lo, cr_lo, wy_lo, qy_lo)
    clear(dict(dy=1), yr_hi, cr_hi, wy_hi, qy_hi)
    clear(dict(dx=-1), wn_lo)
    clear(dict(dx=1), wn_hi)
    clear(dict(dx=-1), qn.at[0])
    clear(dict(dx=1), qn.at[1])
    for i, by in enumerate((dict(dy=1, dx=-1), dict(dy=1, dx=1), dict(dy=-1, dx=-1), dict(dy=-1, dx=1))):
        clear(by, wd.at[i], qn.at[2 + i])

    for c in range(2):
        total = jnp.zeros((CY, CX), jnp.float32)
        for k in range(2):
            loads[2 * c + k].wait()

            def add(z, total, c=c):
                return total + side_v[pl.ds(c * LEVEL + (z + 1) * CY, CY), :]

            total = lax.fori_loop(k * CZ // 2, (k + 1) * CZ // 2, add, total, unroll=8)
        t_v[pl.ds(c * CY, CY), :] = total
    wait_for(here_sem, answers)

    layers = []
    for c in range(2):
        layers.append(
            Hop(
                side_hbm.at[pl.ds(c * CZ * CY + (CZ - 1) * CY, CY)],
                side_v.at[pl.ds(c * LEVEL, CY)],
                s_z.at[0, c],
                r_z.at[0, c],
                dz=1,
            )
        )
        layers.append(
            Hop(
                side_hbm.at[pl.ds(c * CZ * CY, 2 * CY)],
                side_v.at[pl.ds(c * LEVEL + (CZ + 1) * CY, 2 * CY)],
                s_z.at[1, c],
                r_z.at[1, c],
                dz=-1,
            )
        )

    ups = [Hop(t_v, tr.at[d - 1], s_t.at[d - 1], r_t.at[d - 1], dz=d) for d in range(1, half)]
    for d, one in enumerate(ups, 1):
        one.to = one.to & (place_z + d < half)
        one.back = place_z >= d
    across = [
        Hop(half_s, half_r, s_t.at[half - 2 + d], r_t.at[half - 2 + d], dz=d)
        for d in range(1, half + 1)
    ]
    for d, one in enumerate(across, 1):
        one.to = gz == half - 1
        one.back = gz == half - 1 + d
    for one in ups:
        one.start()
    for one in layers:
        one.start()

    sums = [
        Hop(mc_s, mc_r.at[pl.ds(8 * (d - 1), 8)], s_mc.at[d - 1], r_mc.at[d - 1], dy=d)
        for d in range(1, NY_DEV)
    ] + [
        Hop(mr_s, mr_r.at[pl.ds(CY * (d - 1), CY)], s_mr.at[d - 1], r_mr.at[d - 1], dx=d)
        for d in range(1, NX_DEV)
    ]

    for c in range(2):
        for k in range(2):
            here = pl.ds((2 * c + k) * CZ, CZ)
            ys_lo[here, :] = side_v[pl.ds(c * LEVEL + CY + k, CZ, stride=CY), :]
            ys_hi[here, :] = side_v[pl.ds(c * LEVEL + CY + CY - 2 + k, CZ, stride=CY), :]
    faces = [
        Hop(ys_lo, yr_hi, s_y.at[0], r_y.at[0], dy=-1),
        Hop(ys_hi, yr_lo, s_y.at[1], r_y.at[1], dy=1),
    ]
    for one in faces:
        one.start()

    main_lane = lanes((CY, CX))

    def main(c, level):
        return side_v[pl.ds(pl.multiple_of(c * LEVEL + level * CY, 8), CY), :]

    def place(zi, running, packed):
        first = 2 * zi
        out = []
        for c in range(2):
            turned = pltpu.roll(running[c], first + 2, 1)
            hi, lo = packed[2 * c], packed[2 * c + 1]
            out.append(jnp.where((main_lane == first) | (main_lane == first + 1), turned, hi))
            out.append(jnp.where((main_lane == first + 2) | (main_lane == first + 3), turned, lo))
        return tuple(out)

    nothing = jnp.zeros((CY, CX), jnp.float32)

    def pack(zi, carry):
        running, packed = carry
        running = tuple(running[c] + main(c, zi - 1) for c in range(2))
        return running, place(zi, running, packed)

    running, packed = lax.fori_loop(
        2, CZ + 2, pack, ((nothing,) * 2, (nothing,) * 4), unroll=UNROLL_PACK
    )

    loads[4].wait()
    mag = mag_ref[...]
    mc_s[...] = jnp.broadcast_to(jnp.sum(mag, axis=0, keepdims=True), (8, CX))
    mr_s[...] = jnp.broadcast_to(jnp.sum(mag, axis=1, keepdims=True), (CY, CX))

    wait_for(wide, others)
    for one in sums:
        one.start()

    def slot(k, z, high):
        return pl.ds(pl.multiple_of((k * (CZ + 2) + z + 1) * high, 8), high)

    class Strip:
        def __init__(self, source, store, high):
            self.source, self.store, self.high = source, store, high

        def raw(self, c, level):
            first = pl.multiple_of((c * EZ + level) * self.high, 8)
            return spacing * self.source[pl.ds(first, self.high), :]

        def level(self, z, ax, ay, before):
            bx, by = self.raw(0, z + 2), self.raw(1, z + 2)
            bz = (turn(ay, -1, 1) - ay) - (turn(ax, -1, 0) - ax)
            values = (
                bx,
                by,
                bz,
                (bz - turn(bz, 1, 0)) - (by - before[1]),
                (bx - before[0]) - (bz - turn(bz, 1, 1)),
                (by - turn(by, 1, 1)) - (bx - turn(bx, 1, 0)),
                ax,
                ay,
            )
            for k, x in enumerate(values):
                self.store[slot(k, z, self.high), :] = x
            return ax + by, ay - bx, (bx, by)

        def middle(self, unroll):
            ground = (self.raw(0, 1), self.raw(1, 1))
            return lax.fori_loop(
                0,
                CZ - 1,
                lambda z, carry: self.level(z, *carry),
                (ground[1], -ground[0], ground),
                unroll=unroll,
            )

        def ends(self, ax, ay, before):
            level_zero = jnp.zeros((self.high, CX), jnp.float32)
            self.level(-1, level_zero, level_zero, (self.raw(0, 0), self.raw(1, 0)))
            ax, ay, before = self.level(CZ - 1, ax, ay, before)
            self.level(CZ, ax, ay, before)

        def at_the_bounds(self, qx, qy):
            pre, high = self.store, self.high

            @pl.when(gz == 0)
            def _():
                pre[slot(3, 0, high), :] = pre[slot(3, 0, high), :] + qx
                pre[slot(4, 0, high), :] = pre[slot(4, 0, high), :] + qy

            @pl.when(gz == NZ_DEV - 1)
            def _():
                z = CZ - 1
                bx, by = pre[slot(0, z, high), :], pre[slot(1, z, high), :]
                tx = pre[slot(7, z, high), :] + qy
                ty = -(pre[slot(6, z, high), :] + qx)
                pre[slot(0, z, high), :] = tx
                pre[slot(1, z, high), :] = ty
                pre[slot(3, z, high), :] = pre[slot(3, z, high), :] - (ty - by)
                pre[slot(4, z, high), :] = pre[slot(4, z, high), :] + (tx - bx)
                pre[slot(5, z, high), :] = (ty - turn(ty, 1, 1)) - (tx - turn(tx, 1, 0))

        def finish(self, z, planes_of):
            qx, qy, cz, cjx, cjy = planes_of
            bx, by, bz, jx, jy, jz, ax, ay = (
                self.store[slot(k, z, self.high), :] for k in range(8)
            )
            d = push((bx, by, bz + cz), (jx + cjx, jy + cjy, jz))
            return (ax + qx + d[0], ay + qy + d[1], d[2])

    def planes_for(qx, qy):
        cz = (turn(qy, -1, 1) - qy) - (turn(qx, -1, 0) - qx)
        return qx, qy, cz, cz - turn(cz, 1, 0), turn(cz, 1, 1) - cz

    block = Strip(side_v, pre_m, CY)
    strip = Strip(ext_v, pre_e, 8)
    block_end = block.middle(UNROLL_PRE)

    @pl.when(gz == half - 1)
    def _():
        for one in ups:
            one.copy.wait_recv()
        half_s[...] = (t_v[...] + tr[0]) + (tr[1] + tr[2])
        pl.semaphore_wait(far, half - 1)
        for one in across:
            one.copy.start()

    col = mag
    row_of = rows((CY, CX))
    for k in (1, 2, 4, 8, 16):
        col = col + jnp.where(row_of >= k, pltpu.roll(col, k, 0), 0.0)
    lin = mag
    lane_of = lanes((CY, CX))
    for k in (1, 2, 4, 8, 16, 32, 64):
        lin = lin + jnp.where(lane_of >= k, pltpu.roll(lin, k, 1), 0.0)
    q_v[pl.ds(0, CY), :] = col
    q_v[pl.ds(CY, CY), :] = lin
    for d, one in enumerate(sums[: NY_DEV - 1]):

        @pl.when(one.back)
        def _(d=d, one=one):
            one.wait_recv()
            q_v[pl.ds(0, CY), :] = q_v[pl.ds(0, CY), :] + mc_r[pl.ds(8 * d, 1), :]

    for d, one in enumerate(sums[NY_DEV - 1 :]):

        @pl.when(one.back)
        def _(d=d, one=one):
            one.wait_recv()
            q_v[pl.ds(CY, CY), :] = q_v[pl.ds(CY, CY), :] + mr_r[pl.ds(CY * d, CY), :]

    q_v[pl.ds(0, CY), :] = (-0.5 * spacing) * q_v[pl.ds(0, CY), :]
    q_v[pl.ds(CY, CY), :] = (0.5 * spacing) * q_v[pl.ds(CY, CY), :]

    for one in layers:
        one.wait_recv()
    for zi in (CZ + 2, CZ + 3):
        running, packed = pack(zi, (running, packed))
    packed = place(0, tuple(-main(c, 0) for c in range(2)), packed)
    for c in range(2):
        o, sign = (1, spacing) if c == 0 else (0, -spacing)
        for k, (ref, x) in enumerate(((w_hi, packed[2 * o]), (w_lo, packed[2 * o + 1]))):
            x = sign * x
            ref[pl.ds(c * CY, CY), :] = x
            wt_lo[pl.ds((2 * k + c) * 8, 8), :] = x[:8]
            wt_hi[pl.ds((2 * k + c) * 8, 8), :] = x[CY - 8 :]
    columns = [
        Hop(w_hi, wn_lo, s_w.at[0], r_w.at[0], dx=1),
        Hop(w_lo, wn_hi, s_w.at[1], r_w.at[1], dx=-1),
        Hop(wt_lo.at[pl.ds(0, 16)], wd.at[0], s_w.at[4], r_w.at[4], dy=-1, dx=1),
        Hop(wt_lo.at[pl.ds(16, 16)], wd.at[1], s_w.at[5], r_w.at[5], dy=-1, dx=-1),
        Hop(wt_hi.at[pl.ds(0, 16)], wd.at[2], s_w.at[6], r_w.at[6], dy=1, dx=1),
        Hop(wt_hi.at[pl.ds(16, 16)], wd.at[3], s_w.at[7], r_w.at[7], dy=1, dx=-1),
        Hop(wt_lo, wy_hi, s_w.at[2], r_w.at[2], dy=-1),
        Hop(wt_hi, wy_lo, s_w.at[3], r_w.at[3], dy=1),
    ]
    for one in columns:
        one.start()

    for c in range(2):
        for i, level in enumerate((0, CZ + 1, CZ + 2)):
            first = c * LEVEL + level * CY
            to = (c * 3 + i) * 2
            cs_lo[pl.ds(to, 2), :] = side_v[pl.ds(first, 2), :]
            cs_hi[pl.ds(to, 2), :] = side_v[pl.ds(first + CY - 2, 2), :]
    cs_lo[pl.ds(12, 4), :] = jnp.zeros((4, CX), jnp.float32)
    cs_hi[pl.ds(12, 4), :] = jnp.zeros((4, CX), jnp.float32)
    corners = [
        Hop(cs_lo, cr_hi, s_c.at[0], r_c.at[0], dy=-1),
        Hop(cs_hi, cr_lo, s_c.at[1], r_c.at[1], dy=1),
    ]
    for one in corners:
        one.start()

    block.ends(*block_end)

    def raise_q(x):
        q_v[pl.ds(0, CY), :] = q_v[pl.ds(0, CY), :] + spacing * x[CY:]
        q_v[pl.ds(CY, CY), :] = q_v[pl.ds(CY, CY), :] - spacing * x[:CY]

    for d, one in enumerate(ups, 1):
        pl.when(one.back & (gz != half - 1))(one.copy.wait_recv)

        @pl.when(one.back)
        def _(d=d):
            raise_q(tr[d - 1])

    for one in faces:
        one.wait_recv()
    for c in range(2):
        for k in range(2):
            here = pl.ds((2 * c + k) * CZ, CZ)
            for j, ref in enumerate((ys_hi, yr_hi, yr_lo, ys_lo)):
                ext_v[pl.ds((c * EZ + 1) * 8 + 2 * j + k, CZ, stride=8), :] = ref[here, :]

    strip_end = strip.middle(UNROLL_STRIP)

    for one in across:
        one.wait_recv()

    @pl.when(gz >= half)
    def _():
        raise_q(half_r[...])

    q = tuple(q_v[pl.ds(c * CY, CY), :] for c in range(2))
    lane8 = lanes((8, CX))
    few = jnp.zeros((8, CX), jnp.float32)
    for c in range(2):
        for t in range(CY // 8):
            first = 4 * (CY // 8 * c + t)
            here = (lane8 >= first) & (lane8 < first + 4)
            few = jnp.where(here, turn(q[c][8 * t : 8 * t + 8], first + 2, 1), few)
        qt_lo[pl.ds(c * 8, 8), :] = q[c][:8]
        qt_hi[pl.ds(c * 8, 8), :] = q[c][CY - 8 :]
    qc[...] = few
    planes = [
        Hop(qc, qn.at[0], s_q.at[0], r_q.at[0], dx=1),
        Hop(qc, qn.at[1], s_q.at[1], r_q.at[1], dx=-1),
        Hop(qc, qn.at[2], s_q.at[2], r_q.at[2], dy=-1, dx=1),
        Hop(qc, qn.at[3], s_q.at[3], r_q.at[3], dy=-1, dx=-1),
        Hop(qc, qn.at[4], s_q.at[4], r_q.at[4], dy=1, dx=1),
        Hop(qc, qn.at[5], s_q.at[5], r_q.at[5], dy=1, dx=-1),
        Hop(qt_lo, qy_hi, s_q.at[6], r_q.at[6], dy=-1),
        Hop(qt_hi, qy_lo, s_q.at[7], r_q.at[7], dy=1),
    ]
    for one in planes:
        one.start()

    block.at_the_bounds(*q)
    block_planes = planes_for(*q)

    def finish_block(z, _):
        new = block.finish(z, block_planes)
        for c in range(3):
            first = pl.multiple_of((c * (CZ + 2) + z + 1) * EY, 8)
            a1_out[pl.ds(first, CY), :] = new[c]
        return 0

    lax.fori_loop(-1, CZ + 1, finish_block, 0, unroll=UNROLL_POST)

    for one in corners:
        one.wait_recv()
    for c in range(2):
        for i, level in enumerate((0, CZ + 1, CZ + 2)):
            first = (c * EZ + level) * 8
            of = pl.ds((c * 3 + i) * 2, 2)
            for j, ref in enumerate((cs_hi, cr_hi, cr_lo, cs_lo)):
                ext_v[pl.ds(first + 2 * j, 2), :] = ref[of, :]
    strip.ends(*strip_end)

    row8 = rows((8, CX))

    def plane(middle, from_hi, from_lo):
        tile = jnp.where(row8 < 2, from_hi, jnp.where(row8 >= 6, from_lo, 0.0))
        return jnp.concatenate([middle, tile], axis=0)

    for one in columns:
        one.wait_recv()
    lane, row = lanes((EY, CX)), rows((EY, CX))
    even = lane % 2 == 0
    level_ok = ((lane >= 4) | (gz > 0)) & ((lane < 2 * (CZ + 2)) | (gz < NZ_DEV - 1))
    grown = []
    for c in range(2):
        mine, tile, other = pl.ds(c * CY, CY), pl.ds(c * 8, 8), pl.ds(16 + c * 8, 8)
        hi = plane(w_hi[mine, :], wy_hi[tile, :], wy_lo[tile, :])
        lo = plane(w_lo[mine, :], wy_hi[other, :], wy_lo[other, :])
        lon = plane(wn_lo[mine, :], wd[0, tile, :], wd[2, tile, :])
        hin = plane(wn_hi[mine, :], wd[1, tile, :], wd[3, tile, :])
        pairs = (
            (hi, turn(lon, 1, 1)),
            (turn(hi, -1, 1), lon),
            (turn(hin, -2, 1), turn(lo, -1, 1)),
            (turn(hin, -3, 1), turn(lo, -2, 1)),
        )
        grown.append([jnp.where(even, *pair) for pair in pairs])

    for one in planes:
        one.wait_recv()

    def spread(x, i):
        return jnp.broadcast_to(x[:, i : i + 1], x.shape)

    def beyond(side, from_hi, from_lo, c, i):
        first = 4 * (CY // 8) * c + i
        x, x_hi, x_lo = qn[side], qn[from_hi], qn[from_lo]
        middle = [spread(x, first + 4 * t) for t in range(CY // 8)]
        middle = jnp.concatenate(middle, axis=0)
        return plane(middle, spread(x_hi, first), spread(x_lo, first + 4 * (CY // 8 - 1)))

    ea = [[None, None] for _ in range(4)]
    carry_plane = []
    for c in range(2):
        tile = pl.ds(c * 8, 8)
        own = plane(q[c], qy_hi[tile, :], qy_lo[tile, :])
        sides = (
            (spread(own, CX - 2), beyond(0, 2, 4, c, 0)),
            (spread(own, CX - 1), beyond(0, 2, 4, c, 1)),
            (beyond(1, 3, 5, c, 2), spread(own, 0)),
            (beyond(1, 3, 5, c, 3), spread(own, 1)),
        )
        for m, pair in enumerate(sides):
            value = jnp.where(even, *pair) + grown[c][m]
            ea[m][c] = jnp.where(level_ok, value, 0.0)
        around = (q[c][CY - 8 :], qy_hi[tile, :], qy_lo[tile, :], q[c][:8])
        turned = [turn(x, by, 0) for x, by in zip(around, (2, 2, -2, -2))]
        carry_plane.append(
            jnp.where(
                row8 < 4,
                jnp.where(row8 < 2, turned[0], turned[1]),
                jnp.where(row8 < 6, turned[2], turned[3]),
            )
        )

    row_ok = ((row < CY) | (row >= CY + 2) | (gy < NY_DEV - 1)) & ((row < CY + 2) | (gy > 0))
    eb = []
    for m in range(3):
        up_y = (turn(ea[m][0], -1, 0),)
        up_z = tuple(turn(x, -2, 1) for x in ea[m])
        eb.append(fields(ea[m], up_z, up_y, ea[m + 1], True))
    ea1 = []
    for m in (1, 2):
        down_z = tuple(turn(x, 2, 1) for x in eb[m])
        down_y = tuple(turn(x, 1, 0) for x in eb[m])
        d = drive(eb[m], down_z, down_y, eb[m - 1])
        if m == 1:
            outside = (lane % 2 == 1) & (gx == 0)
        else:
            outside = (lane % 2 == 0) & (gx == NX_DEV - 1)
        ok = row_ok & jnp.logical_not(outside) & level_ok
        a = (ea[m][0] + d[0], ea[m][1] + d[1], d[2])
        ea1.append(tuple(jnp.where(ok, x, 0.0) for x in a))
    near = ea1[0]
    eb1 = fields(
        near,
        tuple(turn(x, -2, 1) for x in near),
        tuple(turn(x, -1, 0) for x in near),
        ea1[1],
        False,
    )
    v_out[pl.ds(0, EY), :] = jnp.where(even, ea1[1][1], eb1[2])
    v_out[pl.ds(EY, EY), :] = jnp.where(even, ea1[1][2], eb1[1])
    edge = tuple(jnp.where(even, ea1[0][c], ea1[1][c]) for c in range(3))

    strip.at_the_bounds(*carry_plane)
    strip_planes = planes_for(*carry_plane)
    rim = (lane == 0) | (lane == CX - 1)
    tile_ok = ((row8 >= 2) | (gy < NY_DEV - 1)) & ((row8 < 2) | (gy > 0))

    def finish_strip(z, _):
        new = strip.finish(z, strip_planes)
        shift = lax.rem(2 * CX - 1 - 2 * (z + 2), CX)
        for c in range(3):
            first = pl.multiple_of((c * (CZ + 2) + z + 1) * EY, 8)
            left, right = turn(new[c], -2, 0), turn(new[c], 2, 0)
            x = jnp.concatenate(
                [
                    jnp.where(row8 == 0, right, a1_out[pl.ds(first, 8), :]),
                    a1_out[pl.ds(first + 8, 16), :],
                    jnp.where(row8 == 7, left, a1_out[pl.ds(first + 24, 8), :]),
                    jnp.where(row8 < 4, left, right),
                ],
                axis=0,
            )
            x = jnp.where(rim, pltpu.roll(edge[c], shift, 1), x)
            a1_out[pl.ds(first, CY), :] = x[:CY]
            a1_out[pl.ds(first + CY, 8), :] = jnp.where(tile_ok, x[CY:], 0.0)
        return 0

    lax.fori_loop(-1, CZ + 1, finish_strip, 0, unroll=UNROLL_EDGE)

    @pl.when(gz == 0)
    def _():
        for c in range(3):
            a1_out[slot(c, -1, EY), :] = jnp.zeros((EY, CX), jnp.float32)

    @pl.when(gz == NZ_DEV - 1)
    def _():
        for c in range(3):
            a1_out[slot(c, CZ, EY), :] = jnp.zeros((EY, CX), jnp.float32)

    for one in ups + across + sums + layers + faces + corners + columns + planes:
        one.wait_send()


def step_kernel(a1, v_ref, out_hbm, out_v, store_sem):
    lane = lanes((EY, CX))
    first_lane, last_lane = lane == 0, lane == CX - 1

    def new_at(z):
        return tuple(
            a1[pl.ds(pl.multiple_of((c * (CZ + 2) + z + 1) * EY, 8), EY), :] for c in range(3)
        )

    def beside(z):
        shift = lax.rem(2 * CX - 1 - 2 * (z + 2), CX)
        return tuple(pltpu.roll(v_ref[pl.ds(k * EY, EY), :], shift, 1) for k in range(2))

    def second_field(a, a_up, v):
        yp = (turn(a[0], -1, 0), None, turn(a[2], -1, 0))
        xp = (
            None,
            jnp.where(last_lane, v[0], turn(a[1], -1, 1)),
            jnp.where(last_lane, v[1], turn(a[2], -1, 1)),
        )
        return fields(a, a_up, yp, xp, False)

    first_main, main = first_lane[:CY], slice(0, CY)

    def level_two(z, carry):
        a, before = carry
        v = beside(z)
        a_up = new_at(z + 1)
        b = second_field(a, a_up, v)
        ym = (turn(b[0], 1, 0)[main], None, turn(b[2], 1, 0)[main])
        own = tuple(x[main] for x in b)
        xm = (
            None,
            jnp.where(first_main, v[1][main], turn(own[1], 1, 1)),
            jnp.where(first_main, v[0][main], turn(own[2], 1, 1)),
        )
        d = drive(own, before, ym, xm)
        for c in range(3):
            out_v[pl.ds(pl.multiple_of((c * CZ + z) * CY, 8), CY), :] = a[c][main] + d[c]
        return a_up, (own[0], own[1])

    below, a = new_at(-1), new_at(0)
    b = second_field(below, a, beside(-1))
    carry = (a, (b[0][main], b[1][main]))
    part = 8

    def store(k, c):
        there = pl.ds(pl.multiple_of((c * CZ + k * part) * CY, 8), part * CY)
        return pltpu.make_async_copy(out_v.at[there], out_hbm.at[there], store_sem.at[k, c])

    def chunk(k, carry):
        carry = lax.fori_loop(
            0, part, lambda i, x: level_two(k * part + i, x), carry, unroll=4
        )
        for c in range(3):
            store(k, c).start()
        return carry

    lax.fori_loop(0, CZ // part, chunk, carry)
    for k in range(CZ // part):
        for c in range(3):
            store(k, c).wait()


def f32(*shape):
    return jax.ShapeDtypeStruct(shape, jnp.float32)


def vmem(*shape):
    return pltpu.VMEM(shape, jnp.float32)


def local(side_field, magnetogram):
    side = pltpu.with_memory_space_constraint(side_field.reshape(2 * CZ * CY, CX), pltpu.HBM)
    magnetogram = pltpu.with_memory_space_constraint(magnetogram, pltpu.HBM)
    whole = pl.BlockSpec(memory_space=pltpu.VMEM)
    dma = pltpu.SemaphoreType.DMA
    a1, v = pl.pallas_call(
        comm_kernel,
        out_shape=(f32(3 * (CZ + 2) * EY, CX), f32(2 * EY, CX)),
        in_specs=[pl.BlockSpec(memory_space=pltpu.HBM)] * 2,
        out_specs=(whole,) * 2,
        scratch_shapes=[
            vmem(CY, CX),
            vmem(2 * EZ * 8, CX),
            vmem(8 * (CZ + 2) * CY, CX),
            vmem(8 * (CZ + 2) * 8, CX),
            vmem(2 * LEVEL, CX),
            vmem(2 * CY, CX),
            vmem(NZ_DEV // 2 - 1, 2 * CY, CX),
            vmem(2 * CY, CX),
            vmem(2 * CY, CX),
        ]
        + [vmem(4 * CZ, CX)] * 4
        + [vmem(16, CX)] * 4
        + [vmem(2 * CY, CX)] * 4
        + [vmem(32, CX)] * 4
        + [
            vmem(4, 16, CX),
            vmem(8, CX),
            vmem(CY, CX),
            vmem(8 * (NY_DEV - 1), CX),
            vmem(CY * (NX_DEV - 1), CX),
            vmem(2 * CY, CX),
            vmem(8, CX),
            vmem(6, 8, CX),
            vmem(16, CX),
            vmem(16, CX),
            vmem(16, CX),
            vmem(16, CX),
        ]
        + [pltpu.SemaphoreType.REGULAR] * 3
        + [dma((5,))]
        + [dma((NZ_DEV - 1,))] * 2
        + [dma((2, 2))] * 2
        + [dma((2,))] * 4
        + [dma((8,))] * 2
        + [dma((NY_DEV - 1,))] * 2
        + [dma((NX_DEV - 1,))] * 2
        + [dma((8,))] * 2,
        compiler_params=pltpu.CompilerParams(
            collective_id=0, has_side_effects=True, vmem_limit_bytes=VMEM_BYTES
        ),
        name="exchange",
    )(side, magnetogram)
    out = pl.pallas_call(
        step_kernel,
        out_shape=f32(3 * CZ * CY, CX),
        in_specs=[whole] * 2,
        out_specs=pl.BlockSpec(memory_space=pltpu.HBM),
        scratch_shapes=[vmem(3 * CZ * CY, CX), dma((CZ // 8, 3))],
        compiler_params=pltpu.CompilerParams(vmem_limit_bytes=VMEM_BYTES),
        name="steps",
    )(a1, v)
    return out.reshape(3, CZ, CY, CX)


def solution(mesh):
    return jax.shard_map(
        local,
        mesh=mesh,
        in_specs=(P(None, "gz", "gy", "gx"), P("gy", "gx")),
        out_specs=P(None, "gz", "gy", "gx"),
        check_vma=False,
    )
```
